32 devices in a mesh: dp: 16 (over z, x, core), ffn: 2 (over y).
Axes of the slice: x: 2, y: 2, z: 4, core: 2. Of those that a mesh axis runs over, the one named last changes fastest.
Arguments:
- inputs: bfloat16 [65536, 768], P(('dp', 'ffn')), may hold values from -6 to 6
- segments: int32 [128, 512], P(('dp', 'ffn')), may hold values from 0 to 3, never falling along the last dimension, each value on 1 to 256 neighbouring positions
- cotangent: bfloat16 [65536, 768], P(('dp', 'ffn')), may hold values from -6 to 6
- qkv_weight: bfloat16 [3, 4, 192, 192], replicated, may hold values from -0.4375 to 0.4375
- qv_bias: float32 [2, 768], replicated, may hold values from -1.75 to 1.75
- out_weight: bfloat16 [768, 768], replicated, may hold values from -2.5 to 2.5
- out_bias: float32 [768], replicated, may hold values from -1.75 to 1.75
- ln1_gain: float32 [768], replicated, may hold values from 0.1 to 1.9
- ln1_bias: float32 [768], replicated, may hold values from -1.75 to 1.75
- up_weight: bfloat16 [4, 192, 768], P(None, None, 'ffn'), may hold values from -0.4375 to 0.4375
- up_bias: bfloat16 [4, 768], P(None, 'ffn'), may hold values from -1.75 to 1.75
- down_weight: bfloat16 [4, 192, 768], P(None, None, 'ffn'), may hold values from -0.4375 to 0.4375
- down_bias: float32 [768], replicated, may hold values from -1.75 to 1.75
- ln2_gain: float32 [768], replicated, may hold values from 0.1 to 1.9
- ln2_bias: float32 [768], replicated, may hold values from -1.75 to 1.75
Outputs:
- layer_out: float32 [65536, 768], P(('dp', 'ffn'))
- grad_inputs: float32 [65536, 768], P(('dp', 'ffn'))
- grad_qkv_weight: float32 [3, 4, 192, 192], replicated
- grad_qv_bias: float32 [2, 768], replicated
- grad_out_weight: float32 [768, 768], replicated
- grad_out_bias: float32 [768], replicated
- grad_ln1_gain: float32 [768], replicated
- grad_ln1_bias: float32 [768], replicated
- grad_up_weight: float32 [4, 192, 768], P(None, None, 'ffn')
- grad_up_bias: float32 [4, 768], P(None, 'ffn')
- grad_down_weight: float32 [4, 192, 768], P(None, None, 'ffn')
- grad_down_bias: float32 [768], replicated
- grad_ln2_gain: float32 [768], replicated
- grad_ln2_bias: float32 [768], replicated
The draws below stay inside these ranges and needn't reach their ends.
Inputs may be any that keep to these rules, and one draw needn't show every extreme that they name: `segments`: within each row the numbers never fall, start at 0 and count up by one; a document spans 1 to 256 positions.
All inputs are finite; a program needn't handle non-finite values.
Results may differ from the reference program's by a relative error of at most 0.013.
The reference program's roundings to bfloat16 on the way count: a program that leaves them out, or rounds other values in their place, can miss the bound.
Values may be sent and summed in bfloat16 or wider, within the bound.
No kernel may reach another device: no remote copies, remote signals or barrier semaphores. Data moves between devices by JAX's collectives and lax.ppermute only.
A program may use at most 256 MiB of HBM per device.

```python
import math
import jax
import jax.numpy as jnp
import numpy as np
from jax import lax

D = 768
HEADS = 12
HEAD_DIM = 64
GROUPS = 4
SEQ = 512
SEGS = 4
DG = 192
FG = 768
ROWS = 128
TOKENS = 65536


def block_levels(stream_key, extent, split, low, top_value):
    level = 1.0
    for position, shards_of in split:
        draws = jax.random.uniform(jax.random.fold_in(jax.random.fold_in(stream_key, 6), position), (shards_of,), jnp.float32, low / len(split), top_value / len(split))
        level = level * jnp.repeat(jnp.exp(draws), extent[position] // shards_of).reshape((-1,) + (1,) * (len(extent) - 1 - position))
    return level


def length_profile(count, total, most, slope):
    weights = [(1 << 20) // math.isqrt(rank ** slope) + 1 for rank in range(2, count + 1)]
    surplus, given = total - most - (count - 1), [1] * (count - 1)
    while surplus > 0:
        candidates = [i for i in range(count - 1) if given[i] < most]
        whole, left = sum([weights[i] for i in candidates]), surplus
        for i in candidates:
            addition = min(most - given[i], max(1, left * weights[i] // whole), surplus)
            given[i] = given[i] + addition
            surplus = surplus - addition
    return np.array([most] + given)


def ragged(own_key, amount, total, reach, skew):
    if amount == 2:
        one = jax.random.randint(own_key, (), max(1, total - reach), min(reach, total - 1) + 1)
        return jnp.stack([one, total - one])
    lengths = jnp.asarray(length_profile(amount, total, reach, skew), jnp.int32)
    twos = (amount - 1) // 2
    donor, receiver = lengths[1:1 + 2 * twos:2], lengths[2:2 + 2 * twos:2]
    room = jnp.minimum(donor - 1, reach - receiver)
    shifted = jax.random.randint(jax.random.fold_in(own_key, 1), (twos,), 0, 1 << 20) % (room + 1)
    lengths = lengths.at[1:1 + 2 * twos:2].set(donor - shifted).at[2:2 + 2 * twos:2].set(receiver + shifted)
    return lengths[jax.random.permutation(jax.random.fold_in(own_key, 2), amount)]


def gaussian(stream_key, shape, scale, most, cuts=(), dtype=jnp.bfloat16):
    loudness = block_levels(stream_key, shape, cuts, -0.22, 0.18) if cuts else 1.0
    entries = jax.random.normal(stream_key, shape, jnp.float32) * scale * loudness
    return jnp.minimum(jnp.maximum(entries, -most), most).astype(dtype)


def setup_inputs(seed: int = 0) -> dict:
    seeds = jax.random.split(jax.random.key(seed), 16)
    inputs = gaussian(seeds[0], (TOKENS, D), 1.0, 6.0, ((0, 32),))
    segments = jax.vmap(lambda own: jnp.searchsorted(jnp.cumsum(ragged(own, SEGS, SEQ, SEQ // 2, 1)), jnp.arange(SEQ), side="right"))(jax.random.split(seeds[1], ROWS)).reshape((ROWS, SEQ)).astype(jnp.int32)
    cotangent = gaussian(seeds[2], (TOKENS, D), 1.0, 6.0, ((0, 32),))
    qkv_weight = gaussian(seeds[3], (3, GROUPS, DG, DG), DG ** -0.5, 0.4375)
    qv_bias = gaussian(seeds[4], (2, D), 0.3, 1.75, (), jnp.float32)
    out_weight = gaussian(seeds[5], (D, D), (max(D * SEGS // SEQ, 4)) ** -0.5, 2.5)
    out_bias = gaussian(seeds[6], (D,), 0.3, 1.75, (), jnp.float32)
    ln1_gain = jnp.clip(1.0 + 0.18 * jax.random.normal(seeds[7], (D,), jnp.float32), 0.1, 1.9)
    ln1_bias = gaussian(seeds[8], (D,), 0.3, 1.75, (), jnp.float32)
    up_weight = gaussian(seeds[9], (GROUPS, DG, FG), DG ** -0.5, 0.4375, ((2, 2),))
    up_bias = gaussian(seeds[10], (GROUPS, FG), 0.3, 1.75, ((1, 2),))
    down_weight = gaussian(seeds[11], (GROUPS, DG, FG), (FG // 4) ** -0.5, 0.4375, ((2, 2),))
    down_bias = gaussian(seeds[12], (D,), 0.3, 1.75, (), jnp.float32)
    ln2_gain = jnp.clip(1.0 + 0.18 * jax.random.normal(seeds[13], (D,), jnp.float32), 0.1, 1.9)
    ln2_bias = gaussian(seeds[14], (D,), 0.3, 1.75, (), jnp.float32)
    return {"inputs": inputs, "segments": segments, "cotangent": cotangent, "qkv_weight": qkv_weight, "qv_bias": qv_bias, "out_weight": out_weight, "out_bias": out_bias, "ln1_gain": ln1_gain, "ln1_bias": ln1_bias, "up_weight": up_weight, "up_bias": up_bias, "down_weight": down_weight, "down_bias": down_bias, "ln2_gain": ln2_gain, "ln2_bias": ln2_bias}


@jax.custom_vjp
def low(v):
    return lax.optimization_barrier(v.astype(jnp.bfloat16)).astype(jnp.float32)

@jax.custom_vjp
def low_back(v):
    return v

def low_keep(v):
    return (low(v), None)

def low_pass(kept, grad):
    return (grad,)

def back_keep(v):
    return (v, None)

def back_low(kept, grad):
    return (low(grad),)
low.defvjp(low_keep, low_pass)
low_back.defvjp(back_keep, back_low)
norm_eps = 1e-05
highest = lax.Precision.HIGHEST

def layer_norm(values, gain, shift):
    average = lax.optimization_barrier(jnp.mean(values, axis=-1, keepdims=True))
    centered = values - average
    variance = lax.optimization_barrier(jnp.mean(centered * centered, axis=-1, keepdims=True))
    return centered * lax.rsqrt(variance + norm_eps) * gain + shift

def grouped_in(values, weight):
    tok_count = values.shape[0]
    grouped = values.reshape(tok_count, weight.shape[0], weight.shape[1])
    return jnp.einsum('ngi,gio->ngo', grouped, weight, precision=highest).reshape(tok_count, -1)

def grouped_out(values, weight):
    tok_count = values.shape[0]
    grouped = values.reshape(tok_count, weight.shape[0], weight.shape[2])
    return jnp.einsum('ngi,goi->ngo', grouped, weight, precision=highest).reshape(tok_count, -1)

def attend_row(packed):
    query, keyed, valued, segment = packed
    head_q = query.reshape(SEQ, HEADS, HEAD_DIM)
    head_k = keyed.reshape(SEQ, HEADS, HEAD_DIM)
    head_v = valued.reshape(SEQ, HEADS, HEAD_DIM)
    raw_scores = jnp.einsum('qhd,khd->hqk', head_q, head_k, precision=highest)
    scores = low_back(raw_scores) * HEAD_DIM ** (-0.5)
    same_doc = segment[:, None] == segment[None, :]
    scores = jnp.where(same_doc[None, :, :], scores, -1e+30)
    weights = low(jax.nn.softmax(scores, axis=-1))
    mixed = jnp.einsum('hqk,khd->qhd', weights, head_v, precision=highest)
    return mixed.reshape(SEQ, D)

def forward(inputs, qkv_weight, qv_bias, out_weight, out_bias, ln1_gain, ln1_bias, up_weight, up_bias, down_weight, down_bias, ln2_gain, ln2_bias, segments):
    query = low(low_back(grouped_in(inputs, qkv_weight[0])) + qv_bias[0])
    keyed = low(low_back(grouped_in(inputs, qkv_weight[1])))
    valued = low(low_back(grouped_in(inputs, qkv_weight[2])) + qv_bias[1])
    by_rows = (ROWS, SEQ, D)
    attended = lax.map(jax.checkpoint(attend_row), (query.reshape(by_rows), keyed.reshape(by_rows), valued.reshape(by_rows), segments))
    attended = low(low_back(attended.reshape(TOKENS, D)))
    mixed = low_back(jnp.dot(attended, out_weight, precision=highest)) + out_bias
    normed = layer_norm(inputs + mixed, ln1_gain, ln1_bias)
    upward = low_back(grouped_in(low(normed), up_weight)) + up_bias.reshape(-1)
    activated = low(jax.nn.gelu(upward, approximate=False))
    downward = low_back(grouped_out(activated, down_weight)) + down_bias
    return layer_norm(normed + downward, ln2_gain, ln2_bias)

def reference(inputs, segments, cotangent, qkv_weight, qv_bias, out_weight, out_bias, ln1_gain, ln1_bias, up_weight, up_bias, down_weight, down_bias, ln2_gain, ln2_bias):
    params = (inputs, qkv_weight, qv_bias, out_weight, out_bias, ln1_gain, ln1_bias, up_weight, up_bias, down_weight, down_bias, ln2_gain, ln2_bias)
    floats = tuple((values.astype(jnp.float32) for values in params))

    def apply_layer(*arrays):
        return forward(*arrays, segments)
    result, pullback = jax.vjp(apply_layer, *floats)
    gradients = pullback(cotangent.astype(jnp.float32))
    return (result, gradients[0], gradients[1], gradients[2], gradients[3], gradients[4], gradients[5], gradients[6], gradients[7], gradients[8], gradients[9], gradients[10], gradients[11], gradients[12])
```

```python
from functools import partial

import jax
import jax.numpy as jnp
from jax import lax
from jax.experimental import pallas as pl
from jax.experimental.pallas import tpu as pltpu
from jax.sharding import PartitionSpec as P

HEADS = 12
HEAD_DIM = 64
EPS = 1e-05
NEG = -1e30
VMEM = 60 * 1024 * 1024
BF = jnp.bfloat16
F32 = jnp.float32


def dot_nn(a, b):
    return jnp.dot(a, b, preferred_element_type=F32)


def dot_nt(a, b):
    return lax.dot_general(a, b, (((1,), (1,)), ((), ())), preferred_element_type=F32)


def params(*sem):
    return pltpu.CompilerParams(vmem_limit_bytes=VMEM, dimension_semantics=sem)


def wide(column, lanes):
    return jnp.concatenate([column] * (lanes // 128), axis=1)


def fold(values):
    total = values[:, 0:128]
    for start in range(128, values.shape[1], 128):
        total = total + values[:, start : start + 128]
    return total


def sub_sum(values):
    total = values[0:8]
    for start in range(8, values.shape[0], 8):
        total = total + values[start : start + 8]
    return total


def attend_kernel(x_ref, seg_ref, wt_ref, bias_ref, xt_ref, qkv_ref, att_ref, lse_ref, qa_ref, ka_ref):
    seq, width = x_ref.shape
    groups = wt_ref.shape[1]
    group = width // groups
    xt_ref[0] = x_ref[...].T
    seg = seg_ref[0]
    rank = lax.broadcasted_iota(jnp.int32, (16, seq), 0)
    same = rank == seg
    qa_ref[64:80, :] = jnp.where(same, 1.0, 0.0).astype(BF)
    ka_ref[64:80, :] = jnp.where(same | (rank >= 4), 0.0, NEG).astype(BF)

    def project(g, carry):
        rows = pl.ds(pl.multiple_of(g * group, group), group)
        xg = xt_ref[0, rows, :]
        for j in range(3):
            out = dot_nn(wt_ref[j, g], xg) + wide(bias_ref[j, rows, :], seq)
            qkv_ref[0, j, rows, :] = out.astype(BF)
        return carry

    lax.fori_loop(0, groups, project, 0)

    def head(h, carry):
        rows = pl.ds(pl.multiple_of(h * HEAD_DIM, HEAD_DIM), HEAD_DIM)
        qa_ref[0:64, :] = qkv_ref[0, 0, rows, :] * jnp.asarray(0.125, BF)
        ka_ref[0:64, :] = qkv_ref[0, 1, rows, :]
        kn = ka_ref[...].T
        vt = qkv_ref[0, 2, rows, :]
        for t in range(seq // 256):
            cols = slice(t * 256, t * 256 + 256)
            s = dot_nn(kn, qa_ref[:, cols])
            peak = jnp.max(s, axis=0, keepdims=True)
            e = jnp.exp(s - peak)
            total = jnp.sum(e, axis=0, keepdims=True)
            p = (e * (1.0 / total)).astype(BF)
            att_ref[0, rows, cols] = dot_nn(vt, p).astype(BF)
            lse_ref[0, pl.ds(h, 1), cols] = peak + jnp.log(total)
        return carry

    lax.fori_loop(0, HEADS, head, 0)


def attend(x, seg, wt, bias):
    width = x.shape[1]
    rows, seq = seg.shape
    return pl.pallas_call(
        attend_kernel,
        grid=(rows,),
        in_specs=[
            pl.BlockSpec((seq, width), lambda r: (r, 0)),
            pl.BlockSpec((1, 1, seq), lambda r: (r, 0, 0)),
            pl.BlockSpec(wt.shape, lambda r: (0, 0, 0, 0)),
            pl.BlockSpec(bias.shape, lambda r: (0, 0, 0)),
        ],
        out_specs=[
            pl.BlockSpec((1, width, seq), lambda r: (r, 0, 0)),
            pl.BlockSpec((1, 3, width, seq), lambda r: (r, 0, 0, 0)),
            pl.BlockSpec((1, width, seq), lambda r: (r, 0, 0)),
            pl.BlockSpec((1, 16, seq), lambda r: (r, 0, 0)),
        ],
        out_shape=[
            jax.ShapeDtypeStruct((rows, width, seq), BF),
            jax.ShapeDtypeStruct((rows, 3, width, seq), BF),
            jax.ShapeDtypeStruct((rows, width, seq), BF),
            jax.ShapeDtypeStruct((rows, 16, seq), F32),
        ],
        scratch_shapes=[pltpu.VMEM((80, seq), BF), pltpu.VMEM((80, seq), BF)],
        compiler_params=params("arbitrary"),
        name="attend",
    )(x, seg.reshape(rows, 1, seq), wt, bias)


CH = 128


def ffn_kernel(
    xt_ref, att_ref, cot_ref, wot_ref, wo_ref, wu_ref, wut_ref, wd_ref, wdt_ref, vec_ref,
    out_ref, gr1_ref, gatt_ref, delta_ref, dwo_ref, dff_ref, sums_ref,
    a_ref, u1_ref, v2_ref, nlow_ref, act_ref, gp_ref, gd_ref, gup_ref, ct_ref, acc_ref,
):
    width, seq = a_ref.shape
    halves, groups = wu_ref.shape[:2]
    group = width // groups
    part = wut_ref.shape[2]
    first = pl.program_id(0) == 0
    last = pl.program_id(0) == pl.num_programs(0) - 1
    inv_width = 1.0 / width

    @pl.when(first)
    def _():
        acc_ref[...] = jnp.zeros_like(acc_ref)
        dwo_ref[...] = jnp.zeros_like(dwo_ref)
        dff_ref[...] = jnp.zeros_like(dff_ref)
        row = lax.broadcasted_iota(jnp.int32, (16, seq), 0)
        for g in range(groups):
            nlow_ref[g, group : group + 16, :] = jnp.where(row == 0, 1.0, 0.0).astype(BF)

    ct_ref[...] = cot_ref[...].T

    part_sum = jnp.zeros((8, seq), F32)
    for c in range(0, width, CH):
        s = slice(c, c + CH)
        v = dot_nn(wot_ref[s, :], att_ref[0]) + wide(vec_ref[0, s, :], seq) + xt_ref[0, s, :].astype(F32)
        a_ref[s, :] = v
        part_sum = part_sum + sub_sum(v)
    mean = jnp.sum(part_sum, axis=0, keepdims=True) * inv_width
    part_sum = jnp.zeros((8, seq), F32)
    for c in range(0, width, CH):
        s = slice(c, c + CH)
        v = a_ref[s, :] - mean
        a_ref[s, :] = v
        part_sum = part_sum + sub_sum(v * v)
    r1 = lax.rsqrt(jnp.sum(part_sum, axis=0, keepdims=True) * inv_width + EPS)
    for g in range(groups):
        for c in range(0, group, 64):
            s = slice(g * group + c, g * group + c + 64)
            u = a_ref[s, :] * r1
            u1_ref[s, :] = u
            n = u * wide(vec_ref[1, s, :], seq) + wide(vec_ref[2, s, :], seq)
            v2_ref[s, :] = n + wide(vec_ref[3, s, :], seq)
            nlow_ref[g, c : c + 64, :] = n.astype(BF)

    def up(i, carry):
        h, g = i // groups, i % groups
        for c in range(0, part, CH):
            s = slice(c, c + CH)
            u = dot_nn(wut_ref[h, g, s, :], nlow_ref[g])
            y = u * 0.7071067811865476
            one = 1.0 + lax.erf(y)
            act_ref[i, s, :] = (u * one).astype(BF)
            gp_ref[i, s, :] = one + (y * 1.1283791670955126) * jnp.exp(-(y * y))
        rows = pl.ds(pl.multiple_of(g * group, group), group)
        v2_ref[rows, :] += dot_nn(wd_ref[h, g], act_ref[i])
        return carry

    lax.fori_loop(0, halves * groups, up, 0)

    part_sum = jnp.zeros((8, seq), F32)
    for c in range(0, width, CH):
        part_sum = part_sum + sub_sum(v2_ref[c : c + CH, :])
    mean = jnp.sum(part_sum, axis=0, keepdims=True) * inv_width
    part_sum = jnp.zeros((8, seq), F32)
    for c in range(0, width, CH):
        s = slice(c, c + CH)
        v = v2_ref[s, :] - mean
        v2_ref[s, :] = v
        part_sum = part_sum + sub_sum(v * v)
    r2 = lax.rsqrt(jnp.sum(part_sum, axis=0, keepdims=True) * inv_width + EPS)
    sum_e = jnp.zeros((8, seq), F32)
    sum_eu = jnp.zeros((8, seq), F32)
    for c in range(0, width, CH):
        s = slice(c, c + CH)
        u = v2_ref[s, :] * r2
        v2_ref[s, :] = u
        gain = wide(vec_ref[4, s, :], seq)
        out_ref[:, s] = (u * gain + wide(vec_ref[5, s, :], seq)).T
        cot = ct_ref[s, :].astype(F32)
        acc_ref[4, s, :] += fold(cot * u)
        acc_ref[5, s, :] += fold(cot)
        e = cot * gain
        sum_e = sum_e + sub_sum(e)
        sum_eu = sum_eu + sub_sum(e * u)
    mean_e = jnp.sum(sum_e, axis=0, keepdims=True) * inv_width
    mean_eu = jnp.sum(sum_eu, axis=0, keepdims=True) * inv_width
    for c in range(0, width, CH):
        s = slice(c, c + CH)
        e = ct_ref[s, :].astype(F32) * wide(vec_ref[4, s, :], seq)
        gr = r2 * (e - mean_e - v2_ref[s, :] * mean_eu)
        a_ref[s, :] = gr
        acc_ref[3, s, :] += fold(gr)
        gd_ref[s, :] = gr.astype(BF)

    def down(i, carry):
        h, g = i // groups, i % groups
        rows = pl.ds(pl.multiple_of(g * group, group), group)
        for c in range(0, part, CH):
            s = slice(c, c + CH)
            gup_ref[s, :] = (dot_nn(wdt_ref[h, g, s, :], gd_ref[rows, :]) * gp_ref[i, s, :]).astype(BF)
        dff_ref[h, g, 0 : group + 16, :] += dot_nt(nlow_ref[g], gup_ref[...])
        dff_ref[h, g, group + 16 : 2 * group + 16, :] += dot_nt(gd_ref[rows, :], act_ref[i])
        a_ref[rows, :] += dot_nn(wu_ref[h, g], gup_ref[...])
        return carry

    lax.fori_loop(0, halves * groups, down, 0)

    sum_e = jnp.zeros((8, seq), F32)
    sum_eu = jnp.zeros((8, seq), F32)
    for c in range(0, width, CH):
        s = slice(c, c + CH)
        gn = a_ref[s, :]
        u = u1_ref[s, :]
        acc_ref[1, s, :] += fold(gn * u)
        acc_ref[2, s, :] += fold(gn)
        e = gn * wide(vec_ref[1, s, :], seq)
        sum_e = sum_e + sub_sum(e)
        sum_eu = sum_eu + sub_sum(e * u)
    mean_e = jnp.sum(sum_e, axis=0, keepdims=True) * inv_width
    mean_eu = jnp.sum(sum_eu, axis=0, keepdims=True) * inv_width
    for c in range(0, width, CH):
        s = slice(c, c + CH)
        e = a_ref[s, :] * wide(vec_ref[1, s, :], seq)
        gr = r1 * (e - mean_e - u1_ref[s, :] * mean_eu)
        gr1_ref[0, s, :] = gr
        acc_ref[0, s, :] += fold(gr)
        gd_ref[s, :] = gr.astype(BF)
    for c in range(0, width, CH):
        s = slice(c, c + CH)
        ga = dot_nn(wo_ref[s, :], gd_ref[...]).astype(BF)
        gatt_ref[0, s, :] = ga
        prod = ga.astype(F32) * att_ref[0, s, :].astype(F32)
        for k in range(0, CH, HEAD_DIM):
            head = (c + k) // HEAD_DIM
            delta_ref[0, head : head + 1, :] = jnp.sum(prod[k : k + HEAD_DIM], axis=0, keepdims=True)
        dwo_ref[s, :] += dot_nt(att_ref[0, s, :], gd_ref[...])

    @pl.when(last)
    def _():
        dff_ref[:, :, group + 16 : 2 * group + 16, :] = dff_ref[:, :, group + 16 : 2 * group + 16, :] * 0.5
        for n in range(6):
            sums_ref[n : n + 1, :] = jnp.sum(acc_ref[n].T, axis=0, keepdims=True)
        sums_ref[6:8, :] = jnp.zeros((2, width), F32)


def feed(xt, att, cot, wot, wo, wu, wut, wd, wdt, vec):
    rows, width, seq = xt.shape
    halves, groups, group, part = wu.shape

    def whole(a):
        return pl.BlockSpec(a.shape, lambda r: (0,) * len(a.shape))

    per_row = pl.BlockSpec((1, width, seq), lambda r: (r, 0, 0))
    token = pl.BlockSpec((seq, width), lambda r: (r, 0))
    outs = [
        jax.ShapeDtypeStruct((rows * seq, width), F32),
        jax.ShapeDtypeStruct((rows, width, seq), F32),
        jax.ShapeDtypeStruct((rows, width, seq), BF),
        jax.ShapeDtypeStruct((rows, 16, seq), F32),
        jax.ShapeDtypeStruct((width, width), F32),
        jax.ShapeDtypeStruct((halves, groups, 2 * group + 32, part), F32),
        jax.ShapeDtypeStruct((8, width), F32),
    ]
    return pl.pallas_call(
        ffn_kernel,
        grid=(rows,),
        in_specs=[per_row, per_row, token] + [whole(a) for a in (wot, wo, wu, wut, wd, wdt, vec)],
        out_specs=[token, per_row, per_row, pl.BlockSpec((1, 16, seq), lambda r: (r, 0, 0))]
        + [whole(a) for a in outs[4:]],
        out_shape=outs,
        scratch_shapes=[
            pltpu.VMEM((width, seq), F32),
            pltpu.VMEM((width, seq), F32),
            pltpu.VMEM((width, seq), F32),
            pltpu.VMEM((groups, group + 16, seq), BF),
            pltpu.VMEM((halves * groups, part, seq), BF),
            pltpu.VMEM((halves * groups, part, seq), F32),
            pltpu.VMEM((width, seq), BF),
            pltpu.VMEM((part, seq), BF),
            pltpu.VMEM((width, seq), BF),
            pltpu.VMEM((6, width, 128), F32),
        ],
        compiler_params=params("arbitrary"),
        name="feed",
    )(xt, att, cot, wot, wo, wu, wut, wd, wdt, vec)


def split3(v):
    hi = v.astype(BF).astype(F32)
    mid = (v - hi).astype(BF).astype(F32)
    return hi, mid, v - hi - mid


def back_kernel(
    qkv_ref, gatt_ref, xt_ref, gr1_ref, lse_ref, delta_ref, seg_ref, w_ref, *rest, head0
):
    gin_ref, dw_ref, bsum_ref, qa_ref, ka_ref, va_ref, ga_ref, p_ref, ds_ref, d_ref = rest[-10:]
    chans, seq = xt_ref.shape[1:]
    groups, group = w_ref.shape[1:3]
    first = pl.program_id(0) == 0

    @pl.when(first)
    def _():
        dw_ref[...] = jnp.zeros_like(dw_ref)
        bsum_ref[...] = jnp.zeros_like(bsum_ref)

    seg = seg_ref[0]
    rank = lax.broadcasted_iota(jnp.int32, (16, seq), 0)
    same = rank == seg
    hot = jnp.where(same, 1.0, 0.0)
    ka_ref[64:80, :] = jnp.where(rank < 4, jnp.where(same, 0.0, NEG), jnp.where(rank < 7, -1.0, 0.0)).astype(BF)
    va_ref[64:80, :] = jnp.where(rank < 3, -1.0, 0.0).astype(BF)

    def head(h, carry):
        rows = pl.ds(pl.multiple_of(h * HEAD_DIM, HEAD_DIM), HEAD_DIM)
        hi, mid, lo = split3(lse_ref[0, pl.ds(head0 + h, 1), :])
        tail = jnp.where(rank == 4, hi, jnp.where(rank == 5, mid, jnp.where(rank == 6, lo, 0.0)))
        qa_ref[64:80, :] = jnp.where(rank < 4, hot, tail).astype(BF)
        hi, mid, lo = split3(delta_ref[0, pl.ds(head0 + h, 1), :])
        ga_ref[64:80, :] = jnp.where(rank == 0, hi, jnp.where(rank == 1, mid, jnp.where(rank == 2, lo, 0.0))).astype(BF)
        qs = qkv_ref[0, 0, rows, :] * jnp.asarray(0.125, BF)
        kt = qkv_ref[0, 1, rows, :]
        gt = gatt_ref[0, rows, :]
        qa_ref[0:64, :] = qs
        ka_ref[0:64, :] = kt
        va_ref[0:64, :] = qkv_ref[0, 2, rows, :]
        ga_ref[0:64, :] = gt
        kn = ka_ref[...].T
        vn = va_ref[...].T
        dk = jnp.zeros((HEAD_DIM, seq), F32)
        dv = jnp.zeros((HEAD_DIM, seq), F32)
        dq = []
        for t in range(seq // 256):
            cols = slice(t * 256, t * 256 + 256)
            p = jnp.exp(dot_nn(kn, qa_ref[:, cols]))
            p_ref[t] = p.astype(BF)
            ds_ref[t] = (p * dot_nn(vn, ga_ref[:, cols])).astype(BF)
            dv = dv + dot_nt(gt[:, cols], p_ref[t])
            dk = dk + dot_nt(qs[:, cols], ds_ref[t])
            dq.append(dot_nn(kt, ds_ref[t]) * 0.125)
        dq = jnp.concatenate(dq, axis=1)
        bsum_ref[0, rows, :] += fold(dq)
        bsum_ref[1, rows, :] += fold(dv)
        d_ref[0, rows, :] = dq.astype(BF)
        d_ref[1, rows, :] = dk.astype(BF)
        d_ref[2, rows, :] = dv.astype(BF)
        return carry

    lax.fori_loop(0, chans // HEAD_DIM, head, 0)
    parts = []
    for g in range(groups):
        s = slice(g * group, (g + 1) * group)
        total = gr1_ref[0, s, :]
        for j in range(3):
            d = d_ref[j, s, :]
            dw_ref[j, g] += dot_nt(xt_ref[0, s, :], d)
            total = total + dot_nn(w_ref[j, g], d)
        parts.append(total)
    gin_ref[...] = jnp.concatenate(parts, axis=0).T


def back(qkv, gatt, xt, gr1, lse, delta, seg, w, index, parts, into):
    rows, _, width, seq = qkv.shape
    chans = width // parts
    groups, group = w.shape[1] // parts, w.shape[2]
    per_row = pl.BlockSpec((1, chans, seq), lambda r: (r, index, 0))
    full = pl.BlockSpec((1, 16, seq), lambda r: (r, 0, 0))
    in_specs = [
        pl.BlockSpec((1, 3, chans, seq), lambda r: (r, 0, index, 0)),
        per_row,
        per_row,
        per_row,
        full,
        full,
        pl.BlockSpec((1, 1, seq), lambda r: (r, 0, 0)),
        pl.BlockSpec((3, groups, group, group), lambda r: (0, index, 0, 0)),
    ]
    args = [qkv, gatt, xt, gr1, lse, delta, seg.reshape(rows, 1, seq), w]
    alias = {}
    if into is not None:
        in_specs.append(pl.BlockSpec(memory_space=pl.ANY))
        args.append(into)
        alias = {len(args) - 1: 0}
    return pl.pallas_call(
        partial(back_kernel, head0=index * (chans // HEAD_DIM)),
        grid=(rows,),
        in_specs=in_specs,
        out_specs=[
            pl.BlockSpec((seq, chans), lambda r: (r, index)),
            pl.BlockSpec((3, groups, group, group), lambda r: (0, 0, 0, 0)),
            pl.BlockSpec((2, chans, 128), lambda r: (0, 0, 0)),
        ],
        out_shape=[
            jax.ShapeDtypeStruct((rows * seq, width), F32),
            jax.ShapeDtypeStruct((3, groups, group, group), F32),
            jax.ShapeDtypeStruct((2, chans, 128), F32),
        ],
        scratch_shapes=[pltpu.VMEM((80, seq), BF) for _ in range(4)]
        + [pltpu.VMEM((seq // 256, seq, 256), BF) for _ in range(2)]
        + [pltpu.VMEM((3, chans, seq), BF)],
        input_output_aliases=alias,
        compiler_params=params("arbitrary"),
        name="back",
    )(*args)


def swap(value, axis, size, bit):
    return lax.ppermute(value, axis, [(i, i ^ bit) for i in range(size)])


def scatter(value, axis, size, bit):
    half = value.shape[0] // 2
    mine = (lax.axis_index(axis) // bit) % 2
    keep = lax.dynamic_slice_in_dim(value, mine * half, half, 0)
    send = lax.dynamic_slice_in_dim(value, (1 - mine) * half, half, 0).astype(BF)
    return keep + swap(send, axis, size, bit).astype(F32)


def gather(value, axis, size, bit):
    mine = (lax.axis_index(axis) // bit) % 2
    other = swap(value, axis, size, bit)
    return jnp.where(mine == 0, jnp.concatenate([value, other]), jnp.concatenate([other, value]))


def sum_over(value, steps):
    done = []
    for axis, size, bit in steps:
        if value.shape[0] % 2 == 0:
            value = scatter(value, axis, size, bit)
            done.append((axis, size, bit))
        else:
            low = value.astype(BF)
            value = low.astype(F32) + swap(low, axis, size, bit).astype(F32)
    low = value.astype(BF)
    for step in reversed(done):
        low = gather(low, *step)
    return low.astype(F32)


def bits_of(axis, size):
    return [(axis, size, 1 << k) for k in range(size.bit_length() - 1)]


def per_device(
    inputs, segments, cotangent, qkv_weight, qv_bias, out_weight, out_bias, ln1_gain, ln1_bias,
    up_weight, up_bias, down_weight, down_bias, ln2_gain, ln2_bias, *, dp, ffn,
):
    width = inputs.shape[1]
    groups, group = qkv_weight.shape[1:3]
    part = up_weight.shape[2]

    def all_parts(a):
        return lax.all_gather(a, "ffn", axis=0)

    up_aug = jnp.concatenate(
        [up_weight, up_bias[:, None, :], jnp.zeros((groups, 15, part), BF)], axis=1
    )
    up_all = all_parts(up_aug)
    down_all = all_parts(down_weight)

    def lanes(v):
        return jnp.broadcast_to(v[..., None], v.shape + (128,))

    bias = lanes(jnp.stack([qv_bias[0], jnp.zeros_like(qv_bias[0]), qv_bias[1]]))
    xt, qkv, att, lse = attend(inputs, segments, qkv_weight.swapaxes(2, 3), bias)
    vec = lanes(jnp.stack([out_bias, ln1_gain, ln1_bias, down_bias, ln2_gain, ln2_bias]))
    half = jnp.asarray(0.5, BF)
    layer_out, gr1, gatt, delta, dwo, dff, sums = feed(
        xt, att, cotangent, out_weight.T, out_weight,
        up_all[:, :, :group], up_all.swapaxes(2, 3), down_all * half, down_all.swapaxes(2, 3) * half, vec,
    )
    everyone = [("dp", dp, 1)] + bits_of("ffn", ffn) + bits_of("dp", dp)[1:]
    parts = 2
    grad_inputs = None
    dws, bsums = [], []
    for index in range(parts):
        grad_inputs, dw, bsum = back(qkv, gatt, xt, gr1, lse, delta, segments, qkv_weight, index, parts, grad_inputs)
        dws.append(dw)
        bsums.append(jnp.sum(bsum, axis=2))
    mine = lax.axis_index("ffn")
    assert ffn == 2
    keep = lax.dynamic_index_in_dim(dff, mine, 0, keepdims=False)
    send = lax.dynamic_index_in_dim(dff, 1 - mine, 0, keepdims=False).astype(BF)
    own = keep + swap(send, "ffn", ffn, 1).astype(F32)
    own = own.reshape(16, -1, part)
    own = sum_over(own, bits_of("dp", dp)).reshape(groups, -1, part)
    dwo = sum_over(dwo.reshape(32, -1, width), everyone).reshape(width, width)
    dqkv = jnp.concatenate(dws, axis=1)
    shape = dqkv.shape
    dqkv = sum_over(dqkv.reshape(32, -1, 384), everyone).reshape(shape)
    small = jnp.concatenate([sums[:6], jnp.concatenate(bsums, axis=1)])
    small = sum_over(small[None], everyone)[0]
    return (
        layer_out,
        grad_inputs,
        dqkv,
        small[6:8],
        dwo,
        small[0],
        small[1],
        small[2],
        own[:, :group],
        own[:, group],
        own[:, group + 16 : 2 * group + 16],
        small[3],
        small[4],
        small[5],
    )


def solution(mesh):
    rows = P(("dp", "ffn"), None)
    shared = P()
    split = P(None, None, "ffn")
    return jax.shard_map(
        partial(per_device, dp=mesh.shape["dp"], ffn=mesh.shape["ffn"]),
        mesh=mesh,
        in_specs=(rows, rows, rows) + (shared,) * 6 + (split, P(None, "ffn"), split) + (shared,) * 3,
        out_specs=(rows, rows) + (shared,) * 6 + (split, P(None, "ffn"), split) + (shared,) * 3,
        check_vma=False,
    )
```

```python
from functools import partial

import jax
import jax.numpy as jnp
from jax import lax
from jax.experimental import pallas as pl
from jax.experimental.pallas import tpu as pltpu
from jax.sharding import PartitionSpec as P

HEADS = 12
HEAD_DIM = 64
EPS = 1e-05
NEG = -1e30
VMEM = 60 * 1024 * 1024
BF = jnp.bfloat16
F32 = jnp.float32


def dot_nn(a, b):
    return jnp.dot(a, b, preferred_element_type=F32)


def dot_nt(a, b):
    return lax.dot_general(a, b, (((1,), (1,)), ((), ())), preferred_element_type=F32)


def params(*sem):
    return pltpu.CompilerParams(vmem_limit_bytes=VMEM, dimension_semantics=sem)


def wide(column, lanes):
    return jnp.concatenate([column] * (lanes // 128), axis=1)


def fold(values):
    total = values[:, 0:128]
    for start in range(128, values.shape[1], 128):
        total = total + values[:, start : start + 128]
    return total


def sub_sum(values):
    total = values[0:8]
    for start in range(8, values.shape[0], 8):
        total = total + values[start : start + 8]
    return total


def attend_kernel(x_ref, seg_ref, wt_ref, bias_ref, xt_ref, qkv_ref, att_ref, lse_ref, qa_ref, ka_ref):
    seq, width = x_ref.shape
    groups = wt_ref.shape[1]
    group = width // groups
    xt_ref[0] = x_ref[...].T
    seg = seg_ref[0]
    rank = lax.broadcasted_iota(jnp.int32, (16, seq), 0)
    same = rank == seg
    qa_ref[64:80, :] = jnp.where(same, 1.0, 0.0).astype(BF)
    ka_ref[64:80, :] = jnp.where(same | (rank >= 4), 0.0, NEG).astype(BF)

    def project(g, carry):
        rows = pl.ds(pl.multiple_of(g * group, group), group)
        xg = xt_ref[0, rows, :]
        for j in range(3):
            out = dot_nn(wt_ref[j, g], xg) + wide(bias_ref[j, rows, :], seq)
            qkv_ref[0, j, rows, :] = out.astype(BF)
        return carry

    lax.fori_loop(0, groups, project, 0)

    def head(h, carry):
        rows = pl.ds(pl.multiple_of(h * HEAD_DIM, HEAD_DIM), HEAD_DIM)
        qa_ref[0:64, :] = qkv_ref[0, 0, rows, :] * jnp.asarray(0.125, BF)
        ka_ref[0:64, :] = qkv_ref[0, 1, rows, :]
        kn = ka_ref[...].T
        vt = qkv_ref[0, 2, rows, :]
        for t in range(seq // 256):
            cols = slice(t * 256, t * 256 + 256)
            s = dot_nn(kn, qa_ref[:, cols])
            peak = jnp.max(s, axis=0, keepdims=True)
            e = jnp.exp(s - peak)
            total = jnp.sum(e, axis=0, keepdims=True)
            p = (e * (1.0 / total)).astype(BF)
            att_ref[0, rows, cols] = dot_nn(vt, p).astype(BF)
            lse_ref[0, pl.ds(h, 1), cols] = peak + jnp.log(total)
        return carry

    lax.fori_loop(0, HEADS, head, 0)


def attend(x, seg, wt, bias):
    width = x.shape[1]
    rows, seq = seg.shape
    return pl.pallas_call(
        attend_kernel,
        grid=(rows,),
        in_specs=[
            pl.BlockSpec((seq, width), lambda r: (r, 0)),
            pl.BlockSpec((1, 1, seq), lambda r: (r, 0, 0)),
            pl.BlockSpec(wt.shape, lambda r: (0, 0, 0, 0)),
            pl.BlockSpec(bias.shape, lambda r: (0, 0, 0)),
        ],
        out_specs=[
            pl.BlockSpec((1, width, seq), lambda r: (r, 0, 0)),
            pl.BlockSpec((1, 3, width, seq), lambda r: (r, 0, 0, 0)),
            pl.BlockSpec((1, width, seq), lambda r: (r, 0, 0)),
            pl.BlockSpec((1, 16, seq), lambda r: (r, 0, 0)),
        ],
        out_shape=[
            jax.ShapeDtypeStruct((rows, width, seq), BF),
            jax.ShapeDtypeStruct((rows, 3, width, seq), BF),
            jax.ShapeDtypeStruct((rows, width, seq), BF),
            jax.ShapeDtypeStruct((rows, 16, seq), F32),
        ],
        scratch_shapes=[pltpu.VMEM((80, seq), BF), pltpu.VMEM((80, seq), BF)],
        compiler_params=params("arbitrary"),
        name="attend",
    )(x, seg.reshape(rows, 1, seq), wt, bias)


CH = 128


def ffn_kernel(
    xt_ref, att_ref, cot_ref, wot_ref, wo_ref, wu_ref, wut_ref, wd_ref, wdt_ref, vec_ref,
    out_ref, gr1_ref, gatt_ref, delta_ref, dwo_ref, dff_ref, sums_ref,
    a_ref, u1_ref, v2_ref, nlow_ref, act_ref, gp_ref, gd_ref, gup_ref, ct_ref, acc_ref,
):
    width, seq = a_ref.shape
    halves, groups = wu_ref.shape[:2]
    group = width // groups
    part = wut_ref.shape[2]
    first = pl.program_id(0) == 0
    last = pl.program_id(0) == pl.num_programs(0) - 1
    inv_width = 1.0 / width

    @pl.when(first)
    def _():
        acc_ref[...] = jnp.zeros_like(acc_ref)
        dwo_ref[...] = jnp.zeros_like(dwo_ref)
        dff_ref[...] = jnp.zeros_like(dff_ref)
        row = lax.broadcasted_iota(jnp.int32, (16, seq), 0)
        for g in range(groups):
            nlow_ref[g, group : group + 16, :] = jnp.where(row == 0, 1.0, 0.0).astype(BF)

    ct_ref[...] = cot_ref[...].T

    part_sum = jnp.zeros((8, seq), F32)
    for c in range(0, width, CH):
        s = slice(c, c + CH)
        v = dot_nn(wot_ref[s, :], att_ref[0]) + wide(vec_ref[0, s, :], seq) + xt_ref[0, s, :].astype(F32)
        a_ref[s, :] = v
        part_sum = part_sum + sub_sum(v)
    mean = jnp.sum(part_sum, axis=0, keepdims=True) * inv_width
    part_sum = jnp.zeros((8, seq), F32)
    for c in range(0, width, CH):
        s = slice(c, c + CH)
        v = a_ref[s, :] - mean
        a_ref[s, :] = v
        part_sum = part_sum + sub_sum(v * v)
    r1 = lax.rsqrt(jnp.sum(part_sum, axis=0, keepdims=True) * inv_width + EPS)
    for g in range(groups):
        for c in range(0, group, 64):
            s = slice(g * group + c, g * group + c + 64)
            u = a_ref[s, :] * r1
            u1_ref[s, :] = u
            n = u * wide(vec_ref[1, s, :], seq) + wide(vec_ref[2, s, :], seq)
            v2_ref[s, :] = n + wide(vec_ref[3, s, :], seq)
            nlow_ref[g, c : c + 64, :] = n.astype(BF)

    def up(i, carry):
        h, g = i // groups, i % groups
        for c in range(0, part, CH):
            s = slice(c, c + CH)
            u = dot_nn(wut_ref[h, g, s, :], nlow_ref[g])
            y = u * 0.7071067811865476
            one = 1.0 + lax.erf(y)
            act_ref[i, s, :] = (u * one).astype(BF)
            gp_ref[i, s, :] = one + (y * 1.1283791670955126) * jnp.exp(-(y * y))
        rows = pl.ds(pl.multiple_of(g * group, group), group)
        v2_ref[rows, :] += dot_nn(wd_ref[h, g], act_ref[i])
        return carry

    lax.fori_loop(0, halves * groups, up, 0)

    part_sum = jnp.zeros((8, seq), F32)
    for c in range(0, width, CH):
        part_sum = part_sum + sub_sum(v2_ref[c : c + CH, :])
    mean = jnp.sum(part_sum, axis=0, keepdims=True) * inv_width
    part_sum = jnp.zeros((8, seq), F32)
    for c in range(0, width, CH):
        s = slice(c, c + CH)
        v = v2_ref[s, :] - mean
        v2_ref[s, :] = v
        part_sum = part_sum + sub_sum(v * v)
    r2 = lax.rsqrt(jnp.sum(part_sum, axis=0, keepdims=True) * inv_width + EPS)
    sum_e = jnp.zeros((8, seq), F32)
    sum_eu = jnp.zeros((8, seq), F32)
    for c in range(0, width, CH):
        s = slice(c, c + CH)
        u = v2_ref[s, :] * r2
        v2_ref[s, :] = u
        gain = wide(vec_ref[4, s, :], seq)
        out_ref[:, s] = (u * gain + wide(vec_ref[5, s, :], seq)).T
        cot = ct_ref[s, :].astype(F32)
        acc_ref[4, s, :] += fold(cot * u)
        acc_ref[5, s, :] += fold(cot)
        e = cot * gain
        sum_e = sum_e + sub_sum(e)
        sum_eu = sum_eu + sub_sum(e * u)
    mean_e = jnp.sum(sum_e, axis=0, keepdims=True) * inv_width
    mean_eu = jnp.sum(sum_eu, axis=0, keepdims=True) * inv_width
    for c in range(0, width, CH):
        s = slice(c, c + CH)
        e = ct_ref[s, :].astype(F32) * wide(vec_ref[4, s, :], seq)
        gr = r2 * (e - mean_e - v2_ref[s, :] * mean_eu)
        a_ref[s, :] = gr
        acc_ref[3, s, :] += fold(gr)
        gd_ref[s, :] = gr.astype(BF)

    def down(i, carry):
        h, g = i // groups, i % groups
        rows = pl.ds(pl.multiple_of(g * group, group), group)
        for c in range(0, part, CH):
            s = slice(c, c + CH)
            gup_ref[s, :] = (dot_nn(wdt_ref[h, g, s, :], gd_ref[rows, :]) * gp_ref[i, s, :]).astype(BF)
        dff_ref[h, g, 0 : group + 16, :] += dot_nt(nlow_ref[g], gup_ref[...])
        dff_ref[h, g, group + 16 : 2 * group + 16, :] += dot_nt(gd_ref[rows, :], act_ref[i])
        a_ref[rows, :] += dot_nn(wu_ref[h, g], gup_ref[...])
        return carry

    lax.fori_loop(0, halves * groups, down, 0)

    sum_e = jnp.zeros((8, seq), F32)
    sum_eu = jnp.zeros((8, seq), F32)
    for c in range(0, width, CH):
        s = slice(c, c + CH)
        gn = a_ref[s, :]
        u = u1_ref[s, :]
        acc_ref[1, s, :] += fold(gn * u)
        acc_ref[2, s, :] += fold(gn)
        e = gn * wide(vec_ref[1, s, :], seq)
        sum_e = sum_e + sub_sum(e)
        sum_eu = sum_eu + sub_sum(e * u)
    mean_e = jnp.sum(sum_e, axis=0, keepdims=True) * inv_width
    mean_eu = jnp.sum(sum_eu, axis=0, keepdims=True) * inv_width
    for c in range(0, width, CH):
        s = slice(c, c + CH)
        e = a_ref[s, :] * wide(vec_ref[1, s, :], seq)
        gr = r1 * (e - mean_e - u1_ref[s, :] * mean_eu)
        gr1_ref[0, s, :] = gr
        acc_ref[0, s, :] += fold(gr)
        gd_ref[s, :] = gr.astype(BF)
    for c in range(0, width, CH):
        s = slice(c, c + CH)
        ga = dot_nn(wo_ref[s, :], gd_ref[...]).astype(BF)
        gatt_ref[0, s, :] = ga
        prod = ga.astype(F32) * att_ref[0, s, :].astype(F32)
        for k in range(0, CH, HEAD_DIM):
            head = (c + k) // HEAD_DIM
            delta_ref[0, head : head + 1, :] = jnp.sum(prod[k : k + HEAD_DIM], axis=0, keepdims=True)
        dwo_ref[s, :] += dot_nt(att_ref[0, s, :], gd_ref[...])

    @pl.when(last)
    def _():
        dff_ref[:, :, group + 16 : 2 * group + 16, :] = dff_ref[:, :, group + 16 : 2 * group + 16, :] * 0.5
        for n in range(6):
            sums_ref[n : n + 1, :] = jnp.sum(acc_ref[n].T, axis=0, keepdims=True)
        sums_ref[6:8, :] = jnp.zeros((2, width), F32)


def feed(xt, att, cot, wot, wo, wu, wut, wd, wdt, vec):
    rows, width, seq = xt.shape
    halves, groups, group, part = wu.shape

    def whole(a):
        return pl.BlockSpec(a.shape, lambda r: (0,) * len(a.shape))

    per_row = pl.BlockSpec((1, width, seq), lambda r: (r, 0, 0))
    token = pl.BlockSpec((seq, width), lambda r: (r, 0))
    outs = [
        jax.ShapeDtypeStruct((rows * seq, width), F32),
        jax.ShapeDtypeStruct((rows, width, seq), F32),
        jax.ShapeDtypeStruct((rows, width, seq), BF),
        jax.ShapeDtypeStruct((rows, 16, seq), F32),
        jax.ShapeDtypeStruct((width, width), F32),
        jax.ShapeDtypeStruct((halves, groups, 2 * group + 32, part), F32),
        jax.ShapeDtypeStruct((8, width), F32),
    ]
    return pl.pallas_call(
        ffn_kernel,
        grid=(rows,),
        in_specs=[per_row, per_row, token] + [whole(a) for a in (wot, wo, wu, wut, wd, wdt, vec)],
        out_specs=[token, per_row, per_row, pl.BlockSpec((1, 16, seq), lambda r: (r, 0, 0))]
        + [whole(a) for a in outs[4:]],
        out_shape=outs,
        scratch_shapes=[
            pltpu.VMEM((width, seq), F32),
            pltpu.VMEM((width, seq), F32),
            pltpu.VMEM((width, seq), F32),
            pltpu.VMEM((groups, group + 16, seq), BF),
            pltpu.VMEM((halves * groups, part, seq), BF),
            pltpu.VMEM((halves * groups, part, seq), F32),
            pltpu.VMEM((width, seq), BF),
            pltpu.VMEM((part, seq), BF),
            pltpu.VMEM((width, seq), BF),
            pltpu.VMEM((6, width, 128), F32),
        ],
        compiler_params=params("arbitrary"),
        name="feed",
    )(xt, att, cot, wot, wo, wu, wut, wd, wdt, vec)


def split3(v):
    hi = v.astype(BF).astype(F32)
    mid = (v - hi).astype(BF).astype(F32)
    return hi, mid, v - hi - mid


def back_kernel(
    core_ref, qkv_ref, gatt_ref, xt_ref, gr1_ref, lse_ref, delta_ref, seg_ref, w_ref, *rest, head0, fresh, final, passed
):
    rest = list(rest)
    if passed:
        del rest[-12 - passed : -12]
    if not fresh:
        dwin_ref, bsin_ref = rest[:2]
    gin_ref = rest[-12]
    oa_ref, ob_ref = rest[-11:-9]
    qa_ref, ka_ref, va_ref, ga_ref, p_ref, ds_ref, d_ref, dw_ref, bsum_ref = rest[-9:]
    chans, seq = xt_ref.shape[1:]
    groups, group = w_ref.shape[1:3]
    first = pl.program_id(0) == 0
    last = pl.program_id(0) == pl.num_programs(0) - 1

    @pl.when(first)
    def _():
        if fresh:
            dw_ref[...] = jnp.zeros_like(dw_ref)
            bsum_ref[...] = jnp.zeros_like(bsum_ref)
        else:
            dw_ref[...] = dwin_ref[...]
            bsum_ref[...] = bsin_ref[...]

    seg = seg_ref[0]
    rank = lax.broadcasted_iota(jnp.int32, (16, seq), 0)
    same = rank == seg
    hot = jnp.where(same, 1.0, 0.0)
    ka_ref[64:80, :] = jnp.where(rank < 4, jnp.where(same, 0.0, NEG), jnp.where(rank < 7, -1.0, 0.0)).astype(BF)
    va_ref[64:80, :] = jnp.where(rank < 3, -1.0, 0.0).astype(BF)

    def head(h, carry):
        rows = pl.ds(pl.multiple_of(h * HEAD_DIM, HEAD_DIM), HEAD_DIM)
        hi, mid, lo = split3(lse_ref[0, pl.ds(head0 + h, 1), :])
        tail = jnp.where(rank == 4, hi, jnp.where(rank == 5, mid, jnp.where(rank == 6, lo, 0.0)))
        qa_ref[64:80, :] = jnp.where(rank < 4, hot, tail).astype(BF)
        hi, mid, lo = split3(delta_ref[0, pl.ds(head0 + h, 1), :])
        ga_ref[64:80, :] = jnp.where(rank == 0, hi, jnp.where(rank == 1, mid, jnp.where(rank == 2, lo, 0.0))).astype(BF)
        qs = qkv_ref[0, 0, rows, :] * jnp.asarray(0.125, BF)
        kt = qkv_ref[0, 1, rows, :]
        gt = gatt_ref[0, rows, :]
        qa_ref[0:64, :] = qs
        ka_ref[0:64, :] = kt
        va_ref[0:64, :] = qkv_ref[0, 2, rows, :]
        ga_ref[0:64, :] = gt
        kn = ka_ref[...].T
        vn = va_ref[...].T
        dk = jnp.zeros((HEAD_DIM, seq), F32)
        dv = jnp.zeros((HEAD_DIM, seq), F32)
        dq = []
        for t in range(seq // 256):
            cols = slice(t * 256, t * 256 + 256)
            p = jnp.exp(dot_nn(kn, qa_ref[:, cols]))
            p_ref[t] = p.astype(BF)
            ds_ref[t] = (p * dot_nn(vn, ga_ref[:, cols])).astype(BF)
            dv = dv + dot_nt(gt[:, cols], p_ref[t])
            dk = dk + dot_nt(qs[:, cols], ds_ref[t])
            dq.append(dot_nn(kt, ds_ref[t]) * 0.125)
        dq = jnp.concatenate(dq, axis=1)
        bsum_ref[0, rows, :] += fold(dq)
        bsum_ref[1, rows, :] += fold(dv)
        d_ref[0, rows, :] = dq.astype(BF)
        d_ref[1, rows, :] = dk.astype(BF)
        d_ref[2, rows, :] = dv.astype(BF)
        return carry

    lax.fori_loop(0, chans // HEAD_DIM, head, 0)
    parts = []
    for g in range(groups):
        s = slice(g * group, (g + 1) * group)
        total = gr1_ref[0, s, :]
        for j in range(3):
            d = d_ref[j, s, :]
            dw_ref[j, g] += dot_nt(xt_ref[0, s, :], d)
            total = total + dot_nn(w_ref[j, g], d)
        parts.append(total)
    gin_ref[...] = jnp.concatenate(parts, axis=0).T

    if not final:
        @pl.when(last)
        def _():
            oa_ref[...] = dw_ref[...]
            ob_ref[...] = bsum_ref[...]

    else:
        @pl.when(last)
        def _():
            half = PACK // 2
            core = core_ref[0]

            def put(row, value):
                rows = value.shape[0]
                where = row // half
                at = slice(row % half, row % half + rows)

                @pl.when(core == where)
                def _():
                    oa_ref[at, :] = value

                @pl.when(core != where)
                def _():
                    ob_ref[at, :] = value.astype(BF)

            tiles = chans // 128
            bias = jnp.concatenate([jnp.sum(bsum_ref[n].T, axis=0, keepdims=True) for n in range(2)], axis=0)
            bias = jnp.concatenate([bias, jnp.zeros((6, chans), F32)], axis=0)
            for j in range(3):
                both = jnp.concatenate([dw_ref[j, g] for g in range(groups)], axis=1)
                for c in range(tiles):
                    for a in range(0, group, 64):
                        put(c * 3 * group + j * group + a, both[a : a + 64, c * 128 : c * 128 + 128])
            for c in range(tiles):
                put(tiles * 3 * group + 8 * c, bias[:, c * 128 : c * 128 + 128])
            for row in range(tiles * 3 * group + 8 * tiles, PACK, 8):
                put(row, jnp.zeros((8, 128), F32))


PACK = 1792


def back(core, qkv, gatt, xt, gr1, lse, delta, seg, w, index, parts, row0, count, carried, into, final, sends, keeps):
    rows, _, width, seq = qkv.shape
    chans = width // parts
    groups, group = w.shape[1] // parts, w.shape[2]
    per_row = pl.BlockSpec((1, chans, seq), lambda r: (r + row0, index, 0))
    full = pl.BlockSpec((1, 16, seq), lambda r: (r + row0, 0, 0))
    in_specs = [
        pl.BlockSpec(memory_space=pltpu.SMEM),
        pl.BlockSpec((1, 3, chans, seq), lambda r: (r + row0, 0, index, 0)),
        per_row,
        per_row,
        per_row,
        full,
        full,
        pl.BlockSpec((1, 1, seq), lambda r: (r + row0, 0, 0)),
        pl.BlockSpec((3, groups, group, group), lambda r: (0, index, 0, 0)),
    ]
    args = [core, qkv, gatt, xt, gr1, lse, delta, seg.reshape(rows, 1, seq), w]
    sums = [jax.ShapeDtypeStruct((3, groups, group, group), F32), jax.ShapeDtypeStruct((2, chans, 128), F32)]
    if carried is not None:
        in_specs += [pl.BlockSpec((3, groups, group, group), lambda r: (0, 0, 0, 0)), pl.BlockSpec((2, chans, 128), lambda r: (0, 0, 0))]
        args += list(carried)
    alias = {}
    if into is not None:
        in_specs.append(pl.BlockSpec(memory_space=pl.ANY))
        args.append(into)
        alias = {len(args) - 1: len(keeps)}
    for n, value in enumerate(keeps):
        alias[len(args)] = n
        in_specs.append(pl.BlockSpec(memory_space=pl.ANY))
        args.append(value)
    for value in sends:
        in_specs.append(pl.BlockSpec(memory_space=pl.ANY))
        args.append(value)
    if final:
        outs = [jax.ShapeDtypeStruct((PACK // 2, 128), F32), jax.ShapeDtypeStruct((PACK // 2, 128), BF)]
    else:
        outs = sums
    return pl.pallas_call(
        partial(back_kernel, head0=index * (chans // HEAD_DIM), fresh=carried is None, final=final, passed=len(keeps)),
        grid=(count,),
        in_specs=in_specs,
        out_specs=[pl.BlockSpec(memory_space=pl.ANY) for _ in keeps]
        + [pl.BlockSpec((seq, chans), lambda r: (r + row0, index))]
        + [pl.BlockSpec(o.shape, lambda r, n=len(o.shape): (0,) * n) for o in outs],
        out_shape=[jax.ShapeDtypeStruct(value.shape, value.dtype) for value in keeps]
        + [jax.ShapeDtypeStruct((rows * seq, width), F32)]
        + outs,
        scratch_shapes=[pltpu.VMEM((80, seq), BF) for _ in range(4)]
        + [pltpu.VMEM((seq // 256, seq, 256), BF) for _ in range(2)]
        + [pltpu.VMEM((3, chans, seq), BF)]
        + [pltpu.VMEM(o.shape, F32) for o in sums],
        input_output_aliases=alias,
        compiler_params=params("arbitrary"),
        cost_estimate=pl.CostEstimate(flops=int(7e9 * count / 2), transcendentals=0, bytes_accessed=20 * 2**20),
        name="back",
    )(*args)


class Axis:
    def __init__(self, name, size, bit):
        self.name, self.pairs = name, [(i, i ^ bit) for i in range(size)]
        self.side = (lax.axis_index(name) // bit) % 2

    def swap(self, value):
        return lax.ppermute(value, self.name, self.pairs)

    def split(self, value):
        half = value.shape[0] // 2
        keep = lax.dynamic_slice_in_dim(value, self.side * half, half, 0)
        send = lax.dynamic_slice_in_dim(value, (1 - self.side) * half, half, 0)
        return keep, send.astype(BF)

    def join(self, value):
        other = self.swap(value)
        return jnp.where(self.side == 0, jnp.concatenate([value, other]), jnp.concatenate([other, value]))


def add(keep, got):
    return keep + got.astype(F32)


def sum_down(value, axes):
    for axis in axes:
        keep, send = axis.split(value)
        value = add(keep, axis.swap(send))
    return value


def sum_across(value, axes):
    low = value.astype(BF)
    for axis in axes:
        low = (low.astype(F32) + axis.swap(low).astype(F32)).astype(BF)
    return low


def gather_up(low, axes):
    for axis in reversed(axes):
        low = axis.join(low)
    return low


def per_device(
    inputs, segments, cotangent, qkv_weight, qv_bias, out_weight, out_bias, ln1_gain, ln1_bias,
    up_weight, up_bias, down_weight, down_bias, ln2_gain, ln2_bias, *, dp, ffn,
):
    width = inputs.shape[1]
    groups, group = qkv_weight.shape[1:3]
    part = up_weight.shape[2]
    assert ffn == 2
    bits = [Axis("dp", dp, 1 << k) for k in range(dp.bit_length() - 1)]
    core, ax, rest = bits[0], bits[1], bits[2:]
    ay = Axis("ffn", ffn, 1)

    up_aug = jnp.concatenate(
        [up_weight, up_bias[:, None, :], jnp.zeros((groups, 15, part), BF)], axis=1
    )
    up_all = lax.all_gather(up_aug, "ffn", axis=0)
    down_all = lax.all_gather(down_weight, "ffn", axis=0)

    def lanes(v):
        return jnp.broadcast_to(v[..., None], v.shape + (128,))

    bias = lanes(jnp.stack([qv_bias[0], jnp.zeros_like(qv_bias[0]), qv_bias[1]]))
    xt, qkv, att, lse = attend(inputs, segments, qkv_weight.swapaxes(2, 3), bias)
    vec = lanes(jnp.stack([out_bias, ln1_gain, ln1_bias, down_bias, ln2_gain, ln2_bias]))
    half = jnp.asarray(0.5, BF)
    layer_out, gr1, gatt, delta, dwo, dff, sums = feed(
        xt, att, cotangent, out_weight.T, out_weight,
        up_all[:, :, :group], up_all.swapaxes(2, 3), down_all * half, down_all.swapaxes(2, 3) * half, vec,
    )
    dff = lax.dynamic_update_slice(
        dff, jnp.broadcast_to(sums[:6].reshape(1, 1, 12, part), (2, 1, 12, part)), (0, 0, 2 * group + 16, 0)
    )

    core_id = core.side.astype(jnp.int32).reshape(1)
    rows = segments.shape[0]
    step = max(rows // 2, 1)
    parts = 2
    state = {"grad_inputs": None, "carried": None}
    packs = []

    def under(call, *stages):
        keeps, sends = [keep for _, keep, _ in stages], [send for _, _, send in stages]
        got = [axis.swap(send) for axis, _, send in stages]
        if call is not None:
            index, row0 = call
            final = row0 + step >= rows
            outs = back(
                core_id, qkv, gatt, xt, gr1, lse, delta, segments, qkv_weight, index, parts, row0, step,
                state["carried"], state["grad_inputs"], final, sends, keeps,
            )
            keeps, (state["grad_inputs"], *carried) = outs[: len(keeps)], outs[len(keeps) :]
            state["carried"] = None if final else carried
            if final:
                packs.append(carried)
        return [add(keep, arrived) for keep, arrived in zip(keeps, got)]

    calls = [(index, row0) for index in range(parts) for row0 in range(0, rows, step)]
    calls += [None] * (4 - len(calls))
    ffn1, out1 = under(calls[0], (core, *core.split(dff.swapaxes(0, 1))), (core, *core.split(dwo)))
    ffn2, out2 = under(calls[1], (ay, *ay.split(ffn1.swapaxes(0, 1))), (ax, *ax.split(out1)))
    ffn3, out3, sum0 = under(calls[2], (ax, *ax.split(ffn2[0])), (ay, *ay.split(out2)), (core, *packs[0]))
    low, olow = ffn3.astype(BF), out3.astype(BF)
    ffn4, out4, sum0 = under(
        calls[3], (rest[0], low.astype(F32), low), (rest[0], olow.astype(F32), olow), (ay, *ay.split(sum0))
    )
    own = gather_up(sum_across(ffn4, rest[1:]), [core, ax]).astype(F32)
    dwo = gather_up(sum_across(out4, rest[1:]), [core, ax, ay]).astype(F32)
    grad_inputs = state["grad_inputs"]
    totals = [gather_up(sum_across(sum_down(sum0, [ax]), rest), [core, ay, ax])]
    pkeep, psend = packs[1]
    first = add(pkeep, core.swap(psend))
    totals.append(gather_up(sum_across(sum_down(first, [ay, ax]), rest), [core, ay, ax]))
    grads, biases = [], []
    for total in totals:
        total = total.astype(F32)
        tiles = width // parts // 128
        body = total[: tiles * 3 * group].reshape(tiles, 3, group, 128).transpose(1, 2, 0, 3)
        body = body.reshape(3, group, groups // parts, group).swapaxes(1, 2)
        grads.append(body)
        tail = total[tiles * 3 * group : tiles * 3 * group + 8 * tiles].reshape(tiles, 8, 128)[:, :2]
        biases.append(tail.transpose(1, 0, 2).reshape(2, -1))
    dqkv = jnp.concatenate(grads, axis=1)
    qvb = jnp.concatenate(biases, axis=1)
    small = own[0, 2 * group + 16 : 2 * group + 28].reshape(6, width)
    return (
        layer_out,
        grad_inputs,
        dqkv,
        qvb,
        dwo,
        small[0],
        small[1],
        small[2],
        own[:, :group],
        own[:, group],
        own[:, group + 16 : 2 * group + 16],
        small[3],
        small[4],
        small[5],
    )


def solution(mesh):
    rows = P(("dp", "ffn"), None)
    shared = P()
    split = P(None, None, "ffn")
    return jax.shard_map(
        partial(per_device, dp=mesh.shape["dp"], ffn=mesh.shape["ffn"]),
        mesh=mesh,
        in_specs=(rows, rows, rows) + (shared,) * 6 + (split, P(None, "ffn"), split) + (shared,) * 3,
        out_specs=(rows, rows) + (shared,) * 6 + (split, P(None, "ffn"), split) + (shared,) * 3,
        check_vma=False,
    )


def specs(which):
    bf, f, i = jnp.bfloat16, jnp.float32, jnp.int32
    if which == "attend":
        return attend, [((2048, 768), bf), ((4, 512), i), ((3, 4, 192, 192), bf), ((3, 768, 128), f)]
    if which == "feed":
        return feed, [((4, 768, 512), bf), ((4, 768, 512), bf), ((2048, 768), bf), ((768, 768), bf), ((768, 768), bf), ((2, 4, 192, 384), bf),
                      ((2, 4, 384, 208), bf), ((2, 4, 192, 384), bf), ((2, 4, 384, 192), bf), ((6, 768, 128), f)]
    if which == "back":
        return (lambda *a: back(*a, 0, 2, None)), [((4, 3, 768, 512), bf), ((4, 768, 512), bf), ((4, 768, 512), bf), ((4, 768, 512), f),
                                                   ((4, 16, 512), f), ((4, 16, 512), f), ((4, 512), i), ((3, 4, 192, 192), bf)]
```

```python
from functools import partial

import jax
import jax.numpy as jnp
from jax import lax
from jax.experimental import pallas as pl
from jax.experimental.pallas import tpu as pltpu
from jax.sharding import PartitionSpec as P

HEADS = 12
HEAD_DIM = 64
EPS = 1e-05
NEG = -1e30
VMEM = 60 * 1024 * 1024
BF = jnp.bfloat16
F32 = jnp.float32


def dot_nn(a, b):
    return jnp.dot(a, b, preferred_element_type=F32)


def dot_nt(a, b):
    return lax.dot_general(a, b, (((1,), (1,)), ((), ())), preferred_element_type=F32)


def params(*sem):
    return pltpu.CompilerParams(vmem_limit_bytes=VMEM, dimension_semantics=sem)


def wide(column, lanes):
    return jnp.concatenate([column] * (lanes // 128), axis=1)


def fold(values):
    total = values[:, 0:128]
    for start in range(128, values.shape[1], 128):
        total = total + values[:, start : start + 128]
    return total


def sub_sum(values):
    total = values[0:8]
    for start in range(8, values.shape[0], 8):
        total = total + values[start : start + 8]
    return total


HB = 1
LT = 256


def attend_kernel(
    x_ref, seg_ref, w_ref, bias_in_ref, xt_ref, qkv_ref, att_ref, lse_ref,
    qa_ref, ka_ref, s_ref, p_ref, tot_ref, wt_ref, bias_ref,
):
    seq, width = x_ref.shape
    groups = wt_ref.shape[0]
    group = width // groups

    @pl.when(pl.program_id(0) == 0)
    def _():
        for g in range(groups):
            for j in range(3):
                wt_ref[g, j * group : (j + 1) * group, :] = w_ref[j, g].T
        columns = jnp.concatenate([bias_in_ref[...], jnp.zeros((6, width), F32)], axis=0).T
        for n in range(2):
            bias_ref[n] = jnp.broadcast_to(columns[:, n : n + 1], (width, 128))

    xt_ref[0] = x_ref[...].T
    seg = seg_ref[0]
    rank = lax.broadcasted_iota(jnp.int32, (16, seq), 0)
    same = rank == seg
    for n in range(2 * HB):
        qa_ref[n, 64:80, :] = jnp.where(same, 1.0, 0.0).astype(BF)
        ka_ref[n, 64:80, :] = jnp.where(same | (rank >= 4), 0.0, NEG).astype(BF)

    for g in range(groups):
        rows = slice(g * group, (g + 1) * group)
        out = dot_nn(wt_ref[g], xt_ref[0, rows, :])
        for j in range(3):
            part = out[j * group : (j + 1) * group]
            if j != 1:
                part = part + wide(bias_ref[j // 2, rows, :], seq)
            qkv_ref[0, j, rows, :] = part.astype(BF)

    def head_rows(h):
        return slice(h * HEAD_DIM, (h + 1) * HEAD_DIM)

    def scores(h, n):
        rows = head_rows(h)
        qa_ref[n, 0:64, :] = qkv_ref[0, 0, rows, :] * jnp.asarray(0.125, BF)
        ka_ref[n, 0:64, :] = qkv_ref[0, 1, rows, :]
        s_ref[n] = dot_nn(ka_ref[n].T, qa_ref[n])

    def soften(h, n):
        for l in range(0, seq, LT):
            cols = slice(l, l + LT)
            peak = s_ref[n, 0:8, cols]
            for c in range(8, seq, 8):
                peak = jnp.maximum(peak, s_ref[n, c : c + 8, cols])
            peak = jnp.max(peak, axis=0, keepdims=True)
            total = jnp.zeros((8, LT), F32)
            for c in range(0, seq, 16):
                e = jnp.exp(s_ref[n, c : c + 16, cols] - peak)
                total = total + (e[0:8] + e[8:16])
                p_ref[n, c : c + 16, cols] = e.astype(BF)
            total = jnp.sum(total, axis=0, keepdims=True)
            tot_ref[n, 0:1, cols] = 1.0 / total
            tot_ref[n, 1:2, cols] = peak + jnp.log(total)
        lse_ref[0, h : h + 1, :] = tot_ref[n, 1:2, :]

    def mix(h, n):
        rows = head_rows(h)
        att_ref[0, rows, :] = (dot_nn(qkv_ref[0, 2, rows, :], p_ref[n]) * tot_ref[n, 0:1, :]).astype(BF)

    G = HB
    def many(fn, b):
        for k in range(G):
            fn(b * G + k, (b % 2) * G + k)

    batches = HEADS // G
    for b in range(batches + 2):
        if b < batches:
            many(scores, b)
        if 0 <= b - 1 < batches:
            many(soften, b - 1)
        if 0 <= b - 2 < batches:
            many(mix, b - 2)


def attend(x, seg, w, bias):
    width = x.shape[1]
    groups, group = w.shape[1:3]
    rows, seq = seg.shape
    return pl.pallas_call(
        attend_kernel,
        grid=(rows,),
        in_specs=[
            pl.BlockSpec((seq, width), lambda r: (r, 0)),
            pl.BlockSpec((1, 1, seq), lambda r: (r, 0, 0)),
            pl.BlockSpec(w.shape, lambda r: (0, 0, 0, 0)),
            pl.BlockSpec(bias.shape, lambda r: (0, 0)),
        ],
        out_specs=[
            pl.BlockSpec((1, width, seq), lambda r: (r, 0, 0)),
            pl.BlockSpec((1, 3, width, seq), lambda r: (r, 0, 0, 0)),
            pl.BlockSpec((1, width, seq), lambda r: (r, 0, 0)),
            pl.BlockSpec((1, 16, seq), lambda r: (r, 0, 0)),
        ],
        out_shape=[
            jax.ShapeDtypeStruct((rows, width, seq), BF),
            jax.ShapeDtypeStruct((rows, 3, width, seq), BF),
            jax.ShapeDtypeStruct((rows, width, seq), BF),
            jax.ShapeDtypeStruct((rows, 16, seq), F32),
        ],
        scratch_shapes=[pltpu.VMEM((2*HB, 80, seq), BF), pltpu.VMEM((2*HB, 80, seq), BF), pltpu.VMEM((2*HB, seq, seq), F32), pltpu.VMEM((2*HB, seq, seq), BF), pltpu.VMEM((2*HB, 8, seq), F32)]
        + [pltpu.VMEM((groups, 3 * group, group), BF), pltpu.VMEM((2, width, 128), F32)],
        compiler_params=params("arbitrary"),
        name="attend",
    )(x, seg.reshape(rows, 1, seq), w, bias)

CH = 64
EC = 64
DU = 768
DO = 384
ROOT_HALF = 0.7071067811865476
LOG2E = 1.4426950408889634


def feed_kernel(
    core_ref, xt_ref, att_ref, cot_ref, wo_ref, wall_ref, vec_in_ref,
    out_ref, gr1_ref, gatt_ref, delta_ref, keep_ref, send_ref, okeep_ref, osend_ref,
    a_ref, u1_ref, v2_ref, nlow_ref, act_ref, gp_ref, gd_ref, gup_ref, ct_ref, acc_ref,
    wot_ref, wut_ref, wdt_ref, vec_ref, dwo_ref, dff_ref,
):
    width, seq = a_ref.shape
    halves, groups = wall_ref.shape[:2]
    group = width // groups
    part = wall_ref.shape[3]
    full = halves * part
    first = pl.program_id(0) == 0
    last = pl.program_id(0) == pl.num_programs(0) - 1
    inv_width = 1.0 / width
    aug = group + 16

    @pl.when(first)
    def _():
        acc_ref[...] = jnp.zeros_like(acc_ref)
        dwo_ref[...] = jnp.zeros_like(dwo_ref)
        dff_ref[...] = jnp.zeros_like(dff_ref)
        row = lax.broadcasted_iota(jnp.int32, (16, seq), 0)
        for g in range(groups):
            nlow_ref[g, group:aug, :] = jnp.where(row == 0, 1.0, 0.0).astype(BF)
        columns = vec_in_ref[...].T
        for n in range(6):
            vec_ref[n] = jnp.broadcast_to(columns[:, n : n + 1], (width, 128))
        wot_ref[...] = wo_ref[...].T

        def prepare(i, carry):
            h, g = i // groups, i % groups
            rows = pl.ds(pl.multiple_of(h * part, part), part)
            wut_ref[g, rows, :] = wall_ref[h, g, 0:aug, :].T
            wdt_ref[g, rows, :] = (wall_ref[h, g, aug : aug + group, :] * jnp.asarray(0.5, BF)).T
            return carry

        lax.fori_loop(0, halves * groups, prepare, 0)

    ct_ref[...] = cot_ref[...].T

    part_sum = jnp.zeros((8, seq), F32)
    for b in range(0, width, DO):
        mixed = dot_nn(wot_ref[b : b + DO, :], att_ref[0])
        for c in range(0, DO, EC):
            s = slice(b + c, b + c + EC)
            v = mixed[c : c + EC] + wide(vec_ref[0, s, :], seq) + xt_ref[0, s, :].astype(F32)
            a_ref[s, :] = v
            part_sum = part_sum + sub_sum(v)
    mean = jnp.sum(part_sum, axis=0, keepdims=True) * inv_width
    part_sum = jnp.zeros((8, seq), F32)
    for c in range(0, width, CH):
        v = a_ref[c : c + CH, :] - mean
        part_sum = part_sum + sub_sum(v * v)
    r1 = lax.rsqrt(jnp.sum(part_sum, axis=0, keepdims=True) * inv_width + EPS)
    for g in range(groups):
        for c in range(0, group, 64):
            s = slice(g * group + c, g * group + c + 64)
            u = (a_ref[s, :] - mean) * r1
            u1_ref[s, :] = u
            n = u * wide(vec_ref[1, s, :], seq) + wide(vec_ref[2, s, :], seq)
            v2_ref[s, :] = n
            nlow_ref[g, c : c + 64, :] = n.astype(BF)

    part_sum = jnp.zeros((8, seq), F32)
    for g in range(groups):
        for b in range(0, full, DU):
            upward = dot_nn(wut_ref[g, b : b + DU, :], nlow_ref[g])
            for c in range(0, DU, EC):
                s = slice(b + c, b + c + EC)
                u = upward[c : c + EC]
                one = 1.0 + lax.erf(u * ROOT_HALF)
                act_ref[g, s, :] = (u * one).astype(BF)
                bell = jnp.exp2((u * u) * (-0.5 * LOG2E))
                gp_ref[g, s, :] = one + (u * (1.1283791670955126 * ROOT_HALF)) * bell
        s = slice(g * group, (g + 1) * group)
        down = dot_nn(wall_ref[0, g, aug : aug + group, :], act_ref[g, 0:part, :])
        for h in range(1, halves):
            down = down + dot_nn(wall_ref[h, g, aug : aug + group, :], act_ref[g, h * part : (h + 1) * part, :])
        v = v2_ref[s, :] + (down * 0.5 + wide(vec_ref[3, s, :], seq))
        v2_ref[s, :] = v
        part_sum = part_sum + sub_sum(v)

    mean = jnp.sum(part_sum, axis=0, keepdims=True) * inv_width
    part_sum = jnp.zeros((8, seq), F32)
    for c in range(0, width, CH):
        v = v2_ref[c : c + CH, :] - mean
        part_sum = part_sum + sub_sum(v * v)
    r2 = lax.rsqrt(jnp.sum(part_sum, axis=0, keepdims=True) * inv_width + EPS)
    sum_e = jnp.zeros((8, seq), F32)
    sum_eu = jnp.zeros((8, seq), F32)
    for c in range(0, width, CH):
        s = slice(c, c + CH)
        u = (v2_ref[s, :] - mean) * r2
        v2_ref[s, :] = u
        gain = wide(vec_ref[4, s, :], seq)
        out_ref[:, s] = (u * gain + wide(vec_ref[5, s, :], seq)).T
        cot = ct_ref[s, :].astype(F32)
        cu = cot * u
        acc_ref[4, s, :] += fold(cu)
        acc_ref[5, s, :] += fold(cot)
        sum_e = sum_e + sub_sum(cot * gain)
        sum_eu = sum_eu + sub_sum(cu * gain)
    mean_e = jnp.sum(sum_e, axis=0, keepdims=True) * inv_width
    mean_eu = jnp.sum(sum_eu, axis=0, keepdims=True) * inv_width
    for c in range(0, width, CH):
        s = slice(c, c + CH)
        e = ct_ref[s, :].astype(F32) * wide(vec_ref[4, s, :], seq)
        gr = r2 * (e - mean_e - v2_ref[s, :] * mean_eu)
        a_ref[s, :] = gr
        acc_ref[3, s, :] += fold(gr)
        gd_ref[s, :] = gr.astype(BF)

    for g in range(groups):
        rows = slice(g * group, (g + 1) * group)
        for b in range(0, full, DU):
            gact = dot_nn(wdt_ref[g, b : b + DU, :], gd_ref[rows, :])
            for c in range(0, DU, EC):
                s = slice(b + c, b + c + EC)
                gup_ref[g % 2, s, :] = (gact[c : c + EC] * gp_ref[g, s, :]).astype(BF)
        for h in range(halves):
            s = slice(h * part, (h + 1) * part)
            dff_ref[h, g, aug : aug + group, :] += dot_nt(gd_ref[rows, :], act_ref[g, s, :])
            dff_ref[h, g, 0:aug, :] += dot_nt(nlow_ref[g], gup_ref[g % 2, s, :])
        back = dot_nn(wall_ref[0, g, 0:group, :], gup_ref[g % 2, 0:part, :])
        for h in range(1, halves):
            back = back + dot_nn(wall_ref[h, g, 0:group, :], gup_ref[g % 2, h * part : (h + 1) * part, :])
        a_ref[rows, :] += back

    sum_e = jnp.zeros((8, seq), F32)
    sum_eu = jnp.zeros((8, seq), F32)
    for c in range(0, width, CH):
        s = slice(c, c + CH)
        gn = a_ref[s, :]
        gu = gn * u1_ref[s, :]
        acc_ref[1, s, :] += fold(gu)
        acc_ref[2, s, :] += fold(gn)
        gain = wide(vec_ref[1, s, :], seq)
        sum_e = sum_e + sub_sum(gn * gain)
        sum_eu = sum_eu + sub_sum(gu * gain)
    mean_e = jnp.sum(sum_e, axis=0, keepdims=True) * inv_width
    mean_eu = jnp.sum(sum_eu, axis=0, keepdims=True) * inv_width
    for c in range(0, width, CH):
        s = slice(c, c + CH)
        e = a_ref[s, :] * wide(vec_ref[1, s, :], seq)
        gr = r1 * (e - mean_e - u1_ref[s, :] * mean_eu)
        gr1_ref[0, s, :] = gr
        acc_ref[0, s, :] += fold(gr)
        gd_ref[s, :] = gr.astype(BF)
    for b in range(0, width, DO):
        grad = dot_nn(wo_ref[b : b + DO, :], gd_ref[...])
        for c in range(0, DO, HEAD_DIM):
            s = slice(b + c, b + c + HEAD_DIM)
            ga = grad[c : c + HEAD_DIM].astype(BF)
            gatt_ref[0, s, :] = ga
            prod = ga.astype(F32) * att_ref[0, s, :].astype(F32)
            head = (b + c) // HEAD_DIM
            delta_ref[0, head : head + 1, :] = jnp.sum(prod, axis=0, keepdims=True)
    half = width // 2
    for k in range(2):
        dwo_ref[k] += dot_nt(att_ref[0, k * half : (k + 1) * half, :], gd_ref[...])

    @pl.when(last)
    def _():
        for n in range(6):
            line = jnp.sum(acc_ref[n].T, axis=0, keepdims=True)
            for k in range(width // part):
                for h in range(halves):
                    at = aug + group + n * (width // part) + k
                    dff_ref[h, 0, at : at + 1, :] = line[:, k * part : (k + 1) * part]
        core = core_ref[0]
        okeep_ref[...] = dwo_ref[core]
        osend_ref[...] = dwo_ref[1 - core].astype(BF)
        two = groups // 2

        def hand(i, carry):
            h, k = i // two, i % two
            for ref, g in ((keep_ref, core * two + k), (send_ref, (1 - core) * two + k)):
                ref[h, k, 0:aug, :] = dff_ref[h, g, 0:aug, :].astype(ref.dtype)
                ref[h, k, aug : aug + group, :] = (dff_ref[h, g, aug : aug + group, :] * 0.5).astype(ref.dtype)
                ref[h, k, aug + group :, :] = dff_ref[h, g, aug + group :, :].astype(ref.dtype)
            return carry

        lax.fori_loop(0, halves * two, hand, 0)


def feed(core, xt, att, cot, wo, wall, vec):
    rows, width, seq = xt.shape
    halves, groups, depth, part = wall.shape
    group = width // groups
    aug = group + 16
    full = halves * part

    def whole(a):
        return pl.BlockSpec(a.shape, lambda r: (0,) * len(a.shape), pipeline_mode=pl.Buffered(1))

    per_row = pl.BlockSpec((1, width, seq), lambda r: (r, 0, 0))
    token = pl.BlockSpec((seq, width), lambda r: (r, 0))
    sums = (halves, groups // 2, 2 * group + 32, part)
    outs = [
        jax.ShapeDtypeStruct((rows * seq, width), F32),
        jax.ShapeDtypeStruct((rows, width, seq), F32),
        jax.ShapeDtypeStruct((rows, width, seq), BF),
        jax.ShapeDtypeStruct((rows, 16, seq), F32),
        jax.ShapeDtypeStruct(sums, F32),
        jax.ShapeDtypeStruct(sums, BF),
        jax.ShapeDtypeStruct((width // 2, width), F32),
        jax.ShapeDtypeStruct((width // 2, width), BF),
    ]
    return pl.pallas_call(
        feed_kernel,
        grid=(rows,),
        in_specs=[pl.BlockSpec(memory_space=pltpu.SMEM), per_row, per_row, token] + [whole(a) for a in (wo, wall, vec)],
        out_specs=[token, per_row, per_row, pl.BlockSpec((1, 16, seq), lambda r: (r, 0, 0))]
        + [whole(a) for a in outs[4:]],
        out_shape=outs,
        scratch_shapes=[
            pltpu.VMEM((width, seq), F32),
            pltpu.VMEM((width, seq), F32),
            pltpu.VMEM((width, seq), F32),
            pltpu.VMEM((groups, aug, seq), BF),
            pltpu.VMEM((groups, full, seq), BF),
            pltpu.VMEM((groups, full, seq), F32),
            pltpu.VMEM((width, seq), BF),
            pltpu.VMEM((2, full, seq), BF),
            pltpu.VMEM((width, seq), BF),
            pltpu.VMEM((6, width, 128), F32),
            pltpu.VMEM((width, width), BF),
            pltpu.VMEM((groups, full, aug), BF),
            pltpu.VMEM((groups, full, group), BF),
            pltpu.VMEM((6, width, 128), F32),
            pltpu.VMEM((2, width // 2, width), F32),
            pltpu.VMEM((halves, groups, 2 * group + 32, part), F32),
        ],
        compiler_params=pltpu.CompilerParams(vmem_limit_bytes=63 * 2**20),
        name="feed",
    )(core, xt, att, cot, wo, wall, vec)


def split3(v):
    hi = v.astype(BF).astype(F32)
    mid = (v - hi).astype(BF).astype(F32)
    return hi, mid, v - hi - mid


def back_kernel(
    core_ref, qkv_ref, gatt_ref, xt_ref, gr1_ref, lse_ref, delta_ref, seg_ref, w_ref, *rest, head0, fresh, final, passed
):
    rest = list(rest)
    if passed:
        del rest[-12 - passed : -12]
    if not fresh:
        dwin_ref, bsin_ref = rest[:2]
    gin_ref = rest[-12]
    oa_ref, ob_ref = rest[-11:-9]
    qa_ref, ka_ref, va_ref, ga_ref, p_ref, ds_ref, d_ref, dw_ref, bsum_ref = rest[-9:]
    chans, seq = xt_ref.shape[1:]
    groups, group = w_ref.shape[1:3]
    first = pl.program_id(0) == 0
    last = pl.program_id(0) == pl.num_programs(0) - 1

    @pl.when(first)
    def _():
        if fresh:
            dw_ref[...] = jnp.zeros_like(dw_ref)
            bsum_ref[...] = jnp.zeros_like(bsum_ref)
        else:
            dw_ref[...] = dwin_ref[...]
            bsum_ref[...] = bsin_ref[...]

    seg = seg_ref[0]
    rank = lax.broadcasted_iota(jnp.int32, (16, seq), 0)
    same = rank == seg
    hot = jnp.where(same, 1.0, 0.0)
    ka_ref[64:80, :] = jnp.where(rank < 4, jnp.where(same, 0.0, NEG), jnp.where(rank < 7, -1.0, 0.0)).astype(BF)
    va_ref[64:80, :] = jnp.where(rank < 3, -1.0, 0.0).astype(BF)

    def head(h, carry):
        rows = pl.ds(pl.multiple_of(h * HEAD_DIM, HEAD_DIM), HEAD_DIM)
        hi, mid, lo = split3(lse_ref[0, pl.ds(head0 + h, 1), :])
        tail = jnp.where(rank == 4, hi, jnp.where(rank == 5, mid, jnp.where(rank == 6, lo, 0.0)))
        qa_ref[64:80, :] = jnp.where(rank < 4, hot, tail).astype(BF)
        hi, mid, lo = split3(delta_ref[0, pl.ds(head0 + h, 1), :])
        ga_ref[64:80, :] = jnp.where(rank == 0, hi, jnp.where(rank == 1, mid, jnp.where(rank == 2, lo, 0.0))).astype(BF)
        qs = qkv_ref[0, 0, rows, :] * jnp.asarray(0.125, BF)
        kt = qkv_ref[0, 1, rows, :]
        gt = gatt_ref[0, rows, :]
        qa_ref[0:64, :] = qs
        ka_ref[0:64, :] = kt
        va_ref[0:64, :] = qkv_ref[0, 2, rows, :]
        ga_ref[0:64, :] = gt
        kn = ka_ref[...].T
        vn = va_ref[...].T
        dk = jnp.zeros((HEAD_DIM, seq), F32)
        dv = jnp.zeros((HEAD_DIM, seq), F32)
        dq = []
        for t in range(seq // 256):
            cols = slice(t * 256, t * 256 + 256)
            p = jnp.exp(dot_nn(kn, qa_ref[:, cols]))
            p_ref[t] = p.astype(BF)
            ds_ref[t] = (p * dot_nn(vn, ga_ref[:, cols])).astype(BF)
            dv = dv + dot_nt(gt[:, cols], p_ref[t])
            dk = dk + dot_nt(qs[:, cols], ds_ref[t])
            dq.append(dot_nn(kt, ds_ref[t]) * 0.125)
        dq = jnp.concatenate(dq, axis=1)
        bsum_ref[0, rows, :] += fold(dq)
        bsum_ref[1, rows, :] += fold(dv)
        d_ref[0, rows, :] = dq.astype(BF)
        d_ref[1, rows, :] = dk.astype(BF)
        d_ref[2, rows, :] = dv.astype(BF)
        return carry

    lax.fori_loop(0, chans // HEAD_DIM, head, 0)
    parts = []
    for g in range(groups):
        s = slice(g * group, (g + 1) * group)
        total = gr1_ref[0, s, :]
        for j in range(3):
            d = d_ref[j, s, :]
            dw_ref[j, g] += dot_nt(xt_ref[0, s, :], d)
            total = total + dot_nn(w_ref[j, g], d)
        parts.append(total)
    gin_ref[...] = jnp.concatenate(parts, axis=0).T

    if not final:
        @pl.when(last)
        def _():
            oa_ref[...] = dw_ref[...]
            ob_ref[...] = bsum_ref[...]

    else:
        @pl.when(last)
        def _():
            half = PACK // 2
            core = core_ref[0]

            def put(row, value):
                rows = value.shape[0]
                where = row // half
                at = slice(row % half, row % half + rows)

                @pl.when(core == where)
                def _():
                    oa_ref[at, :] = value

                @pl.when(core != where)
                def _():
                    ob_ref[at, :] = value.astype(BF)

            tiles = chans // 128
            bias = jnp.concatenate([jnp.sum(bsum_ref[n].T, axis=0, keepdims=True) for n in range(2)], axis=0)
            bias = jnp.concatenate([bias, jnp.zeros((6, chans), F32)], axis=0)
            for j in range(3):
                both = jnp.concatenate([dw_ref[j, g] for g in range(groups)], axis=1)
                for c in range(tiles):
                    for a in range(0, group, 64):
                        put(c * 3 * group + j * group + a, both[a : a + 64, c * 128 : c * 128 + 128])
            for c in range(tiles):
                put(tiles * 3 * group + 8 * c, bias[:, c * 128 : c * 128 + 128])
            for row in range(tiles * 3 * group + 8 * tiles, PACK, 8):
                put(row, jnp.zeros((8, 128), F32))


PACK = 1792


def back(core, qkv, gatt, xt, gr1, lse, delta, seg, w, index, parts, row0, count, carried, into, final, sends, keeps):
    rows, _, width, seq = qkv.shape
    chans = width // parts
    groups, group = w.shape[1] // parts, w.shape[2]
    per_row = pl.BlockSpec((1, chans, seq), lambda r: (r + row0, index, 0))
    full = pl.BlockSpec((1, 16, seq), lambda r: (r + row0, 0, 0))
    in_specs = [
        pl.BlockSpec(memory_space=pltpu.SMEM),
        pl.BlockSpec((1, 3, chans, seq), lambda r: (r + row0, 0, index, 0)),
        per_row,
        per_row,
        per_row,
        full,
        full,
        pl.BlockSpec((1, 1, seq), lambda r: (r + row0, 0, 0)),
        pl.BlockSpec((3, groups, group, group), lambda r: (0, index, 0, 0)),
    ]
    args = [core, qkv, gatt, xt, gr1, lse, delta, seg.reshape(rows, 1, seq), w]
    sums = [jax.ShapeDtypeStruct((3, groups, group, group), F32), jax.ShapeDtypeStruct((2, chans, 128), F32)]
    if carried is not None:
        in_specs += [pl.BlockSpec((3, groups, group, group), lambda r: (0, 0, 0, 0)), pl.BlockSpec((2, chans, 128), lambda r: (0, 0, 0))]
        args += list(carried)
    alias = {}
    if into is not None:
        in_specs.append(pl.BlockSpec(memory_space=pl.ANY))
        args.append(into)
        alias = {len(args) - 1: len(keeps)}
    for n, value in enumerate(keeps):
        alias[len(args)] = n
        in_specs.append(pl.BlockSpec(memory_space=pl.ANY))
        args.append(value)
    for value in sends:
        in_specs.append(pl.BlockSpec(memory_space=pl.ANY))
        args.append(value)
    if final:
        outs = [jax.ShapeDtypeStruct((PACK // 2, 128), F32), jax.ShapeDtypeStruct((PACK // 2, 128), BF)]
    else:
        outs = sums
    return pl.pallas_call(
        partial(back_kernel, head0=index * (chans // HEAD_DIM), fresh=carried is None, final=final, passed=len(keeps)),
        grid=(count,),
        in_specs=in_specs,
        out_specs=[pl.BlockSpec(memory_space=pl.ANY) for _ in keeps]
        + [pl.BlockSpec((seq, chans), lambda r: (r + row0, index))]
        + [pl.BlockSpec(o.shape, lambda r, n=len(o.shape): (0,) * n) for o in outs],
        out_shape=[jax.ShapeDtypeStruct(value.shape, value.dtype) for value in keeps]
        + [jax.ShapeDtypeStruct((rows * seq, width), F32)]
        + outs,
        scratch_shapes=[pltpu.VMEM((80, seq), BF) for _ in range(4)]
        + [pltpu.VMEM((seq // 256, seq, 256), BF) for _ in range(2)]
        + [pltpu.VMEM((3, chans, seq), BF)]
        + [pltpu.VMEM(o.shape, F32) for o in sums],
        input_output_aliases=alias,
        compiler_params=params("arbitrary"),
        cost_estimate=pl.CostEstimate(flops=int(7e9 * count / 2), transcendentals=0, bytes_accessed=20 * 2**20),
        name="back",
    )(*args)


class Axis:
    def __init__(self, name, size, bit):
        self.name, self.pairs = name, [(i, i ^ bit) for i in range(size)]
        self.side = (lax.axis_index(name) // bit) % 2

    def swap(self, value):
        return lax.ppermute(value, self.name, self.pairs)

    def split(self, value):
        half = value.shape[0] // 2
        keep = lax.dynamic_slice_in_dim(value, self.side * half, half, 0)
        send = lax.dynamic_slice_in_dim(value, (1 - self.side) * half, half, 0)
        return keep, send.astype(BF)

    def join(self, value):
        other = self.swap(value)
        return jnp.where(self.side == 0, jnp.concatenate([value, other]), jnp.concatenate([other, value]))


def add(keep, got):
    return keep + got.astype(F32)


def sum_down(value, axes):
    for axis in axes:
        keep, send = axis.split(value)
        value = add(keep, axis.swap(send))
    return value


def sum_across(value, axes):
    low = value.astype(BF)
    for axis in axes:
        low = (low.astype(F32) + axis.swap(low).astype(F32)).astype(BF)
    return low


def gather_up(low, axes):
    for axis in reversed(axes):
        low = axis.join(low)
    return low


def per_device(
    inputs, segments, cotangent, qkv_weight, qv_bias, out_weight, out_bias, ln1_gain, ln1_bias,
    up_weight, up_bias, down_weight, down_bias, ln2_gain, ln2_bias, *, dp, ffn,
):
    width = inputs.shape[1]
    groups, group = qkv_weight.shape[1:3]
    part = up_weight.shape[2]
    assert ffn == 2
    bits = [Axis("dp", dp, 1 << k) for k in range(dp.bit_length() - 1)]
    core, ax, rest = bits[0], bits[1], bits[2:]
    ay = Axis("ffn", ffn, 1)

    wall = jnp.concatenate(
        [up_weight, up_bias[:, None, :], jnp.zeros((groups, 15, part), BF), down_weight], axis=1
    )
    wall = lax.all_gather(wall, "ffn", axis=0)
    core_id = core.side.astype(jnp.int32).reshape(1)
    zero = jnp.zeros_like(out_bias)
    vec = jnp.stack([out_bias, ln1_gain, ln1_bias, down_bias, ln2_gain, ln2_bias, zero, zero])
    xt, qkv, att, lse = attend(inputs, segments, qkv_weight, qv_bias)
    layer_out, gr1, gatt, delta, *first = feed(core_id, xt, att, cotangent, out_weight, wall, vec)
    rows = segments.shape[0]
    step = max(rows // 2, 1)
    parts = 2
    state = {"grad_inputs": None, "carried": None}
    packs = []

    def under(call, *stages):
        keeps, sends = [keep for _, keep, _ in stages], [send for _, _, send in stages]
        got = [axis.swap(send) for axis, _, send in stages]
        if call is not None:
            index, row0 = call
            final = row0 + step >= rows
            outs = back(
                core_id, qkv, gatt, xt, gr1, lse, delta, segments, qkv_weight, index, parts, row0, step,
                state["carried"], state["grad_inputs"], final, sends, keeps,
            )
            keeps, (state["grad_inputs"], *carried) = outs[: len(keeps)], outs[len(keeps) :]
            state["carried"] = None if final else carried
            if final:
                packs.append(carried)
        return [add(keep, arrived) for keep, arrived in zip(keeps, got)]

    calls = [(index, row0) for index in range(parts) for row0 in range(0, rows, step)]
    calls += [None] * (4 - len(calls))
    ffn1, out1 = under(calls[0], (core, *first[:2]), (core, *first[2:]))
    ffn2, out2 = under(calls[1], (ay, *ay.split(ffn1)), (ax, *ax.split(out1)))
    ffn3, out3, sum0 = under(calls[2], (ax, *ax.split(ffn2[0])), (ay, *ay.split(out2)), (core, *packs[0]))
    low, olow = ffn3.astype(BF), out3.astype(BF)
    ffn4, out4, sum0 = under(
        calls[3], (rest[0], low.astype(F32), low), (rest[0], olow.astype(F32), olow), (ay, *ay.split(sum0))
    )
    own = gather_up(sum_across(ffn4, rest[1:]), [core, ax]).astype(F32)
    dwo = gather_up(sum_across(out4, rest[1:]), [core, ax, ay]).astype(F32)
    grad_inputs = state["grad_inputs"]
    totals = [gather_up(sum_across(sum_down(sum0, [ax]), rest), [core, ay, ax])]
    pkeep, psend = packs[1]
    last = add(pkeep, core.swap(psend))
    totals.append(gather_up(sum_across(sum_down(last, [ay, ax]), rest), [core, ay, ax]))
    grads, biases = [], []
    for total in totals:
        total = total.astype(F32)
        tiles = width // parts // 128
        body = total[: tiles * 3 * group].reshape(tiles, 3, group, 128).transpose(1, 2, 0, 3)
        body = body.reshape(3, group, groups // parts, group).swapaxes(1, 2)
        grads.append(body)
        tail = total[tiles * 3 * group : tiles * 3 * group + 8 * tiles].reshape(tiles, 8, 128)[:, :2]
        biases.append(tail.transpose(1, 0, 2).reshape(2, -1))
    dqkv = jnp.concatenate(grads, axis=1)
    qvb = jnp.concatenate(biases, axis=1)
    small = own[0, 2 * group + 16 : 2 * group + 28].reshape(6, width)
    return (
        layer_out,
        grad_inputs,
        dqkv,
        qvb,
        dwo,
        small[0],
        small[1],
        small[2],
        own[:, :group],
        own[:, group],
        own[:, group + 16 : 2 * group + 16],
        small[3],
        small[4],
        small[5],
    )


def solution(mesh):
    rows = P(("dp", "ffn"), None)
    shared = P()
    split = P(None, None, "ffn")
    return jax.shard_map(
        partial(per_device, dp=mesh.shape["dp"], ffn=mesh.shape["ffn"]),
        mesh=mesh,
        in_specs=(rows, rows, rows) + (shared,) * 6 + (split, P(None, "ffn"), split) + (shared,) * 3,
        out_specs=(rows, rows) + (shared,) * 6 + (split, P(None, "ffn"), split) + (shared,) * 3,
        check_vma=False,
    )
```

```python
from functools import partial

import jax
import jax.numpy as jnp
from jax import lax
from jax.experimental import pallas as pl
from jax.experimental.pallas import tpu as pltpu
from jax.sharding import PartitionSpec as P

HEADS = 12
HEAD_DIM = 64
EPS = 1e-05
NEG = -1e30
VMEM = 60 * 1024 * 1024
BF = jnp.bfloat16
F32 = jnp.float32


def dot_nn(a, b):
    return jnp.dot(a, b, preferred_element_type=F32)


def dot_nt(a, b):
    return lax.dot_general(a, b, (((1,), (1,)), ((), ())), preferred_element_type=F32)


def params(*sem):
    return pltpu.CompilerParams(vmem_limit_bytes=VMEM, dimension_semantics=sem)


def wide(column, lanes):
    return jnp.concatenate([column] * (lanes // 128), axis=1)


def fold(values):
    total = values[:, 0:128]
    for start in range(128, values.shape[1], 128):
        total = total + values[:, start : start + 128]
    return total


def sub_sum(values):
    total = values[0:8]
    for start in range(8, values.shape[0], 8):
        total = total + values[start : start + 8]
    return total


HB = 1
LT = 256


def attend_kernel(
    x_ref, seg_ref, w_ref, bias_in_ref, xt_ref, qkv_ref, att_ref, lse_ref,
    qa_ref, ka_ref, s_ref, p_ref, tot_ref, wt_ref, bias_ref,
):
    seq, width = x_ref.shape
    groups = wt_ref.shape[0]
    group = width // groups

    @pl.when(pl.program_id(0) == 0)
    def _():
        for g in range(groups):
            for j in range(3):
                wt_ref[g, j * group : (j + 1) * group, :] = w_ref[j, g].T
        columns = jnp.concatenate([bias_in_ref[...], jnp.zeros((6, width), F32)], axis=0).T
        for n in range(2):
            bias_ref[n] = jnp.broadcast_to(columns[:, n : n + 1], (width, 128))

    xt_ref[0] = x_ref[...].T
    seg = seg_ref[0]
    rank = lax.broadcasted_iota(jnp.int32, (16, seq), 0)
    same = rank == seg
    for n in range(2 * HB):
        qa_ref[n, 64:80, :] = jnp.where(same, 1.0, 0.0).astype(BF)
        ka_ref[n, 64:80, :] = jnp.where(same | (rank >= 4), 0.0, NEG).astype(BF)

    for g in range(groups):
        rows = slice(g * group, (g + 1) * group)
        out = dot_nn(wt_ref[g], xt_ref[0, rows, :])
        for j in range(3):
            part = out[j * group : (j + 1) * group]
            if j != 1:
                part = part + wide(bias_ref[j // 2, rows, :], seq)
            qkv_ref[0, j, rows, :] = part.astype(BF)

    def head_rows(h):
        return slice(h * HEAD_DIM, (h + 1) * HEAD_DIM)

    def scores(h, n):
        rows = head_rows(h)
        qa_ref[n, 0:64, :] = qkv_ref[0, 0, rows, :] * jnp.asarray(0.125, BF)
        ka_ref[n, 0:64, :] = qkv_ref[0, 1, rows, :]
        s_ref[n] = dot_nn(ka_ref[n].T, qa_ref[n])

    def soften(h, n):
        for l in range(0, seq, LT):
            cols = slice(l, l + LT)
            peak = s_ref[n, 0:8, cols]
            for c in range(8, seq, 8):
                peak = jnp.maximum(peak, s_ref[n, c : c + 8, cols])
            peak = jnp.max(peak, axis=0, keepdims=True)
            total = jnp.zeros((8, LT), F32)
            for c in range(0, seq, 16):
                e = jnp.exp(s_ref[n, c : c + 16, cols] - peak)
                total = total + (e[0:8] + e[8:16])
                p_ref[n, c : c + 16, cols] = e.astype(BF)
            total = jnp.sum(total, axis=0, keepdims=True)
            tot_ref[n, 0:1, cols] = 1.0 / total
            tot_ref[n, 1:2, cols] = peak + jnp.log(total)
        lse_ref[0, h : h + 1, :] = tot_ref[n, 1:2, :]

    def mix(h, n):
        rows = head_rows(h)
        att_ref[0, rows, :] = (dot_nn(qkv_ref[0, 2, rows, :], p_ref[n]) * tot_ref[n, 0:1, :]).astype(BF)

    G = HB
    def many(fn, b):
        for k in range(G):
            fn(b * G + k, (b % 2) * G + k)

    batches = HEADS // G
    for b in range(batches + 2):
        if b < batches:
            many(scores, b)
        if 0 <= b - 1 < batches:
            many(soften, b - 1)
        if 0 <= b - 2 < batches:
            many(mix, b - 2)


def attend(x, seg, w, bias):
    width = x.shape[1]
    groups, group = w.shape[1:3]
    rows, seq = seg.shape
    return pl.pallas_call(
        attend_kernel,
        grid=(rows,),
        in_specs=[
            pl.BlockSpec((seq, width), lambda r: (r, 0)),
            pl.BlockSpec((1, 1, seq), lambda r: (r, 0, 0)),
            pl.BlockSpec(w.shape, lambda r: (0, 0, 0, 0)),
            pl.BlockSpec(bias.shape, lambda r: (0, 0)),
        ],
        out_specs=[
            pl.BlockSpec((1, width, seq), lambda r: (r, 0, 0)),
            pl.BlockSpec((1, 3, width, seq), lambda r: (r, 0, 0, 0)),
            pl.BlockSpec((1, width, seq), lambda r: (r, 0, 0)),
            pl.BlockSpec((1, 16, seq), lambda r: (r, 0, 0)),
        ],
        out_shape=[
            jax.ShapeDtypeStruct((rows, width, seq), BF),
            jax.ShapeDtypeStruct((rows, 3, width, seq), BF),
            jax.ShapeDtypeStruct((rows, width, seq), BF),
            jax.ShapeDtypeStruct((rows, 16, seq), F32),
        ],
        scratch_shapes=[pltpu.VMEM((2 * HB, 80, seq), BF) for _ in range(2)]
        + [pltpu.VMEM((2 * HB, seq, seq), F32), pltpu.VMEM((2 * HB, seq, seq), BF), pltpu.VMEM((2 * HB, 8, seq), F32)]
        + [pltpu.VMEM((groups, 3 * group, group), BF), pltpu.VMEM((2, width, 128), F32)],
        compiler_params=params("arbitrary"),
        cost_estimate=pl.CostEstimate(flops=int(10e9), transcendentals=0, bytes_accessed=20 * 2**20),
        name="attend",
    )(x, seg.reshape(rows, 1, seq), w, bias)

CH = 64
EC = 64
DU = 768
DO = 384
ROOT_HALF = 0.7071067811865476
LOG2E = 1.4426950408889634


def feed_kernel(
    core_ref, xt_ref, att_ref, cot_ref, wo_ref, own_ref, other_ref, vec_in_ref,
    out_ref, gr1_ref, gatt_ref, delta_ref, keep_ref, send_ref, okeep_ref, osend_ref,
    a_ref, u1_ref, v2_ref, nlow_ref, act_ref, gp_ref, gd_ref, gup_ref, ct_ref, acc_ref,
    wot_ref, wut_ref, wdt_ref, vec_ref, dwo_ref, dff_ref,
):
    width, seq = a_ref.shape
    walls = (own_ref, other_ref)
    halves, groups = 2, own_ref.shape[0]
    group = width // groups
    part = own_ref.shape[2]
    full = halves * part
    first = pl.program_id(0) == 0
    last = pl.program_id(0) == pl.num_programs(0) - 1
    inv_width = 1.0 / width
    aug = group + 16

    @pl.when(first)
    def _():
        acc_ref[...] = jnp.zeros_like(acc_ref)
        dwo_ref[...] = jnp.zeros_like(dwo_ref)
        dff_ref[...] = jnp.zeros_like(dff_ref)
        row = lax.broadcasted_iota(jnp.int32, (16, seq), 0)
        for g in range(groups):
            nlow_ref[g, group:aug, :] = jnp.where(row == 0, 1.0, 0.0).astype(BF)
        columns = vec_in_ref[...].T
        for n in range(6):
            vec_ref[n] = jnp.broadcast_to(columns[:, n : n + 1], (width, 128))
        wot_ref[...] = wo_ref[...].T

        def prepare(g, carry):
            for h in range(halves):
                rows = slice(h * part, (h + 1) * part)
                wut_ref[g, rows, :] = walls[h][g, 0:aug, :].T
                wdt_ref[g, rows, :] = (walls[h][g, aug : aug + group, :] * jnp.asarray(0.5, BF)).T
            return carry

        lax.fori_loop(0, groups, prepare, 0)

    ct_ref[...] = cot_ref[...].T

    part_sum = jnp.zeros((8, seq), F32)
    for b in range(0, width, DO):
        mixed = dot_nn(wot_ref[b : b + DO, :], att_ref[0])
        for c in range(0, DO, EC):
            s = slice(b + c, b + c + EC)
            v = mixed[c : c + EC] + wide(vec_ref[0, s, :], seq) + xt_ref[0, s, :].astype(F32)
            a_ref[s, :] = v
            part_sum = part_sum + sub_sum(v)
    mean = jnp.sum(part_sum, axis=0, keepdims=True) * inv_width
    part_sum = jnp.zeros((8, seq), F32)
    for c in range(0, width, CH):
        v = a_ref[c : c + CH, :] - mean
        part_sum = part_sum + sub_sum(v * v)
    r1 = lax.rsqrt(jnp.sum(part_sum, axis=0, keepdims=True) * inv_width + EPS)
    for g in range(groups):
        for c in range(0, group, 64):
            s = slice(g * group + c, g * group + c + 64)
            u = (a_ref[s, :] - mean) * r1
            u1_ref[s, :] = u
            n = u * wide(vec_ref[1, s, :], seq) + wide(vec_ref[2, s, :], seq)
            v2_ref[s, :] = n
            nlow_ref[g, c : c + 64, :] = n.astype(BF)

    part_sum = jnp.zeros((8, seq), F32)
    for g in range(groups):
        for b in range(0, full, DU):
            upward = dot_nn(wut_ref[g, b : b + DU, :], nlow_ref[g])
            for c in range(0, DU, EC):
                s = slice(b + c, b + c + EC)
                u = upward[c : c + EC]
                one = 1.0 + lax.erf(u * ROOT_HALF)
                act_ref[g, s, :] = (u * one).astype(BF)
                bell = jnp.exp2((u * u) * (-0.5 * LOG2E))
                gp_ref[g, s, :] = one + (u * (1.1283791670955126 * ROOT_HALF)) * bell
        s = slice(g * group, (g + 1) * group)
        down = dot_nn(walls[0][g, aug : aug + group, :], act_ref[g, 0:part, :])
        for h in range(1, halves):
            down = down + dot_nn(walls[h][g, aug : aug + group, :], act_ref[g, h * part : (h + 1) * part, :])
        v = v2_ref[s, :] + (down * 0.5 + wide(vec_ref[3, s, :], seq))
        v2_ref[s, :] = v
        part_sum = part_sum + sub_sum(v)

    mean = jnp.sum(part_sum, axis=0, keepdims=True) * inv_width
    part_sum = jnp.zeros((8, seq), F32)
    for c in range(0, width, CH):
        v = v2_ref[c : c + CH, :] - mean
        part_sum = part_sum + sub_sum(v * v)
    r2 = lax.rsqrt(jnp.sum(part_sum, axis=0, keepdims=True) * inv_width + EPS)
    sum_e = jnp.zeros((8, seq), F32)
    sum_eu = jnp.zeros((8, seq), F32)
    for c in range(0, width, CH):
        s = slice(c, c + CH)
        u = (v2_ref[s, :] - mean) * r2
        v2_ref[s, :] = u
        gain = wide(vec_ref[4, s, :], seq)
        out_ref[:, s] = (u * gain + wide(vec_ref[5, s, :], seq)).T
        cot = ct_ref[s, :].astype(F32)
        cu = cot * u
        acc_ref[4, s, :] += fold(cu)
        acc_ref[5, s, :] += fold(cot)
        sum_e = sum_e + sub_sum(cot * gain)
        sum_eu = sum_eu + sub_sum(cu * gain)
    mean_e = jnp.sum(sum_e, axis=0, keepdims=True) * inv_width
    mean_eu = jnp.sum(sum_eu, axis=0, keepdims=True) * inv_width
    for c in range(0, width, CH):
        s = slice(c, c + CH)
        e = ct_ref[s, :].astype(F32) * wide(vec_ref[4, s, :], seq)
        gr = r2 * (e - mean_e - v2_ref[s, :] * mean_eu)
        a_ref[s, :] = gr
        acc_ref[3, s, :] += fold(gr)
        gd_ref[s, :] = gr.astype(BF)

    for g in range(groups):
        rows = slice(g * group, (g + 1) * group)
        for b in range(0, full, DU):
            gact = dot_nn(wdt_ref[g, b : b + DU, :], gd_ref[rows, :])
            for c in range(0, DU, EC):
                s = slice(b + c, b + c + EC)
                gup_ref[g % 2, s, :] = (gact[c : c + EC] * gp_ref[g, s, :]).astype(BF)
        for h in range(halves):
            s = slice(h * part, (h + 1) * part)
            dff_ref[h, g, aug : aug + group, :] += dot_nt(gd_ref[rows, :], act_ref[g, s, :])
            dff_ref[h, g, 0:aug, :] += dot_nt(nlow_ref[g], gup_ref[g % 2, s, :])
        back = dot_nn(walls[0][g, 0:group, :], gup_ref[g % 2, 0:part, :])
        for h in range(1, halves):
            back = back + dot_nn(walls[h][g, 0:group, :], gup_ref[g % 2, h * part : (h + 1) * part, :])
        a_ref[rows, :] += back

    sum_e = jnp.zeros((8, seq), F32)
    sum_eu = jnp.zeros((8, seq), F32)
    for c in range(0, width, CH):
        s = slice(c, c + CH)
        gn = a_ref[s, :]
        gu = gn * u1_ref[s, :]
        acc_ref[1, s, :] += fold(gu)
        acc_ref[2, s, :] += fold(gn)
        gain = wide(vec_ref[1, s, :], seq)
        sum_e = sum_e + sub_sum(gn * gain)
        sum_eu = sum_eu + sub_sum(gu * gain)
    mean_e = jnp.sum(sum_e, axis=0, keepdims=True) * inv_width
    mean_eu = jnp.sum(sum_eu, axis=0, keepdims=True) * inv_width
    for c in range(0, width, CH):
        s = slice(c, c + CH)
        e = a_ref[s, :] * wide(vec_ref[1, s, :], seq)
        gr = r1 * (e - mean_e - u1_ref[s, :] * mean_eu)
        gr1_ref[0, s, :] = gr
        acc_ref[0, s, :] += fold(gr)
        gd_ref[s, :] = gr.astype(BF)
    for b in range(0, width, DO):
        grad = dot_nn(wo_ref[b : b + DO, :], gd_ref[...])
        for c in range(0, DO, HEAD_DIM):
            s = slice(b + c, b + c + HEAD_DIM)
            ga = grad[c : c + HEAD_DIM].astype(BF)
            gatt_ref[0, s, :] = ga
            prod = ga.astype(F32) * att_ref[0, s, :].astype(F32)
            head = (b + c) // HEAD_DIM
            delta_ref[0, head : head + 1, :] = jnp.sum(prod, axis=0, keepdims=True)
    half = width // 2
    for k in range(2):
        dwo_ref[k] += dot_nt(att_ref[0, k * half : (k + 1) * half, :], gd_ref[...])

    @pl.when(last)
    def _():
        for n in range(6):
            line = jnp.sum(acc_ref[n].T, axis=0, keepdims=True)
            for k in range(width // part):
                for h in range(halves):
                    at = aug + group + n * (width // part) + k
                    dff_ref[h, 0, at : at + 1, :] = line[:, k * part : (k + 1) * part]
        core = core_ref[0]
        okeep_ref[...] = dwo_ref[core]
        osend_ref[...] = dwo_ref[1 - core].astype(BF)
        two = groups // 2

        def hand(i, carry):
            h, k = i // two, i % two
            for ref, g in ((keep_ref, core * two + k), (send_ref, (1 - core) * two + k)):
                ref[h, k, 0:aug, :] = dff_ref[h, g, 0:aug, :].astype(ref.dtype)
                ref[h, k, aug : aug + group, :] = (dff_ref[h, g, aug : aug + group, :] * 0.5).astype(ref.dtype)
                ref[h, k, aug + group :, :] = dff_ref[h, g, aug + group :, :].astype(ref.dtype)
            return carry

        lax.fori_loop(0, halves * two, hand, 0)


def feed(core, xt, att, cot, wo, own, other, vec):
    rows, width, seq = xt.shape
    halves, (groups, _, part) = 2, own.shape
    group = width // groups
    aug = group + 16
    full = halves * part

    def whole(a):
        return pl.BlockSpec(a.shape, lambda r: (0,) * len(a.shape), pipeline_mode=pl.Buffered(1))

    per_row = pl.BlockSpec((1, width, seq), lambda r: (r, 0, 0))
    token = pl.BlockSpec((seq, width), lambda r: (r, 0))
    sums = (halves, groups // 2, 2 * group + 32, part)
    outs = [
        jax.ShapeDtypeStruct((rows * seq, width), F32),
        jax.ShapeDtypeStruct((rows, width, seq), F32),
        jax.ShapeDtypeStruct((rows, width, seq), BF),
        jax.ShapeDtypeStruct((rows, 16, seq), F32),
        jax.ShapeDtypeStruct(sums, F32),
        jax.ShapeDtypeStruct(sums, BF),
        jax.ShapeDtypeStruct((width // 2, width), F32),
        jax.ShapeDtypeStruct((width // 2, width), BF),
    ]
    return pl.pallas_call(
        feed_kernel,
        grid=(rows,),
        in_specs=[pl.BlockSpec(memory_space=pltpu.SMEM), per_row, per_row, token] + [whole(a) for a in (wo, own, other, vec)],
        out_specs=[token, per_row, per_row, pl.BlockSpec((1, 16, seq), lambda r: (r, 0, 0))]
        + [whole(a) for a in outs[4:]],
        out_shape=outs,
        scratch_shapes=[
            pltpu.VMEM((width, seq), F32),
            pltpu.VMEM((width, seq), F32),
            pltpu.VMEM((width, seq), F32),
            pltpu.VMEM((groups, aug, seq), BF),
            pltpu.VMEM((groups, full, seq), BF),
            pltpu.VMEM((groups, full, seq), F32),
            pltpu.VMEM((width, seq), BF),
            pltpu.VMEM((2, full, seq), BF),
            pltpu.VMEM((width, seq), BF),
            pltpu.VMEM((6, width, 128), F32),
            pltpu.VMEM((width, width), BF),
            pltpu.VMEM((groups, full, aug), BF),
            pltpu.VMEM((groups, full, group), BF),
            pltpu.VMEM((6, width, 128), F32),
            pltpu.VMEM((2, width // 2, width), F32),
            pltpu.VMEM((halves, groups, 2 * group + 32, part), F32),
        ],
        compiler_params=pltpu.CompilerParams(vmem_limit_bytes=63 * 2**20),
        cost_estimate=pl.CostEstimate(flops=int(25e9), transcendentals=0, bytes_accessed=35 * 2**20),
        name="feed",
    )(core, xt, att, cot, wo, own, other, vec)


def split3(v):
    hi = v.astype(BF).astype(F32)
    mid = (v - hi).astype(BF).astype(F32)
    return hi, mid, v - hi - mid


def back_kernel(
    core_ref, qkv_ref, gatt_ref, xt_ref, lse_ref, delta_ref, seg_ref, *rest, head0, fresh, final, passed
):
    rest = list(rest)
    if passed:
        del rest[-12 - passed : -12]
    if not fresh:
        dwin_ref, bsin_ref = rest[:2]
    d_ref = rest[-12]
    oa_ref, ob_ref = rest[-11:-9]
    qa_ref, ka_ref, va_ref, ga_ref, p_ref, dst_ref, ds_ref, dw_ref, bsum_ref = rest[-9:]
    chans, seq = xt_ref.shape[1:]
    groups, group = dw_ref.shape[1:3]
    first = pl.program_id(0) == 0
    last = pl.program_id(0) == pl.num_programs(0) - 1

    @pl.when(first)
    def _():
        if fresh:
            dw_ref[...] = jnp.zeros_like(dw_ref)
            bsum_ref[...] = jnp.zeros_like(bsum_ref)
        else:
            dw_ref[...] = dwin_ref[...]
            bsum_ref[...] = bsin_ref[...]

    seg = seg_ref[0]
    rank = lax.broadcasted_iota(jnp.int32, (16, seq), 0)
    same = rank == seg
    hot = jnp.where(same, 1.0, 0.0)
    for n in range(BUF):
        ka_ref[n, 64:80, :] = jnp.where(rank < 4, jnp.where(same, 0.0, NEG), jnp.where(rank < 7, -1.0, 0.0)).astype(BF)
        va_ref[n, 64:80, :] = jnp.where(rank < 3, -1.0, 0.0).astype(BF)

    def weigh(h):
        n = h % BUF
        rows = slice(h * HEAD_DIM, (h + 1) * HEAD_DIM)
        hi, mid, lo = split3(lse_ref[0, head0 + h : head0 + h + 1, :])
        tail = jnp.where(rank == 4, hi, jnp.where(rank == 5, mid, jnp.where(rank == 6, lo, 0.0)))
        qa_ref[n, 64:80, :] = jnp.where(rank < 4, hot, tail).astype(BF)
        hi, mid, lo = split3(delta_ref[0, head0 + h : head0 + h + 1, :])
        ga_ref[n, 64:80, :] = jnp.where(rank == 0, hi, jnp.where(rank == 1, mid, jnp.where(rank == 2, lo, 0.0))).astype(BF)
        qa_ref[n, 0:64, :] = qkv_ref[0, 0, rows, :] * jnp.asarray(0.125, BF)
        ka_ref[n, 0:64, :] = qkv_ref[0, 1, rows, :]
        va_ref[n, 0:64, :] = qkv_ref[0, 2, rows, :]
        ga_ref[n, 0:64, :] = gatt_ref[0, rows, :]
        kn = ka_ref[n].T
        vn = va_ref[n].T
        for t in range(seq // 256):
            cols = slice(t * 256, t * 256 + 256)
            p = jnp.exp(dot_nn(kn, qa_ref[n, :, cols]))
            low = p.astype(BF)
            p_ref[n, cols, :] = low.T
            ds = (p * dot_nn(vn, ga_ref[n, :, cols])).astype(BF)
            ds_ref[n, t] = ds
            dst_ref[n, cols, :] = ds.T

    def gather_head(h):
        n = h % BUF
        rows = slice(h * HEAD_DIM, (h + 1) * HEAD_DIM)
        kt = qkv_ref[0, 1, rows, :]
        dv = dot_nn(gatt_ref[0, rows, :], p_ref[n])
        dk = dot_nn(qa_ref[n, 0:64, :], dst_ref[n])
        dq = []
        for t in range(seq // 256):
            cols = slice(t * 256, t * 256 + 256)
            dq.append(dot_nn(kt, ds_ref[n, t]) * 0.125)
        dq = jnp.concatenate(dq, axis=1)
        bsum_ref[0, rows, :] += fold(dq)
        bsum_ref[1, rows, :] += fold(dv)
        d_ref[0, 0, rows, :] = dq.astype(BF)
        d_ref[0, 1, rows, :] = dk.astype(BF)
        d_ref[0, 2, rows, :] = dv.astype(BF)

    heads = chans // HEAD_DIM
    for h in range(heads + 1):
        if h < heads:
            weigh(h)
        if h > 0:
            gather_head(h - 1)
    for g in range(groups):
        s = slice(g * group, (g + 1) * group)
        for j in range(3):
            dw_ref[j, g] += dot_nt(xt_ref[0, s, :], d_ref[0, j, s, :])

    if not final:
        @pl.when(last)
        def _():
            oa_ref[...] = dw_ref[...]
            ob_ref[...] = bsum_ref[...]

    else:
        @pl.when(last)
        def _():
            half = PACK // 2
            core = core_ref[0]

            def put(row, value):
                rows = value.shape[0]
                where = row // half
                at = slice(row % half, row % half + rows)

                @pl.when(core == where)
                def _():
                    oa_ref[at, :] = value

                @pl.when(core != where)
                def _():
                    ob_ref[at, :] = value.astype(BF)

            tiles = chans // 128
            bias = jnp.concatenate([jnp.sum(bsum_ref[n].T, axis=0, keepdims=True) for n in range(2)], axis=0)
            bias = jnp.concatenate([bias, jnp.zeros((6, chans), F32)], axis=0)
            for j in range(3):
                both = jnp.concatenate([dw_ref[j, g] for g in range(groups)], axis=1)
                for c in range(tiles):
                    for a in range(0, group, 64):
                        put(c * 3 * group + j * group + a, both[a : a + 64, c * 128 : c * 128 + 128])
            for c in range(tiles):
                put(tiles * 3 * group + 8 * c, bias[:, c * 128 : c * 128 + 128])
            for row in range(tiles * 3 * group + 8 * tiles, PACK, 8):
                put(row, jnp.zeros((8, 128), F32))


PACK = 1792
BUF = 2


def back(core, qkv, gatt, xt, lse, delta, seg, w, index, parts, row0, count, carried, into, final, sends, keeps):
    rows, _, width, seq = qkv.shape
    chans = width // parts
    groups, group = w.shape[1] // parts, w.shape[2]
    per_row = pl.BlockSpec((1, chans, seq), lambda r: (r + row0, index, 0))
    full = pl.BlockSpec((1, 16, seq), lambda r: (r + row0, 0, 0))
    in_specs = [
        pl.BlockSpec(memory_space=pltpu.SMEM),
        pl.BlockSpec((1, 3, chans, seq), lambda r: (r + row0, 0, index, 0)),
        per_row,
        per_row,
        full,
        full,
        pl.BlockSpec((1, 1, seq), lambda r: (r + row0, 0, 0)),
    ]
    args = [core, qkv, gatt, xt, lse, delta, seg.reshape(rows, 1, seq)]
    sums = [jax.ShapeDtypeStruct((3, groups, group, group), F32), jax.ShapeDtypeStruct((2, chans, 128), F32)]
    if carried is not None:
        in_specs += [pl.BlockSpec((3, groups, group, group), lambda r: (0, 0, 0, 0)), pl.BlockSpec((2, chans, 128), lambda r: (0, 0, 0))]
        args += list(carried)
    alias = {}
    if into is not None:
        in_specs.append(pl.BlockSpec(memory_space=pl.ANY))
        args.append(into)
        alias = {len(args) - 1: len(keeps)}
    for n, value in enumerate(keeps):
        alias[len(args)] = n
        in_specs.append(pl.BlockSpec(memory_space=pl.ANY))
        args.append(value)
    for value in sends:
        in_specs.append(pl.BlockSpec(memory_space=pl.ANY))
        args.append(value)
    if final:
        outs = [jax.ShapeDtypeStruct((PACK // 2, 128), F32), jax.ShapeDtypeStruct((PACK // 2, 128), BF)]
    else:
        outs = sums
    return pl.pallas_call(
        partial(back_kernel, head0=index * (chans // HEAD_DIM), fresh=carried is None, final=final, passed=len(keeps)),
        grid=(count,),
        in_specs=in_specs,
        out_specs=[pl.BlockSpec(memory_space=pl.ANY) for _ in keeps]
        + [pl.BlockSpec((1, 3, chans, seq), lambda r: (r + row0, 0, index, 0))]
        + [pl.BlockSpec(o.shape, lambda r, n=len(o.shape): (0,) * n) for o in outs],
        out_shape=[jax.ShapeDtypeStruct(value.shape, value.dtype) for value in keeps]
        + [jax.ShapeDtypeStruct((rows, 3, width, seq), BF)]
        + outs,
        scratch_shapes=[pltpu.VMEM((BUF, 80, seq), BF) for _ in range(4)]
        + [pltpu.VMEM((BUF, seq, seq), BF) for _ in range(2)]
        + [pltpu.VMEM((BUF, seq // 256, seq, 256), BF)]
        + [pltpu.VMEM(o.shape, F32) for o in sums],
        input_output_aliases=alias,
        compiler_params=params("arbitrary"),
        cost_estimate=pl.CostEstimate(flops=int(8e9 * count), transcendentals=0, bytes_accessed=20 * 2**20),
        name="back",
    )(*args)


def input_kernel(d_ref, gr1_ref, w_ref, *rest):
    gin_ref = rest[-1]
    groups, group = w_ref.shape[1:3]
    parts = []
    for g in range(groups):
        s = slice(g * group, (g + 1) * group)
        total = gr1_ref[0, s, :]
        for j in range(3):
            total = total + dot_nn(w_ref[j, g], d_ref[0, j, s, :])
        parts.append(total)
    gin_ref[...] = jnp.concatenate(parts, axis=0).T


def input_grad(d, gr1, w, row0, count, into, sends, keeps):
    rows, _, width, seq = d.shape
    in_specs = [
        pl.BlockSpec((1, 3, width, seq), lambda r: (r + row0, 0, 0, 0)),
        pl.BlockSpec((1, width, seq), lambda r: (r + row0, 0, 0)),
        pl.BlockSpec(w.shape, lambda r: (0, 0, 0, 0)),
    ]
    args = [d, gr1, w]
    alias = {}
    if into is not None:
        alias[len(args)] = len(keeps)
        args.append(into)
    for n, value in enumerate(keeps):
        alias[len(args)] = n
        args.append(value)
    args += sends
    in_specs += [pl.BlockSpec(memory_space=pl.ANY)] * (len(args) - len(in_specs))
    return pl.pallas_call(
        input_kernel,
        grid=(count,),
        in_specs=in_specs,
        out_specs=[pl.BlockSpec(memory_space=pl.ANY) for _ in keeps] + [pl.BlockSpec((seq, width), lambda r: (r + row0, 0))],
        out_shape=[jax.ShapeDtypeStruct(value.shape, value.dtype) for value in keeps]
        + [jax.ShapeDtypeStruct((rows * seq, width), F32)],
        input_output_aliases=alias,
        compiler_params=params("arbitrary"),
        cost_estimate=pl.CostEstimate(flops=int(8e9 * count), transcendentals=0, bytes_accessed=6 * count * 2**20),
        name="input_grad",
    )(*args)


class Axis:
    def __init__(self, name, size, bit):
        self.name, self.pairs = name, [(i, i ^ bit) for i in range(size)]
        self.side = (lax.axis_index(name) // bit) % 2

    def swap(self, value):
        return lax.ppermute(value, self.name, self.pairs)

    def split(self, value):
        half = value.shape[0] // 2
        keep = lax.dynamic_slice_in_dim(value, self.side * half, half, 0)
        send = lax.dynamic_slice_in_dim(value, (1 - self.side) * half, half, 0)
        return keep, send.astype(BF)

    def join(self, value):
        other = self.swap(value)
        return jnp.where(self.side == 0, jnp.concatenate([value, other]), jnp.concatenate([other, value]))


def add(keep, got):
    return keep + got.astype(F32)


def sum_down(value, axes):
    for axis in axes:
        keep, send = axis.split(value)
        value = add(keep, axis.swap(send))
    return value


def sum_across(value, axes):
    low = value.astype(BF)
    for axis in axes:
        low = (low.astype(F32) + axis.swap(low).astype(F32)).astype(BF)
    return low


def gather_up(low, axes):
    for axis in reversed(axes):
        low = axis.join(low)
    return low


def finish_kernel(
    core_ref, fo_ref, fo_got_ref, p_ref, p_got_ref,
    dqkv_ref, qvb_ref, dwo_ref, dup_ref, upb_ref, ddown_ref, small_ref, fo_all, p_all,
):
    core = core_ref[0]
    fo_all[core] = fo_ref[...]
    fo_all[1 - core] = fo_got_ref[...]
    p_all[core] = p_ref[...]
    p_all[1 - core] = p_got_ref[...]
    groups, group, part = dup_ref.shape
    aug = group + 16
    block = 2 * group + 32
    width = dwo_ref.shape[1]
    pairs = p_ref.shape[0]
    for c in range(2):
        for k in range(groups // 2):
            g, row = c * (groups // 2) + k, k * block
            dup_ref[g] = fo_all[c, row : row + group, :].astype(F32)
            upb_ref[g : g + 1, :] = fo_all[c, row + group : row + aug, :].astype(F32)[0:1]
            ddown_ref[g] = fo_all[c, row + aug : row + aug + group, :].astype(F32)
        rows = width // 8
        for y in range(2):
            for x in range(2):
                for k in range(2):
                    at = 2 * block + ((y * 2 + x) * 2 + k) * rows
                    to = c * (width // 2) + x * (width // 4) + y * rows
                    dwo_ref[to : to + rows, k * part : (k + 1) * part] = fo_all[c, at : at + rows, :].astype(F32)
    lines = fo_all[0, aug + group : block, :].astype(F32)
    for n in range(6):
        for k in range(width // part):
            at = n * (width // part) + k
            small_ref[n : n + 1, k * part : (k + 1) * part] = lines[at : at + 1]
    chans = width // pairs
    tiles = chans // 128
    per = groups // pairs
    half = PACK // 2
    for p in range(pairs):
        def take(row, count):
            got = []
            while count:
                c, at = row // half, row % half
                n = min(count, half - at)
                got.append(p_all[c, p, at : at + n, :].astype(F32))
                row, count = row + n, count - n
            return got[0] if len(got) == 1 else jnp.concatenate(got, axis=0)

        for j in range(3):
            both = jnp.concatenate([take((c * 3 + j) * per * group // per, group) for c in range(tiles)], axis=1)
            for g in range(per):
                dqkv_ref[j, p * per + g] = both[:, g * group : (g + 1) * group]
        bias = jnp.concatenate([take(tiles * 3 * group + 8 * c, 8) for c in range(tiles)], axis=1)
        qvb_ref[:, p * chans : (p + 1) * chans] = bias[0:2]


def finish(core, fo, fo_got, p, p_got, groups, group, part):
    width = groups * group
    shapes = [(3, groups, group, group), (2, width), (width, width), (groups, group, part), (groups, part), (groups, group, part), (8, width)]
    args = [fo, fo_got, p, p_got]

    def whole(shape):
        return pl.BlockSpec(shape, lambda i, n=len(shape): (0,) * n)

    return pl.pallas_call(
        finish_kernel,
        grid=(1,),
        in_specs=[pl.BlockSpec(memory_space=pltpu.SMEM)] + [whole(a.shape) for a in args],
        out_specs=[whole(shape) for shape in shapes],
        out_shape=[jax.ShapeDtypeStruct(shape, F32) for shape in shapes],
        scratch_shapes=[pltpu.VMEM((2,) + fo.shape, BF), pltpu.VMEM((2,) + p.shape, BF)],
        compiler_params=params("arbitrary"),
        name="finish",
    )(core, *args)


def per_device(
    inputs, segments, cotangent, qkv_weight, qv_bias, out_weight, out_bias, ln1_gain, ln1_bias,
    up_weight, up_bias, down_weight, down_bias, ln2_gain, ln2_bias, *, dp, ffn,
):
    groups, group = qkv_weight.shape[1:3]
    part = up_weight.shape[2]
    assert ffn == 2
    bits = [Axis("dp", dp, 1 << k) for k in range(dp.bit_length() - 1)]
    core, ax, rest = bits[0], bits[1], bits[2:]
    ay = Axis("ffn", ffn, 1)
    core_id = core.side.astype(jnp.int32).reshape(1)
    rows = segments.shape[0]

    wall = jnp.concatenate(
        [up_weight, up_bias[:, None, :], jnp.zeros((groups, 15, part), BF), down_weight], axis=1
    )
    fetched = ay.swap(lax.dynamic_slice_in_dim(wall, core.side * (groups // 2), groups // 2, 0))
    xt, qkv, att, lse = attend(inputs, segments, qkv_weight, qv_bias)
    other = core.join(jnp.where(lse[0, 0, 0] < jnp.inf, fetched, jnp.zeros_like(fetched)))
    zero = jnp.zeros_like(out_bias)
    vec = jnp.stack([out_bias, ln1_gain, ln1_bias, down_bias, ln2_gain, ln2_bias, zero, zero])
    layer_out, gr1, gatt, delta, *first = feed(core_id, xt, att, cotangent, out_weight, wall, other, vec)

    parts = 2
    state = {"grads": None, "carried": None, "input": None}
    packs = []

    def under(call, *stages):
        keeps, sends = [keep for _, keep, _ in stages], [send for _, _, send in stages]
        got = [axis.swap(send) for axis, _, send in stages]
        if call is not None:
            keeps = call([], keeps)
        return [add(keep, arrived) for keep, arrived in zip(keeps, got)]

    def part_of_back(index, row0, count):
        def call(sends, keeps):
            final = row0 + count >= rows
            outs = back(
                core_id, qkv, gatt, xt, lse, delta, segments, qkv_weight, index, parts, row0, count,
                state["carried"], state["grads"], final, sends, keeps,
            )
            state["grads"], *carried = outs[len(keeps) :]
            state["carried"] = None if final else carried
            if final:
                packs.append(carried)
            return outs[: len(keeps)]

        return call

    def part_of_input(row0, count):
        def call(sends, keeps):
            *kept, state["input"] = input_grad(state["grads"], gr1, qkv_weight, row0, count, state["input"], sends, keeps)
            return kept

        return call

    def cut(index, at):
        return [part_of_back(index, row0, end - row0) for row0, end in zip([0] + at, at + [rows]) if end > row0]

    calls = cut(0, [rows // 4]) + cut(1, [rows // 2])
    calls += [None] * (4 - len(calls))
    ffn1, out1 = under(calls[0], (core, *first[:2]), (core, *first[2:]))
    ffn2, out2 = under(calls[1], (ay, ffn1[0], ffn1[1].astype(BF)), (ax, *ax.split(out1)))
    ffn3, out3, sum0 = under(calls[2], (ax, *ax.split(ffn2)), (ay, *ay.split(out2)), (core, *packs[0]))
    low = jnp.concatenate([ffn3[0], out3[:, :part], out3[:, part:]]).astype(BF)
    both, sum0 = under(calls[3], (rest[0], low.astype(F32), low), (ay, *ay.split(sum0)))
    both, sum0, sum1 = under(
        part_of_input(0, rows - rows // 2), (rest[1], both, both.astype(BF)), (ax, *ax.split(sum0)), (core, *packs[1])
    )
    low = sum0.astype(BF)
    last = part_of_input(rows - rows // 2, rows // 2) if rows > 1 else None
    sum0, sum1 = under(last, (rest[0], low.astype(F32), low), (ay, *ay.split(sum1)))
    sum0 = sum_across(sum0, rest[1:])
    sum1 = sum_across(sum_down(sum1, [ax]), rest)
    both = sum_across(both, rest[2:])
    block = 2 * group + 32
    ffns = ax.join(both[None, :block])
    outs = ax.join(ay.join(both[None, block:])[None]).swapaxes(0, 1)
    fo = jnp.concatenate([ffns.reshape(-1, part), outs.reshape(-1, part)])
    fo_got = core.swap(fo)
    low = jnp.stack([sum0, sum1])
    low = ax.join(low[None]).swapaxes(0, 1).reshape(parts, -1, 128)
    low = ay.join(low[None]).swapaxes(0, 1).reshape(parts, -1, 128)
    p_got = core.swap(low)
    grad_inputs = state["input"]
    dqkv, qvb, dwo, dup, upb, ddown, small = finish(core_id, fo, fo_got, low, p_got, groups, group, part)
    return (
        layer_out, grad_inputs, dqkv, qvb, dwo, small[0], small[1], small[2],
        dup, upb, ddown, small[3], small[4], small[5],
    )


def solution(mesh):
    rows = P(("dp", "ffn"), None)
    shared = P()
    split = P(None, None, "ffn")
    return jax.shard_map(
        partial(per_device, dp=mesh.shape["dp"], ffn=mesh.shape["ffn"]),
        mesh=mesh,
        in_specs=(rows, rows, rows) + (shared,) * 6 + (split, P(None, "ffn"), split) + (shared,) * 3,
        out_specs=(rows, rows) + (shared,) * 6 + (split, P(None, "ffn"), split) + (shared,) * 3,
        check_vma=False,
    )
```

```python
from functools import partial

import jax
import jax.numpy as jnp
from jax import lax
from jax.experimental import pallas as pl
from jax.experimental.pallas import tpu as pltpu
from jax.sharding import PartitionSpec as P

HEADS = 12
HEAD_DIM = 64
EPS = 1e-05
NEG = -1e30
BF = jnp.bfloat16
F32 = jnp.float32


def dot_nn(a, b):
    return jnp.dot(a, b, preferred_element_type=F32)


def dot_nt(a, b):
    return lax.dot_general(a, b, (((1,), (1,)), ((), ())), preferred_element_type=F32)


def params(*sem, mib=32):
    return pltpu.CompilerParams(vmem_limit_bytes=mib * 2**20, dimension_semantics=sem)


def wide(column, lanes):
    return jnp.concatenate([column] * (lanes // 128), axis=1)


def fold(values):
    total = values[:, 0:128]
    for start in range(128, values.shape[1], 128):
        total = total + values[:, start : start + 128]
    return total


def sub_sum(values):
    total = values[0:8]
    for start in range(8, values.shape[0], 8):
        total = total + values[start : start + 8]
    return total


HB = 1
LT = 256


def attend_kernel(
    x_ref, seg_ref, w_ref, bias_in_ref, xt_ref, qkv_ref, att_ref, lse_ref,
    qa_ref, ka_ref, s_ref, p_ref, tot_ref, wt_ref, bias_ref,
):
    seq, width = x_ref.shape
    groups = wt_ref.shape[0]
    group = width // groups

    @pl.when(pl.program_id(0) == 0)
    def _():
        for g in range(groups):
            for j in range(3):
                wt_ref[g, j * group : (j + 1) * group, :] = w_ref[j, g].T
        columns = jnp.concatenate([bias_in_ref[...], jnp.zeros((6, width), F32)], axis=0).T
        for n in range(2):
            bias_ref[n] = jnp.broadcast_to(columns[:, n : n + 1], (width, 128))

    xt_ref[0] = x_ref[...].T
    seg = seg_ref[0]
    rank = lax.broadcasted_iota(jnp.int32, (16, seq), 0)
    same = rank == seg
    for n in range(2 * HB):
        qa_ref[n, 64:80, :] = jnp.where(same, 1.0, 0.0).astype(BF)
        ka_ref[n, 64:80, :] = jnp.where(same | (rank >= 4), 0.0, NEG).astype(BF)

    for g in range(groups):
        rows = slice(g * group, (g + 1) * group)
        out = dot_nn(wt_ref[g], xt_ref[0, rows, :])
        for j in range(3):
            part = out[j * group : (j + 1) * group]
            if j != 1:
                part = part + wide(bias_ref[j // 2, rows, :], seq)
            qkv_ref[0, j, rows, :] = part.astype(BF)

    def head_rows(h):
        return slice(h * HEAD_DIM, (h + 1) * HEAD_DIM)

    def scores(h, n):
        rows = head_rows(h)
        qa_ref[n, 0:64, :] = qkv_ref[0, 0, rows, :] * jnp.asarray(0.125, BF)
        ka_ref[n, 0:64, :] = qkv_ref[0, 1, rows, :]
        s_ref[n] = dot_nn(ka_ref[n].T, qa_ref[n])

    def soften(h, n):
        for l in range(0, seq, LT):
            cols = slice(l, l + LT)
            peak = s_ref[n, 0:8, cols]
            for c in range(8, seq, 8):
                peak = jnp.maximum(peak, s_ref[n, c : c + 8, cols])
            peak = jnp.max(peak, axis=0, keepdims=True)
            total = jnp.zeros((8, LT), F32)
            for c in range(0, seq, 16):
                e = jnp.exp(s_ref[n, c : c + 16, cols] - peak)
                total = total + (e[0:8] + e[8:16])
                p_ref[n, c : c + 16, cols] = e.astype(BF)
            total = jnp.sum(total, axis=0, keepdims=True)
            tot_ref[n, 0:1, cols] = 1.0 / total
            tot_ref[n, 1:2, cols] = peak + jnp.log(total)
        lse_ref[0, h : h + 1, :] = tot_ref[n, 1:2, :]

    def mix(h, n):
        rows = head_rows(h)
        att_ref[0, rows, :] = (dot_nn(qkv_ref[0, 2, rows, :], p_ref[n]) * tot_ref[n, 0:1, :]).astype(BF)

    G = HB
    def many(fn, b):
        for k in range(G):
            fn(b * G + k, (b % 2) * G + k)

    batches = HEADS // G
    for b in range(batches + 2):
        if b < batches:
            many(scores, b)
        if 0 <= b - 1 < batches:
            many(soften, b - 1)
        if 0 <= b - 2 < batches:
            many(mix, b - 2)


def attend(x, seg, w, bias):
    width = x.shape[1]
    groups, group = w.shape[1:3]
    rows, seq = seg.shape
    return pl.pallas_call(
        attend_kernel,
        grid=(rows,),
        in_specs=[
            pl.BlockSpec((seq, width), lambda r: (r, 0)),
            pl.BlockSpec((1, 1, seq), lambda r: (r, 0, 0)),
            pl.BlockSpec(w.shape, lambda r: (0, 0, 0, 0)),
            pl.BlockSpec(bias.shape, lambda r: (0, 0)),
        ],
        out_specs=[
            pl.BlockSpec((1, width, seq), lambda r: (r, 0, 0)),
            pl.BlockSpec((1, 3, width, seq), lambda r: (r, 0, 0, 0)),
            pl.BlockSpec((1, width, seq), lambda r: (r, 0, 0)),
            pl.BlockSpec((1, 16, seq), lambda r: (r, 0, 0)),
        ],
        out_shape=[
            jax.ShapeDtypeStruct((rows, width, seq), BF),
            jax.ShapeDtypeStruct((rows, 3, width, seq), BF),
            jax.ShapeDtypeStruct((rows, width, seq), BF),
            jax.ShapeDtypeStruct((rows, 16, seq), F32),
        ],
        scratch_shapes=[pltpu.VMEM((2 * HB, 80, seq), BF) for _ in range(2)]
        + [pltpu.VMEM((2 * HB, seq, seq), F32), pltpu.VMEM((2 * HB, seq, seq), BF), pltpu.VMEM((2 * HB, 8, seq), F32)]
        + [pltpu.VMEM((groups, 3 * group, group), BF), pltpu.VMEM((2, width, 128), F32)],
        compiler_params=params("arbitrary", mib=60),
        cost_estimate=pl.CostEstimate(flops=int(10e9), transcendentals=0, bytes_accessed=20 * 2**20),
        name="attend",
    )(x, seg.reshape(rows, 1, seq), w, bias)

CH = 64
EC = 64
DU = 768
DO = 384
ROOT_HALF = 0.7071067811865476
LOG2E = 1.4426950408889634


def feed_kernel(
    core_ref, xt_ref, att_ref, cot_ref, wo_ref, own_ref, other_ref, vec_in_ref,
    out_ref, gr1_ref, gatt_ref, delta_ref, keep_ref, send_ref, okeep_ref, osend_ref,
    a_ref, u1_ref, v2_ref, nlow_ref, act_ref, gp_ref, gd_ref, gup_ref, ct_ref, acc_ref,
    wot_ref, wut_ref, wdt_ref, vec_ref, dwo_ref, dff_ref,
):
    width, seq = a_ref.shape
    walls = (own_ref, other_ref)
    halves, groups = 2, own_ref.shape[0]
    group = width // groups
    part = own_ref.shape[2]
    full = halves * part
    first = pl.program_id(0) == 0
    last = pl.program_id(0) == pl.num_programs(0) - 1
    inv_width = 1.0 / width
    aug = group + 16

    @pl.when(first)
    def _():
        acc_ref[...] = jnp.zeros_like(acc_ref)
        dwo_ref[...] = jnp.zeros_like(dwo_ref)
        dff_ref[...] = jnp.zeros_like(dff_ref)
        row = lax.broadcasted_iota(jnp.int32, (16, seq), 0)
        for g in range(groups):
            nlow_ref[g, group:aug, :] = jnp.where(row == 0, 1.0, 0.0).astype(BF)
        columns = vec_in_ref[...].T
        for n in range(6):
            vec_ref[n] = jnp.broadcast_to(columns[:, n : n + 1], (width, 128))
        wot_ref[...] = wo_ref[...].T

        def prepare(g, carry):
            for h in range(halves):
                rows = slice(h * part, (h + 1) * part)
                wut_ref[g, rows, :] = walls[h][g, 0:aug, :].T
                wdt_ref[g, rows, :] = (walls[h][g, aug : aug + group, :] * jnp.asarray(0.5, BF)).T
            return carry

        lax.fori_loop(0, groups, prepare, 0)

    ct_ref[...] = cot_ref[...].T

    part_sum = jnp.zeros((8, seq), F32)
    for b in range(0, width, DO):
        mixed = dot_nn(wot_ref[b : b + DO, :], att_ref[0])
        for c in range(0, DO, EC):
            s = slice(b + c, b + c + EC)
            v = mixed[c : c + EC] + wide(vec_ref[0, s, :], seq) + xt_ref[0, s, :].astype(F32)
            a_ref[s, :] = v
            part_sum = part_sum + sub_sum(v)
    mean = jnp.sum(part_sum, axis=0, keepdims=True) * inv_width
    part_sum = jnp.zeros((8, seq), F32)
    for c in range(0, width, CH):
        v = a_ref[c : c + CH, :] - mean
        part_sum = part_sum + sub_sum(v * v)
    r1 = lax.rsqrt(jnp.sum(part_sum, axis=0, keepdims=True) * inv_width + EPS)
    for g in range(groups):
        for c in range(0, group, 64):
            s = slice(g * group + c, g * group + c + 64)
            u = (a_ref[s, :] - mean) * r1
            u1_ref[s, :] = u
            n = u * wide(vec_ref[1, s, :], seq) + wide(vec_ref[2, s, :], seq)
            v2_ref[s, :] = n
            nlow_ref[g, c : c + 64, :] = n.astype(BF)

    part_sum = jnp.zeros((8, seq), F32)
    for g in range(groups):
        for b in range(0, full, DU):
            upward = dot_nn(wut_ref[g, b : b + DU, :], nlow_ref[g])
            for c in range(0, DU, EC):
                s = slice(b + c, b + c + EC)
                u = upward[c : c + EC]
                one = 1.0 + lax.erf(u * ROOT_HALF)
                act_ref[g, s, :] = (u * one).astype(BF)
                bell = jnp.exp2((u * u) * (-0.5 * LOG2E))
                gp_ref[g, s, :] = one + (u * (1.1283791670955126 * ROOT_HALF)) * bell
        s = slice(g * group, (g + 1) * group)
        down = dot_nn(walls[0][g, aug : aug + group, :], act_ref[g, 0:part, :])
        for h in range(1, halves):
            down = down + dot_nn(walls[h][g, aug : aug + group, :], act_ref[g, h * part : (h + 1) * part, :])
        v = v2_ref[s, :] + (down * 0.5 + wide(vec_ref[3, s, :], seq))
        v2_ref[s, :] = v
        part_sum = part_sum + sub_sum(v)

    mean = jnp.sum(part_sum, axis=0, keepdims=True) * inv_width
    part_sum = jnp.zeros((8, seq), F32)
    for c in range(0, width, CH):
        v = v2_ref[c : c + CH, :] - mean
        part_sum = part_sum + sub_sum(v * v)
    r2 = lax.rsqrt(jnp.sum(part_sum, axis=0, keepdims=True) * inv_width + EPS)
    sum_e = jnp.zeros((8, seq), F32)
    sum_eu = jnp.zeros((8, seq), F32)
    for c in range(0, width, CH):
        s = slice(c, c + CH)
        u = (v2_ref[s, :] - mean) * r2
        v2_ref[s, :] = u
        gain = wide(vec_ref[4, s, :], seq)
        out_ref[:, s] = (u * gain + wide(vec_ref[5, s, :], seq)).T
        cot = ct_ref[s, :].astype(F32)
        cu = cot * u
        acc_ref[4, s, :] += fold(cu)
        acc_ref[5, s, :] += fold(cot)
        sum_e = sum_e + sub_sum(cot * gain)
        sum_eu = sum_eu + sub_sum(cu * gain)
    mean_e = jnp.sum(sum_e, axis=0, keepdims=True) * inv_width
    mean_eu = jnp.sum(sum_eu, axis=0, keepdims=True) * inv_width
    for c in range(0, width, CH):
        s = slice(c, c + CH)
        e = ct_ref[s, :].astype(F32) * wide(vec_ref[4, s, :], seq)
        gr = r2 * (e - mean_e - v2_ref[s, :] * mean_eu)
        a_ref[s, :] = gr
        acc_ref[3, s, :] += fold(gr)
        gd_ref[s, :] = gr.astype(BF)

    for g in range(groups):
        rows = slice(g * group, (g + 1) * group)
        for b in range(0, full, DU):
            gact = dot_nn(wdt_ref[g, b : b + DU, :], gd_ref[rows, :])
            for c in range(0, DU, EC):
                s = slice(b + c, b + c + EC)
                gup_ref[g % 2, s, :] = (gact[c : c + EC] * gp_ref[g, s, :]).astype(BF)
        for h in range(halves):
            s = slice(h * part, (h + 1) * part)
            dff_ref[h, g, aug : aug + group, :] += dot_nt(gd_ref[rows, :], act_ref[g, s, :])
            dff_ref[h, g, 0:aug, :] += dot_nt(nlow_ref[g], gup_ref[g % 2, s, :])
        back = dot_nn(walls[0][g, 0:group, :], gup_ref[g % 2, 0:part, :])
        for h in range(1, halves):
            back = back + dot_nn(walls[h][g, 0:group, :], gup_ref[g % 2, h * part : (h + 1) * part, :])
        a_ref[rows, :] += back

    sum_e = jnp.zeros((8, seq), F32)
    sum_eu = jnp.zeros((8, seq), F32)
    for c in range(0, width, CH):
        s = slice(c, c + CH)
        gn = a_ref[s, :]
        gu = gn * u1_ref[s, :]
        acc_ref[1, s, :] += fold(gu)
        acc_ref[2, s, :] += fold(gn)
        gain = wide(vec_ref[1, s, :], seq)
        sum_e = sum_e + sub_sum(gn * gain)
        sum_eu = sum_eu + sub_sum(gu * gain)
    mean_e = jnp.sum(sum_e, axis=0, keepdims=True) * inv_width
    mean_eu = jnp.sum(sum_eu, axis=0, keepdims=True) * inv_width
    for c in range(0, width, CH):
        s = slice(c, c + CH)
        e = a_ref[s, :] * wide(vec_ref[1, s, :], seq)
        gr = r1 * (e - mean_e - u1_ref[s, :] * mean_eu)
        gr1_ref[0, s, :] = gr
        acc_ref[0, s, :] += fold(gr)
        gd_ref[s, :] = gr.astype(BF)
    for b in range(0, width, DO):
        grad = dot_nn(wo_ref[b : b + DO, :], gd_ref[...])
        for c in range(0, DO, HEAD_DIM):
            s = slice(b + c, b + c + HEAD_DIM)
            ga = grad[c : c + HEAD_DIM].astype(BF)
            gatt_ref[0, s, :] = ga
            prod = ga.astype(F32) * att_ref[0, s, :].astype(F32)
            head = (b + c) // HEAD_DIM
            delta_ref[0, head : head + 1, :] = jnp.sum(prod, axis=0, keepdims=True)
    half = width // 2
    for k in range(2):
        dwo_ref[k] += dot_nt(att_ref[0, k * half : (k + 1) * half, :], gd_ref[...])

    @pl.when(last)
    def _():
        for n in range(6):
            line = jnp.sum(acc_ref[n].T, axis=0, keepdims=True)
            for k in range(width // part):
                for h in range(halves):
                    at = aug + group + n * (width // part) + k
                    dff_ref[h, 0, at : at + 1, :] = line[:, k * part : (k + 1) * part]
        core = core_ref[0]
        okeep_ref[...] = dwo_ref[core]
        osend_ref[...] = dwo_ref[1 - core].astype(BF)
        two = groups // 2

        def hand(i, carry):
            h, k = i // two, i % two
            for ref, g in ((keep_ref, core * two + k), (send_ref, (1 - core) * two + k)):
                ref[h, k, 0:aug, :] = dff_ref[h, g, 0:aug, :].astype(ref.dtype)
                ref[h, k, aug : aug + group, :] = (dff_ref[h, g, aug : aug + group, :] * 0.5).astype(ref.dtype)
                ref[h, k, aug + group :, :] = dff_ref[h, g, aug + group :, :].astype(ref.dtype)
            return carry

        lax.fori_loop(0, halves * two, hand, 0)


def feed(core, xt, att, cot, wo, own, other, vec):
    rows, width, seq = xt.shape
    halves, (groups, _, part) = 2, own.shape
    group = width // groups
    aug = group + 16
    full = halves * part

    def whole(a):
        return pl.BlockSpec(a.shape, lambda r: (0,) * len(a.shape), pipeline_mode=pl.Buffered(1))

    per_row = pl.BlockSpec((1, width, seq), lambda r: (r, 0, 0))
    token = pl.BlockSpec((seq, width), lambda r: (r, 0))
    sums = (halves, groups // 2, 2 * group + 32, part)
    outs = [
        jax.ShapeDtypeStruct((rows * seq, width), F32),
        jax.ShapeDtypeStruct((rows, width, seq), F32),
        jax.ShapeDtypeStruct((rows, width, seq), BF),
        jax.ShapeDtypeStruct((rows, 16, seq), F32),
        jax.ShapeDtypeStruct(sums, F32),
        jax.ShapeDtypeStruct(sums, BF),
        jax.ShapeDtypeStruct((width // 2, width), F32),
        jax.ShapeDtypeStruct((width // 2, width), BF),
    ]
    return pl.pallas_call(
        feed_kernel,
        grid=(rows,),
        in_specs=[pl.BlockSpec(memory_space=pltpu.SMEM), per_row, per_row, token] + [whole(a) for a in (wo, own, other, vec)],
        out_specs=[token, per_row, per_row, pl.BlockSpec((1, 16, seq), lambda r: (r, 0, 0))]
        + [whole(a) for a in outs[4:]],
        out_shape=outs,
        scratch_shapes=[
            pltpu.VMEM((width, seq), F32),
            pltpu.VMEM((width, seq), F32),
            pltpu.VMEM((width, seq), F32),
            pltpu.VMEM((groups, aug, seq), BF),
            pltpu.VMEM((groups, full, seq), BF),
            pltpu.VMEM((groups, full, seq), F32),
            pltpu.VMEM((width, seq), BF),
            pltpu.VMEM((2, full, seq), BF),
            pltpu.VMEM((width, seq), BF),
            pltpu.VMEM((6, width, 128), F32),
            pltpu.VMEM((width, width), BF),
            pltpu.VMEM((groups, full, aug), BF),
            pltpu.VMEM((groups, full, group), BF),
            pltpu.VMEM((6, width, 128), F32),
            pltpu.VMEM((2, width // 2, width), F32),
            pltpu.VMEM((halves, groups, 2 * group + 32, part), F32),
        ],
        compiler_params=pltpu.CompilerParams(vmem_limit_bytes=63 * 2**20),
        cost_estimate=pl.CostEstimate(flops=int(25e9), transcendentals=0, bytes_accessed=35 * 2**20),
        name="feed",
    )(core, xt, att, cot, wo, own, other, vec)


def split3(v):
    hi = v.astype(BF).astype(F32)
    mid = (v - hi).astype(BF).astype(F32)
    return hi, mid, v - hi - mid


def back_kernel(
    core_ref, qkv_ref, gatt_ref, xt_ref, lse_ref, delta_ref, seg_ref, *rest, head0, fresh, final, passed
):
    rest = list(rest)
    if passed:
        del rest[-12 - passed : -12]
    if not fresh:
        dwin_ref, bsin_ref = rest[:2]
    d_ref = rest[-12]
    oa_ref, ob_ref = rest[-11:-9]
    qa_ref, ka_ref, va_ref, ga_ref, p_ref, dst_ref, ds_ref, dw_ref, bsum_ref = rest[-9:]
    chans, seq = xt_ref.shape[1:]
    groups, group = dw_ref.shape[1:3]
    first = pl.program_id(0) == 0
    last = pl.program_id(0) == pl.num_programs(0) - 1

    @pl.when(first)
    def _():
        if fresh:
            dw_ref[...] = jnp.zeros_like(dw_ref)
            bsum_ref[...] = jnp.zeros_like(bsum_ref)
        else:
            dw_ref[...] = dwin_ref[...]
            bsum_ref[...] = bsin_ref[...]

    seg = seg_ref[0]
    rank = lax.broadcasted_iota(jnp.int32, (16, seq), 0)
    same = rank == seg
    hot = jnp.where(same, 1.0, 0.0)
    for n in range(BUF):
        ka_ref[n, 64:80, :] = jnp.where(rank < 4, jnp.where(same, 0.0, NEG), jnp.where(rank < 7, -1.0, 0.0)).astype(BF)
        va_ref[n, 64:80, :] = jnp.where(rank < 3, -1.0, 0.0).astype(BF)

    def weigh(h):
        n = h % BUF
        rows = slice(h * HEAD_DIM, (h + 1) * HEAD_DIM)
        hi, mid, lo = split3(lse_ref[0, head0 + h : head0 + h + 1, :])
        tail = jnp.where(rank == 4, hi, jnp.where(rank == 5, mid, jnp.where(rank == 6, lo, 0.0)))
        qa_ref[n, 64:80, :] = jnp.where(rank < 4, hot, tail).astype(BF)
        hi, mid, lo = split3(delta_ref[0, head0 + h : head0 + h + 1, :])
        ga_ref[n, 64:80, :] = jnp.where(rank == 0, hi, jnp.where(rank == 1, mid, jnp.where(rank == 2, lo, 0.0))).astype(BF)
        qa_ref[n, 0:64, :] = qkv_ref[0, 0, rows, :] * jnp.asarray(0.125, BF)
        ka_ref[n, 0:64, :] = qkv_ref[0, 1, rows, :]
        va_ref[n, 0:64, :] = qkv_ref[0, 2, rows, :]
        ga_ref[n, 0:64, :] = gatt_ref[0, rows, :]
        kn = ka_ref[n].T
        vn = va_ref[n].T
        for t in range(seq // 256):
            cols = slice(t * 256, t * 256 + 256)
            p = jnp.exp(dot_nn(kn, qa_ref[n, :, cols]))
            low = p.astype(BF)
            p_ref[n, cols, :] = low.T
            ds = (p * dot_nn(vn, ga_ref[n, :, cols])).astype(BF)
            ds_ref[n, t] = ds
            dst_ref[n, cols, :] = ds.T

    def gather_head(h):
        n = h % BUF
        rows = slice(h * HEAD_DIM, (h + 1) * HEAD_DIM)
        kt = qkv_ref[0, 1, rows, :]
        dv = dot_nn(gatt_ref[0, rows, :], p_ref[n])
        dk = dot_nn(qa_ref[n, 0:64, :], dst_ref[n])
        dq = []
        for t in range(seq // 256):
            cols = slice(t * 256, t * 256 + 256)
            dq.append(dot_nn(kt, ds_ref[n, t]) * 0.125)
        dq = jnp.concatenate(dq, axis=1)
        bsum_ref[0, rows, :] += fold(dq)
        bsum_ref[1, rows, :] += fold(dv)
        d_ref[0, 0, rows, :] = dq.astype(BF)
        d_ref[0, 1, rows, :] = dk.astype(BF)
        d_ref[0, 2, rows, :] = dv.astype(BF)

    heads = chans // HEAD_DIM
    for h in range(heads + 1):
        if h < heads:
            weigh(h)
        if h > 0:
            gather_head(h - 1)
    for g in range(groups):
        s = slice(g * group, (g + 1) * group)
        for j in range(3):
            dw_ref[j, g] += dot_nt(xt_ref[0, s, :], d_ref[0, j, s, :])

    if not final:
        @pl.when(last)
        def _():
            oa_ref[...] = dw_ref[...]
            ob_ref[...] = bsum_ref[...]

    else:
        @pl.when(last)
        def _():
            half = PACK // 2
            core = core_ref[0]

            def put(row, value):
                rows = value.shape[0]
                where = row // half
                at = slice(row % half, row % half + rows)

                @pl.when(core == where)
                def _():
                    oa_ref[at, :] = value

                @pl.when(core != where)
                def _():
                    ob_ref[at, :] = value.astype(BF)

            tiles = chans // 128
            bias = jnp.concatenate([jnp.sum(bsum_ref[n].T, axis=0, keepdims=True) for n in range(2)], axis=0)
            bias = jnp.concatenate([bias, jnp.zeros((6, chans), F32)], axis=0)
            for j in range(3):
                both = jnp.concatenate([dw_ref[j, g] for g in range(groups)], axis=1)
                for c in range(tiles):
                    for a in range(0, group, 64):
                        put(c * 3 * group + j * group + a, both[a : a + 64, c * 128 : c * 128 + 128])
            for c in range(tiles):
                put(tiles * 3 * group + 8 * c, bias[:, c * 128 : c * 128 + 128])
            for row in range(tiles * 3 * group + 8 * tiles, PACK, 8):
                put(row, jnp.zeros((8, 128), F32))


PACK = 1792
BUF = 2


def back(core, qkv, gatt, xt, lse, delta, seg, w, index, parts, row0, count, carried, into, final, sends, keeps):
    rows, _, width, seq = qkv.shape
    chans = width // parts
    groups, group = w.shape[1] // parts, w.shape[2]
    per_row = pl.BlockSpec((1, chans, seq), lambda r: (r + row0, index, 0))
    full = pl.BlockSpec((1, 16, seq), lambda r: (r + row0, 0, 0))
    in_specs = [
        pl.BlockSpec(memory_space=pltpu.SMEM),
        pl.BlockSpec((1, 3, chans, seq), lambda r: (r + row0, 0, index, 0)),
        per_row,
        per_row,
        full,
        full,
        pl.BlockSpec((1, 1, seq), lambda r: (r + row0, 0, 0)),
    ]
    args = [core, qkv, gatt, xt, lse, delta, seg.reshape(rows, 1, seq)]
    sums = [jax.ShapeDtypeStruct((3, groups, group, group), F32), jax.ShapeDtypeStruct((2, chans, 128), F32)]
    if carried is not None:
        in_specs += [pl.BlockSpec((3, groups, group, group), lambda r: (0, 0, 0, 0)), pl.BlockSpec((2, chans, 128), lambda r: (0, 0, 0))]
        args += list(carried)
    alias = {}
    if into is not None:
        in_specs.append(pl.BlockSpec(memory_space=pl.ANY))
        args.append(into)
        alias = {len(args) - 1: len(keeps)}
    for n, value in enumerate(keeps):
        alias[len(args)] = n
        in_specs.append(pl.BlockSpec(memory_space=pl.ANY))
        args.append(value)
    for value in sends:
        in_specs.append(pl.BlockSpec(memory_space=pl.ANY))
        args.append(value)
    if final:
        outs = [jax.ShapeDtypeStruct((PACK // 2, 128), F32), jax.ShapeDtypeStruct((PACK // 2, 128), BF)]
    else:
        outs = sums
    return pl.pallas_call(
        partial(back_kernel, head0=index * (chans // HEAD_DIM), fresh=carried is None, final=final, passed=len(keeps)),
        grid=(count,),
        in_specs=in_specs,
        out_specs=[pl.BlockSpec(memory_space=pl.ANY) for _ in keeps]
        + [pl.BlockSpec((1, 3, chans, seq), lambda r: (r + row0, 0, index, 0))]
        + [pl.BlockSpec(o.shape, lambda r, n=len(o.shape): (0,) * n) for o in outs],
        out_shape=[jax.ShapeDtypeStruct(value.shape, value.dtype) for value in keeps]
        + [jax.ShapeDtypeStruct((rows, 3, width, seq), BF)]
        + outs,
        scratch_shapes=[pltpu.VMEM((BUF, 80, seq), BF) for _ in range(4)]
        + [pltpu.VMEM((BUF, seq, seq), BF) for _ in range(2)]
        + [pltpu.VMEM((BUF, seq // 256, seq, 256), BF)]
        + [pltpu.VMEM(o.shape, F32) for o in sums],
        input_output_aliases=alias,
        compiler_params=params("arbitrary"),
        cost_estimate=pl.CostEstimate(flops=int(8e9 * count), transcendentals=0, bytes_accessed=20 * 2**20),
        name="back",
    )(*args)


def input_kernel(d_ref, gr1_ref, w_ref, *rest):
    gin_ref = rest[-1]
    groups, group = w_ref.shape[1:3]
    parts = []
    for g in range(groups):
        s = slice(g * group, (g + 1) * group)
        total = gr1_ref[0, s, :]
        for j in range(3):
            total = total + dot_nn(w_ref[j, g], d_ref[0, j, s, :])
        parts.append(total)
    gin_ref[...] = jnp.concatenate(parts, axis=0).T


def input_grad(d, gr1, w, row0, count, into, sends, keeps):
    rows, _, width, seq = d.shape
    in_specs = [
        pl.BlockSpec((1, 3, width, seq), lambda r: (r + row0, 0, 0, 0)),
        pl.BlockSpec((1, width, seq), lambda r: (r + row0, 0, 0)),
        pl.BlockSpec(w.shape, lambda r: (0, 0, 0, 0)),
    ]
    args = [d, gr1, w]
    alias = {}
    if into is not None:
        alias[len(args)] = len(keeps)
        args.append(into)
    for n, value in enumerate(keeps):
        alias[len(args)] = n
        args.append(value)
    args += sends
    in_specs += [pl.BlockSpec(memory_space=pl.ANY)] * (len(args) - len(in_specs))
    return pl.pallas_call(
        input_kernel,
        grid=(count,),
        in_specs=in_specs,
        out_specs=[pl.BlockSpec(memory_space=pl.ANY) for _ in keeps] + [pl.BlockSpec((seq, width), lambda r: (r + row0, 0))],
        out_shape=[jax.ShapeDtypeStruct(value.shape, value.dtype) for value in keeps]
        + [jax.ShapeDtypeStruct((rows * seq, width), F32)],
        input_output_aliases=alias,
        compiler_params=params("arbitrary"),
        cost_estimate=pl.CostEstimate(flops=int(8e9 * count), transcendentals=0, bytes_accessed=6 * count * 2**20),
        name="input_grad",
    )(*args)


class Pair:
    def __init__(self, name, size, bit):
        self.name, self.size, self.bit = name, size, bit
        self.side = (lax.axis_index(name) // bit) % 2

    def swap(self, values):
        pairs = [(i, i ^ self.bit) for i in range(self.size)]
        return [lax.ppermute(value, self.name, pairs) for value in values]

    def split(self, value):
        half = value.shape[0] // 2
        keep = lax.dynamic_slice_in_dim(value, self.side * half, half, 0)
        send = lax.dynamic_slice_in_dim(value, (1 - self.side) * half, half, 0)
        return keep, [send.astype(BF)]

    def join(self, value):
        (other,) = self.swap([value])
        return jnp.where(self.side == 0, jnp.concatenate([value, other]), jnp.concatenate([other, value]))


class Quad:
    def __init__(self, a, b):
        self.a, self.b = a, b

    def swap(self, values):
        a, b = self.a, self.b
        if a.name == b.name:
            both = Pair(a.name, a.size, a.bit | b.bit).swap(values[2:])
        else:
            pairs = [(i * b.size + j, (i ^ a.bit) * b.size + (j ^ b.bit)) for i in range(a.size) for j in range(b.size)]
            both = [lax.ppermute(values[2], (a.name, b.name), pairs)]
        return list(b.swap(values[:1])) + list(a.swap(values[1:2])) + list(both)

    def split(self, value):
        part = value.shape[0] // 4

        def piece(da, db):
            at = (self.a.side ^ da) * 2 + (self.b.side ^ db)
            return lax.dynamic_slice_in_dim(value, at * part, part, 0)

        return piece(0, 0), [piece(*d).astype(BF) for d in ((0, 1), (1, 0), (1, 1))]

    def join(self, value):
        near = jnp.stack([value] + self.swap([value] * 3)).reshape((2, 2) + value.shape)
        near = jnp.where(self.a.side == 0, near, near[::-1])
        near = jnp.where(self.b.side == 0, near, near[:, ::-1])
        return near.reshape((4 * value.shape[0],) + value.shape[1:])


def add(keep, got):
    total = keep
    for value in got:
        total = total + value.astype(F32)
    return total


def sum_across(low, bits):
    for bit in bits:
        (got,) = bit.swap([low])
        low = (low.astype(F32) + got.astype(F32)).astype(BF)
    return low


def finish_kernel(
    core_ref, fo_ref, fo_got_ref, p_ref, p_got_ref,
    dqkv_ref, qvb_ref, dwo_ref, dup_ref, upb_ref, ddown_ref, small_ref, fo_all, p_all,
):
    core = core_ref[0]
    fo_all[core] = fo_ref[...]
    fo_all[1 - core] = fo_got_ref[...]
    p_all[core] = p_ref[...]
    p_all[1 - core] = p_got_ref[...]
    groups, group, part = dup_ref.shape
    aug = group + 16
    block = 2 * group + 32
    width = dwo_ref.shape[1]
    pairs = p_ref.shape[0]
    for c in range(2):
        for k in range(groups // 2):
            g, row = c * (groups // 2) + k, k * block
            dup_ref[g] = fo_all[c, row : row + group, :].astype(F32)
            upb_ref[g : g + 1, :] = fo_all[c, row + group : row + aug, :].astype(F32)[0:1]
            ddown_ref[g] = fo_all[c, row + aug : row + aug + group, :].astype(F32)
        rows = width // 8
        for x in range(2):
            for y in range(2):
                for k in range(2):
                    at = 2 * block + ((x * 2 + y) * 2 + k) * rows
                    to = c * (width // 2) + x * (width // 4) + y * rows
                    dwo_ref[to : to + rows, k * part : (k + 1) * part] = fo_all[c, at : at + rows, :].astype(F32)
    lines = fo_all[0, aug + group : block, :].astype(F32)
    for n in range(6):
        for k in range(width // part):
            at = n * (width // part) + k
            small_ref[n : n + 1, k * part : (k + 1) * part] = lines[at : at + 1]
    chans = width // pairs
    tiles = chans // 128
    per = groups // pairs
    half = PACK // 2
    for p in range(pairs):
        def take(row, count):
            got = []
            while count:
                c, at = row // half, row % half
                n = min(count, half - at)
                got.append(p_all[c, p, at : at + n, :].astype(F32))
                row, count = row + n, count - n
            return got[0] if len(got) == 1 else jnp.concatenate(got, axis=0)

        for j in range(3):
            both = jnp.concatenate([take((c * 3 + j) * per * group // per, group) for c in range(tiles)], axis=1)
            for g in range(per):
                dqkv_ref[j, p * per + g] = both[:, g * group : (g + 1) * group]
        bias = jnp.concatenate([take(tiles * 3 * group + 8 * c, 8) for c in range(tiles)], axis=1)
        qvb_ref[:, p * chans : (p + 1) * chans] = bias[0:2]


def finish(core, fo, fo_got, p, p_got, groups, group, part):
    width = groups * group
    shapes = [(3, groups, group, group), (2, width), (width, width), (groups, group, part), (groups, part), (groups, group, part), (8, width)]
    args = [fo, fo_got, p, p_got]

    def whole(shape):
        return pl.BlockSpec(shape, lambda i, n=len(shape): (0,) * n)

    return pl.pallas_call(
        finish_kernel,
        grid=(1,),
        in_specs=[pl.BlockSpec(memory_space=pltpu.SMEM)] + [whole(a.shape) for a in args],
        out_specs=[whole(shape) for shape in shapes],
        out_shape=[jax.ShapeDtypeStruct(shape, F32) for shape in shapes],
        scratch_shapes=[pltpu.VMEM((2,) + fo.shape, BF), pltpu.VMEM((2,) + p.shape, BF)],
        compiler_params=params("arbitrary"),
        name="finish",
    )(core, *args)


def per_device(
    inputs, segments, cotangent, qkv_weight, qv_bias, out_weight, out_bias, ln1_gain, ln1_bias,
    up_weight, up_bias, down_weight, down_bias, ln2_gain, ln2_bias, *, dp, ffn,
):
    groups, group = qkv_weight.shape[1:3]
    part = up_weight.shape[2]
    assert ffn == 2
    bits = [Pair("dp", dp, 1 << k) for k in range(dp.bit_length() - 1)]
    core, ax, rest = bits[0], bits[1], bits[2:]
    ay = Pair("ffn", ffn, 1)
    plane = Quad(ax, ay)
    core_id = core.side.astype(jnp.int32).reshape(1)
    rows = segments.shape[0]

    wall = jnp.concatenate(
        [up_weight, up_bias[:, None, :], jnp.zeros((groups, 15, part), BF), down_weight], axis=1
    )
    (fetched,) = ay.swap([lax.dynamic_slice_in_dim(wall, core.side * (groups // 2), groups // 2, 0)])
    xt, qkv, att, lse = attend(inputs, segments, qkv_weight, qv_bias)
    other = core.join(jnp.where(lse[0, 0, 0] < jnp.inf, fetched, jnp.zeros_like(fetched)))
    zero = jnp.zeros_like(out_bias)
    vec = jnp.stack([out_bias, ln1_gain, ln1_bias, down_bias, ln2_gain, ln2_bias, zero, zero])
    layer_out, gr1, gatt, delta, *first = feed(core_id, xt, att, cotangent, out_weight, wall, other, vec)

    parts = 2
    state = {"grads": None, "carried": None, "input": None}
    packs = []

    def under(calls, *stages):
        keeps = [keep for _, keep, _ in stages]
        got = [exchange.swap(sends) for exchange, _, sends in stages]
        for call in calls:
            keeps = call([], keeps)
        return [add(keep, arrived) for keep, arrived in zip(keeps, got)]

    def part_of_back(index, row0, count):
        def call(sends, keeps):
            final = row0 + count >= rows
            outs = back(
                core_id, qkv, gatt, xt, lse, delta, segments, qkv_weight, index, parts, row0, count,
                state["carried"], state["grads"], final, sends, keeps,
            )
            state["grads"], *carried = outs[len(keeps) :]
            state["carried"] = None if final else carried
            if final:
                packs.append(carried)
            return list(outs[: len(keeps)])

        return call

    def part_of_input(row0, count):
        def call(sends, keeps):
            *kept, state["input"] = input_grad(state["grads"], gr1, qkv_weight, row0, count, state["input"], sends, keeps)
            return kept

        return call

    def cut(index, at):
        return [part_of_back(index, row0, end - row0) for row0, end in zip([0] + at, at + [rows]) if end > row0]

    calls = [cut(0, [rows // 4]), cut(1, [rows // 2])]
    ffn1, out1 = under(calls[0][:1], (core, first[0], [first[1]]), (core, first[2], [first[3]]))
    ffn2, out2 = under(calls[0][1:], (ay, ffn1[0], [ffn1[1].astype(BF)]), (ax, *ax.split(out1)))
    keep, send = packs[0]
    ffn3, out3, sum0 = under(calls[1][:1], (ax, *ax.split(ffn2)), (ay, *ay.split(out2)), (core, keep, [send]))
    both = jnp.concatenate([ffn3[0], out3[:, :part], out3[:, part:]])
    both, sum0 = under(calls[1][1:], (rest[0], *rest[0].split(both)), (plane, *plane.split(sum0)))
    keep, send = packs[1]
    low = both.astype(BF)
    both, sum1 = under(
        [part_of_input(0, rows - rows // 2)], (rest[1], low.astype(F32), [low]), (core, keep, [send])
    )
    (sum1,) = under([part_of_input(rows - rows // 2, rows // 2)] if rows > 1 else [], (plane, *plane.split(sum1)))
    sums = sum_across(jnp.stack([sum0, sum1]).astype(BF), rest)
    both = rest[0].join(sum_across(both.astype(BF), rest[2:]))
    block = 2 * group + 32
    ffns = ax.join(both[None, :block])
    outs = plane.join(both[None, block:])
    fo = jnp.concatenate([ffns.reshape(-1, part), outs.reshape(-1, part)])
    (fo_got,) = core.swap([fo])
    sums = plane.join(sums[None]).swapaxes(0, 1).reshape(parts, -1, 128)
    (p_got,) = core.swap([sums])
    grad_inputs = state["input"]
    dqkv, qvb, dwo, dup, upb, ddown, small = finish(core_id, fo, fo_got, sums, p_got, groups, group, part)
    return (
        layer_out, grad_inputs, dqkv, qvb, dwo, small[0], small[1], small[2],
        dup, upb, ddown, small[3], small[4], small[5],
    )


def solution(mesh):
    rows = P(("dp", "ffn"), None)
    shared = P()
    split = P(None, None, "ffn")
    return jax.shard_map(
        partial(per_device, dp=mesh.shape["dp"], ffn=mesh.shape["ffn"]),
        mesh=mesh,
        in_specs=(rows, rows, rows) + (shared,) * 6 + (split, P(None, "ffn"), split) + (shared,) * 3,
        out_specs=(rows, rows) + (shared,) * 6 + (split, P(None, "ffn"), split) + (shared,) * 3,
        check_vma=False,
    )
```

```python
from functools import partial

import jax
import jax.numpy as jnp
from jax import lax
from jax.experimental import pallas as pl
from jax.experimental.pallas import tpu as pltpu
from jax.sharding import PartitionSpec as P

HEADS = 12
HEAD_DIM = 64
EPS = 1e-05
NEG = -1e30
BF = jnp.bfloat16
F32 = jnp.float32


def dot_nn(a, b):
    return jnp.dot(a, b, preferred_element_type=F32)


def dot_nt(a, b):
    return lax.dot_general(a, b, (((1,), (1,)), ((), ())), preferred_element_type=F32)


def params(*sem, mib=32):
    return pltpu.CompilerParams(vmem_limit_bytes=mib * 2**20, dimension_semantics=sem)


def wide(column, lanes):
    return jnp.concatenate([column] * (lanes // 128), axis=1)


def fold(values):
    total = values[:, 0:128]
    for start in range(128, values.shape[1], 128):
        total = total + values[:, start : start + 128]
    return total


def sub_sum(values):
    total = values[0:8]
    for start in range(8, values.shape[0], 8):
        total = total + values[start : start + 8]
    return total


HB = 1
LT = 256


def attend_kernel(
    x_ref, seg_ref, w_ref, bias_in_ref, xt_ref, qkv_ref, att_ref, lse_ref,
    qa_ref, ka_ref, s_ref, p_ref, tot_ref, wt_ref, bias_ref,
):
    seq, width = x_ref.shape
    groups = wt_ref.shape[0]
    group = width // groups

    @pl.when(pl.program_id(0) == 0)
    def _():
        for g in range(groups):
            for j in range(3):
                wt_ref[g, j * group : (j + 1) * group, :] = w_ref[j, g].T
        columns = jnp.concatenate([bias_in_ref[...], jnp.zeros((6, width), F32)], axis=0).T
        for n in range(2):
            bias_ref[n] = jnp.broadcast_to(columns[:, n : n + 1], (width, 128))

    xt_ref[0] = x_ref[...].T
    seg = seg_ref[0]
    rank = lax.broadcasted_iota(jnp.int32, (16, seq), 0)
    same = rank == seg
    for n in range(2 * HB):
        qa_ref[n, 64:80, :] = jnp.where(same, 1.0, 0.0).astype(BF)
        ka_ref[n, 64:80, :] = jnp.where(same | (rank >= 4), 0.0, NEG).astype(BF)

    for g in range(groups):
        rows = slice(g * group, (g + 1) * group)
        out = dot_nn(wt_ref[g], xt_ref[0, rows, :])
        for j in range(3):
            part = out[j * group : (j + 1) * group]
            if j != 1:
                part = part + wide(bias_ref[j // 2, rows, :], seq)
            qkv_ref[0, j, rows, :] = part.astype(BF)

    def head_rows(h):
        return slice(h * HEAD_DIM, (h + 1) * HEAD_DIM)

    def scores(h, n):
        rows = head_rows(h)
        qa_ref[n, 0:64, :] = qkv_ref[0, 0, rows, :] * jnp.asarray(0.125, BF)
        ka_ref[n, 0:64, :] = qkv_ref[0, 1, rows, :]
        s_ref[n] = dot_nn(ka_ref[n].T, qa_ref[n])

    def soften(h, n):
        for l in range(0, seq, LT):
            cols = slice(l, l + LT)
            peak = s_ref[n, 0:8, cols]
            for c in range(8, seq, 8):
                peak = jnp.maximum(peak, s_ref[n, c : c + 8, cols])
            peak = jnp.max(peak, axis=0, keepdims=True)
            total = jnp.zeros((8, LT), F32)
            for c in range(0, seq, 16):
                e = jnp.exp(s_ref[n, c : c + 16, cols] - peak)
                total = total + (e[0:8] + e[8:16])
                p_ref[n, c : c + 16, cols] = e.astype(BF)
            total = jnp.sum(total, axis=0, keepdims=True)
            tot_ref[n, 0:1, cols] = 1.0 / total
            tot_ref[n, 1:2, cols] = peak + jnp.log(total)
        lse_ref[0, h : h + 1, :] = tot_ref[n, 1:2, :]

    def mix(h, n):
        rows = head_rows(h)
        att_ref[0, rows, :] = (dot_nn(qkv_ref[0, 2, rows, :], p_ref[n]) * tot_ref[n, 0:1, :]).astype(BF)

    G = HB
    def many(fn, b):
        for k in range(G):
            fn(b * G + k, (b % 2) * G + k)

    batches = HEADS // G
    for b in range(batches + 2):
        if b < batches:
            many(scores, b)
        if 0 <= b - 1 < batches:
            many(soften, b - 1)
        if 0 <= b - 2 < batches:
            many(mix, b - 2)


def attend(x, seg, w, bias):
    width = x.shape[1]
    groups, group = w.shape[1:3]
    rows, seq = seg.shape
    return pl.pallas_call(
        attend_kernel,
        grid=(rows,),
        in_specs=[
            pl.BlockSpec((seq, width), lambda r: (r, 0)),
            pl.BlockSpec((1, 1, seq), lambda r: (r, 0, 0)),
            pl.BlockSpec(w.shape, lambda r: (0, 0, 0, 0)),
            pl.BlockSpec(bias.shape, lambda r: (0, 0)),
        ],
        out_specs=[
            pl.BlockSpec((1, width, seq), lambda r: (r, 0, 0)),
            pl.BlockSpec((1, 3, width, seq), lambda r: (r, 0, 0, 0)),
            pl.BlockSpec((1, width, seq), lambda r: (r, 0, 0)),
            pl.BlockSpec((1, 16, seq), lambda r: (r, 0, 0)),
        ],
        out_shape=[
            jax.ShapeDtypeStruct((rows, width, seq), BF),
            jax.ShapeDtypeStruct((rows, 3, width, seq), BF),
            jax.ShapeDtypeStruct((rows, width, seq), BF),
            jax.ShapeDtypeStruct((rows, 16, seq), F32),
        ],
        scratch_shapes=[pltpu.VMEM((2 * HB, 80, seq), BF) for _ in range(2)]
        + [pltpu.VMEM((2 * HB, seq, seq), F32), pltpu.VMEM((2 * HB, seq, seq), BF), pltpu.VMEM((2 * HB, 8, seq), F32)]
        + [pltpu.VMEM((groups, 3 * group, group), BF), pltpu.VMEM((2, width, 128), F32)],
        compiler_params=params("arbitrary", mib=60),
        cost_estimate=pl.CostEstimate(flops=int(10e9), transcendentals=0, bytes_accessed=20 * 2**20),
        name="attend",
    )(x, seg.reshape(rows, 1, seq), w, bias)

CH = 64
EC = 64
DU = 768
DO = 384
ROOT_HALF = 0.7071067811865476
LOG2E = 1.4426950408889634


def feed_kernel(
    core_ref, xt_ref, att_ref, cot_ref, wo_ref, own_ref, other_ref, vec_in_ref,
    out_ref, gr1_ref, gatt_ref, delta_ref, keep_ref, send_ref, okeep_ref, osend_ref,
    a_ref, u1_ref, v2_ref, nlow_ref, act_ref, gp_ref, gd_ref, gup_ref, ct_ref, acc_ref,
    wot_ref, wut_ref, wdt_ref, vec_ref, dwo_ref, dff_ref,
):
    width, seq = a_ref.shape
    walls = (own_ref, other_ref)
    halves, groups = 2, own_ref.shape[0]
    group = width // groups
    part = own_ref.shape[2]
    full = halves * part
    first = pl.program_id(0) == 0
    last = pl.program_id(0) == pl.num_programs(0) - 1
    inv_width = 1.0 / width
    aug = group + 16

    @pl.when(first)
    def _():
        acc_ref[...] = jnp.zeros_like(acc_ref)
        dwo_ref[...] = jnp.zeros_like(dwo_ref)
        dff_ref[...] = jnp.zeros_like(dff_ref)
        row = lax.broadcasted_iota(jnp.int32, (16, seq), 0)
        for g in range(groups):
            nlow_ref[g, group:aug, :] = jnp.where(row == 0, 1.0, 0.0).astype(BF)
        columns = vec_in_ref[...].T
        for n in range(6):
            vec_ref[n] = jnp.broadcast_to(columns[:, n : n + 1], (width, 128))
        wot_ref[...] = wo_ref[...].T

        def prepare(g, carry):
            for h in range(halves):
                rows = slice(h * part, (h + 1) * part)
                wut_ref[g, rows, :] = walls[h][g, 0:aug, :].T
                wdt_ref[g, rows, :] = (walls[h][g, aug : aug + group, :] * jnp.asarray(0.5, BF)).T
            return carry

        lax.fori_loop(0, groups, prepare, 0)

    ct_ref[...] = cot_ref[...].T

    part_sum = jnp.zeros((8, seq), F32)
    for b in range(0, width, DO):
        mixed = dot_nn(wot_ref[b : b + DO, :], att_ref[0])
        for c in range(0, DO, EC):
            s = slice(b + c, b + c + EC)
            v = mixed[c : c + EC] + wide(vec_ref[0, s, :], seq) + xt_ref[0, s, :].astype(F32)
            a_ref[s, :] = v
            part_sum = part_sum + sub_sum(v)
    mean = jnp.sum(part_sum, axis=0, keepdims=True) * inv_width
    part_sum = jnp.zeros((8, seq), F32)
    for c in range(0, width, CH):
        v = a_ref[c : c + CH, :] - mean
        part_sum = part_sum + sub_sum(v * v)
    r1 = lax.rsqrt(jnp.sum(part_sum, axis=0, keepdims=True) * inv_width + EPS)
    for g in range(groups):
        for c in range(0, group, 64):
            s = slice(g * group + c, g * group + c + 64)
            u = (a_ref[s, :] - mean) * r1
            u1_ref[s, :] = u
            n = u * wide(vec_ref[1, s, :], seq) + wide(vec_ref[2, s, :], seq)
            v2_ref[s, :] = n
            nlow_ref[g, c : c + 64, :] = n.astype(BF)

    part_sum = jnp.zeros((8, seq), F32)
    for g in range(groups):
        for b in range(0, full, DU):
            upward = dot_nn(wut_ref[g, b : b + DU, :], nlow_ref[g])
            for c in range(0, DU, EC):
                s = slice(b + c, b + c + EC)
                u = upward[c : c + EC]
                one = 1.0 + lax.erf(u * ROOT_HALF)
                act_ref[g, s, :] = (u * one).astype(BF)
                bell = jnp.exp2((u * u) * (-0.5 * LOG2E))
                gp_ref[g, s, :] = one + (u * (1.1283791670955126 * ROOT_HALF)) * bell
        s = slice(g * group, (g + 1) * group)
        down = dot_nn(walls[0][g, aug : aug + group, :], act_ref[g, 0:part, :])
        for h in range(1, halves):
            down = down + dot_nn(walls[h][g, aug : aug + group, :], act_ref[g, h * part : (h + 1) * part, :])
        v = v2_ref[s, :] + (down * 0.5 + wide(vec_ref[3, s, :], seq))
        v2_ref[s, :] = v
        part_sum = part_sum + sub_sum(v)

    mean = jnp.sum(part_sum, axis=0, keepdims=True) * inv_width
    part_sum = jnp.zeros((8, seq), F32)
    for c in range(0, width, CH):
        v = v2_ref[c : c + CH, :] - mean
        part_sum = part_sum + sub_sum(v * v)
    r2 = lax.rsqrt(jnp.sum(part_sum, axis=0, keepdims=True) * inv_width + EPS)
    sum_e = jnp.zeros((8, seq), F32)
    sum_eu = jnp.zeros((8, seq), F32)
    for c in range(0, width, CH):
        s = slice(c, c + CH)
        u = (v2_ref[s, :] - mean) * r2
        v2_ref[s, :] = u
        gain = wide(vec_ref[4, s, :], seq)
        out_ref[:, s] = (u * gain + wide(vec_ref[5, s, :], seq)).T
        cot = ct_ref[s, :].astype(F32)
        cu = cot * u
        acc_ref[4, s, :] += fold(cu)
        acc_ref[5, s, :] += fold(cot)
        sum_e = sum_e + sub_sum(cot * gain)
        sum_eu = sum_eu + sub_sum(cu * gain)
    mean_e = jnp.sum(sum_e, axis=0, keepdims=True) * inv_width
    mean_eu = jnp.sum(sum_eu, axis=0, keepdims=True) * inv_width
    for c in range(0, width, CH):
        s = slice(c, c + CH)
        e = ct_ref[s, :].astype(F32) * wide(vec_ref[4, s, :], seq)
        gr = r2 * (e - mean_e - v2_ref[s, :] * mean_eu)
        a_ref[s, :] = gr
        acc_ref[3, s, :] += fold(gr)
        gd_ref[s, :] = gr.astype(BF)

    for g in range(groups):
        rows = slice(g * group, (g + 1) * group)
        for b in range(0, full, DU):
            gact = dot_nn(wdt_ref[g, b : b + DU, :], gd_ref[rows, :])
            for c in range(0, DU, EC):
                s = slice(b + c, b + c + EC)
                gup_ref[g % 2, s, :] = (gact[c : c + EC] * gp_ref[g, s, :]).astype(BF)
        for h in range(halves):
            s = slice(h * part, (h + 1) * part)
            dff_ref[h, g, aug : aug + group, :] += dot_nt(gd_ref[rows, :], act_ref[g, s, :])
            dff_ref[h, g, 0:aug, :] += dot_nt(nlow_ref[g], gup_ref[g % 2, s, :])
        back = dot_nn(walls[0][g, 0:group, :], gup_ref[g % 2, 0:part, :])
        for h in range(1, halves):
            back = back + dot_nn(walls[h][g, 0:group, :], gup_ref[g % 2, h * part : (h + 1) * part, :])
        a_ref[rows, :] += back

    sum_e = jnp.zeros((8, seq), F32)
    sum_eu = jnp.zeros((8, seq), F32)
    for c in range(0, width, CH):
        s = slice(c, c + CH)
        gn = a_ref[s, :]
        gu = gn * u1_ref[s, :]
        acc_ref[1, s, :] += fold(gu)
        acc_ref[2, s, :] += fold(gn)
        gain = wide(vec_ref[1, s, :], seq)
        sum_e = sum_e + sub_sum(gn * gain)
        sum_eu = sum_eu + sub_sum(gu * gain)
    mean_e = jnp.sum(sum_e, axis=0, keepdims=True) * inv_width
    mean_eu = jnp.sum(sum_eu, axis=0, keepdims=True) * inv_width
    for c in range(0, width, CH):
        s = slice(c, c + CH)
        e = a_ref[s, :] * wide(vec_ref[1, s, :], seq)
        gr = r1 * (e - mean_e - u1_ref[s, :] * mean_eu)
        gr1_ref[0, s, :] = gr
        acc_ref[0, s, :] += fold(gr)
        gd_ref[s, :] = gr.astype(BF)
    for b in range(0, width, DO):
        grad = dot_nn(wo_ref[b : b + DO, :], gd_ref[...])
        for c in range(0, DO, HEAD_DIM):
            s = slice(b + c, b + c + HEAD_DIM)
            ga = grad[c : c + HEAD_DIM].astype(BF)
            gatt_ref[0, s, :] = ga
            prod = ga.astype(F32) * att_ref[0, s, :].astype(F32)
            head = (b + c) // HEAD_DIM
            delta_ref[0, head : head + 1, :] = jnp.sum(prod, axis=0, keepdims=True)
    half = width // 2
    for k in range(2):
        dwo_ref[k] += dot_nt(att_ref[0, k * half : (k + 1) * half, :], gd_ref[...])

    @pl.when(last)
    def _():
        for n in range(6):
            line = jnp.sum(acc_ref[n].T, axis=0, keepdims=True)
            for k in range(width // part):
                for h in range(halves):
                    at = aug + group + n * (width // part) + k
                    dff_ref[h, 0, at : at + 1, :] = line[:, k * part : (k + 1) * part]
        core = core_ref[0]
        okeep_ref[...] = dwo_ref[core]
        osend_ref[...] = dwo_ref[1 - core].astype(BF)
        two = groups // 2

        def hand(i, carry):
            h, k = i // two, i % two
            for ref, g in ((keep_ref, core * two + k), (send_ref, (1 - core) * two + k)):
                ref[h, k, 0:aug, :] = dff_ref[h, g, 0:aug, :].astype(ref.dtype)
                ref[h, k, aug : aug + group, :] = (dff_ref[h, g, aug : aug + group, :] * 0.5).astype(ref.dtype)
                ref[h, k, aug + group :, :] = dff_ref[h, g, aug + group :, :].astype(ref.dtype)
            return carry

        lax.fori_loop(0, halves * two, hand, 0)


def feed(core, xt, att, cot, wo, own, other, vec):
    rows, width, seq = xt.shape
    halves, (groups, _, part) = 2, own.shape
    group = width // groups
    aug = group + 16
    full = halves * part

    def whole(a):
        return pl.BlockSpec(a.shape, lambda r: (0,) * len(a.shape), pipeline_mode=pl.Buffered(1))

    per_row = pl.BlockSpec((1, width, seq), lambda r: (r, 0, 0))
    token = pl.BlockSpec((seq, width), lambda r: (r, 0))
    sums = (halves, groups // 2, 2 * group + 32, part)
    outs = [
        jax.ShapeDtypeStruct((rows * seq, width), F32),
        jax.ShapeDtypeStruct((rows, width, seq), F32),
        jax.ShapeDtypeStruct((rows, width, seq), BF),
        jax.ShapeDtypeStruct((rows, 16, seq), F32),
        jax.ShapeDtypeStruct(sums, F32),
        jax.ShapeDtypeStruct(sums, BF),
        jax.ShapeDtypeStruct((width // 2, width), F32),
        jax.ShapeDtypeStruct((width // 2, width), BF),
    ]
    return pl.pallas_call(
        feed_kernel,
        grid=(rows,),
        in_specs=[pl.BlockSpec(memory_space=pltpu.SMEM), per_row, per_row, token] + [whole(a) for a in (wo, own, other, vec)],
        out_specs=[token, per_row, per_row, pl.BlockSpec((1, 16, seq), lambda r: (r, 0, 0))]
        + [whole(a) for a in outs[4:]],
        out_shape=outs,
        scratch_shapes=[
            pltpu.VMEM((width, seq), F32),
            pltpu.VMEM((width, seq), F32),
            pltpu.VMEM((width, seq), F32),
            pltpu.VMEM((groups, aug, seq), BF),
            pltpu.VMEM((groups, full, seq), BF),
            pltpu.VMEM((groups, full, seq), F32),
            pltpu.VMEM((width, seq), BF),
            pltpu.VMEM((2, full, seq), BF),
            pltpu.VMEM((width, seq), BF),
            pltpu.VMEM((6, width, 128), F32),
            pltpu.VMEM((width, width), BF),
            pltpu.VMEM((groups, full, aug), BF),
            pltpu.VMEM((groups, full, group), BF),
            pltpu.VMEM((6, width, 128), F32),
            pltpu.VMEM((2, width // 2, width), F32),
            pltpu.VMEM((halves, groups, 2 * group + 32, part), F32),
        ],
        compiler_params=pltpu.CompilerParams(vmem_limit_bytes=63 * 2**20),
        cost_estimate=pl.CostEstimate(flops=int(25e9), transcendentals=0, bytes_accessed=35 * 2**20),
        name="feed",
    )(core, xt, att, cot, wo, own, other, vec)


def split3(v):
    hi = v.astype(BF).astype(F32)
    mid = (v - hi).astype(BF).astype(F32)
    return hi, mid, v - hi - mid


def back_kernel(
    core_ref, qkv_ref, gatt_ref, xt_ref, lse_ref, delta_ref, seg_ref, *rest, head0, fresh, final, passed
):
    rest = list(rest)
    if passed:
        del rest[-12 - passed : -12]
    if not fresh:
        dwin_ref, bsin_ref = rest[:2]
    d_ref = rest[-12]
    oa_ref, ob_ref = rest[-11:-9]
    qa_ref, ka_ref, va_ref, ga_ref, p_ref, dst_ref, ds_ref, dw_ref, bsum_ref = rest[-9:]
    chans, seq = xt_ref.shape[1:]
    groups, group = dw_ref.shape[1:3]
    first = pl.program_id(0) == 0
    last = pl.program_id(0) == pl.num_programs(0) - 1

    @pl.when(first)
    def _():
        if fresh:
            dw_ref[...] = jnp.zeros_like(dw_ref)
            bsum_ref[...] = jnp.zeros_like(bsum_ref)
        else:
            dw_ref[...] = dwin_ref[...]
            bsum_ref[...] = bsin_ref[...]

    seg = seg_ref[0]
    rank = lax.broadcasted_iota(jnp.int32, (16, seq), 0)
    same = rank == seg
    hot = jnp.where(same, 1.0, 0.0)
    for n in range(BUF):
        ka_ref[n, 64:80, :] = jnp.where(rank < 4, jnp.where(same, 0.0, NEG), jnp.where(rank < 7, -1.0, 0.0)).astype(BF)
        va_ref[n, 64:80, :] = jnp.where(rank < 3, -1.0, 0.0).astype(BF)

    def weigh(h):
        n = h % BUF
        rows = slice(h * HEAD_DIM, (h + 1) * HEAD_DIM)
        hi, mid, lo = split3(lse_ref[0, head0 + h : head0 + h + 1, :])
        tail = jnp.where(rank == 4, hi, jnp.where(rank == 5, mid, jnp.where(rank == 6, lo, 0.0)))
        qa_ref[n, 64:80, :] = jnp.where(rank < 4, hot, tail).astype(BF)
        hi, mid, lo = split3(delta_ref[0, head0 + h : head0 + h + 1, :])
        ga_ref[n, 64:80, :] = jnp.where(rank == 0, hi, jnp.where(rank == 1, mid, jnp.where(rank == 2, lo, 0.0))).astype(BF)
        qa_ref[n, 0:64, :] = qkv_ref[0, 0, rows, :] * jnp.asarray(0.125, BF)
        ka_ref[n, 0:64, :] = qkv_ref[0, 1, rows, :]
        va_ref[n, 0:64, :] = qkv_ref[0, 2, rows, :]
        ga_ref[n, 0:64, :] = gatt_ref[0, rows, :]
        kn = ka_ref[n].T
        vn = va_ref[n].T
        for t in range(seq // 256):
            cols = slice(t * 256, t * 256 + 256)
            p = jnp.exp(dot_nn(kn, qa_ref[n, :, cols]))
            low = p.astype(BF)
            p_ref[n, cols, :] = low.T
            ds = (p * dot_nn(vn, ga_ref[n, :, cols])).astype(BF)
            ds_ref[n, t] = ds
            dst_ref[n, cols, :] = ds.T

    def gather_head(h):
        n = h % BUF
        rows = slice(h * HEAD_DIM, (h + 1) * HEAD_DIM)
        kt = qkv_ref[0, 1, rows, :]
        dv = dot_nn(gatt_ref[0, rows, :], p_ref[n])
        dk = dot_nn(qa_ref[n, 0:64, :], dst_ref[n])
        dq = []
        for t in range(seq // 256):
            cols = slice(t * 256, t * 256 + 256)
            dq.append(dot_nn(kt, ds_ref[n, t]) * 0.125)
        dq = jnp.concatenate(dq, axis=1)
        bsum_ref[0, rows, :] += fold(dq)
        bsum_ref[1, rows, :] += fold(dv)
        d_ref[0, 0, rows, :] = dq.astype(BF)
        d_ref[0, 1, rows, :] = dk.astype(BF)
        d_ref[0, 2, rows, :] = dv.astype(BF)

    heads = chans // HEAD_DIM
    for h in range(heads + 1):
        if h < heads:
            weigh(h)
        if h > 0:
            gather_head(h - 1)
    for g in range(groups):
        s = slice(g * group, (g + 1) * group)
        for j in range(3):
            dw_ref[j, g] += dot_nt(xt_ref[0, s, :], d_ref[0, j, s, :])

    if not final:
        @pl.when(last)
        def _():
            oa_ref[...] = dw_ref[...]
            ob_ref[...] = bsum_ref[...]

    else:
        @pl.when(last)
        def _():
            half = PACK // 2
            core = core_ref[0]

            def put(row, value):
                where = row // half
                at = slice(row % half, row % half + value.shape[0])

                @pl.when(core == where)
                def _():
                    oa_ref[at, :] = value

                @pl.when(core != where)
                def _():
                    ob_ref[at, :] = value.astype(BF)

            for j in range(3):
                both = jnp.concatenate([dw_ref[j, g] for g in range(groups)], axis=1)
                for a in range(0, group, 64):
                    put(j * group + a, both[a : a + 64])
            bias = [jnp.sum(bsum_ref[n].T, axis=0, keepdims=True) for n in range(2)]
            put(3 * group, jnp.concatenate(bias + [jnp.zeros((62, chans), F32)], axis=0))


PACK = 640
BUF = 2


def back(core, qkv, gatt, xt, lse, delta, seg, w, index, parts, row0, count, carried, into, final, sends, keeps):
    rows, _, width, seq = qkv.shape
    chans = width // parts
    groups, group = w.shape[1] // parts, w.shape[2]
    per_row = pl.BlockSpec((1, chans, seq), lambda r: (r + row0, index, 0))
    full = pl.BlockSpec((1, 16, seq), lambda r: (r + row0, 0, 0))
    in_specs = [
        pl.BlockSpec(memory_space=pltpu.SMEM),
        pl.BlockSpec((1, 3, chans, seq), lambda r: (r + row0, 0, index, 0)),
        per_row,
        per_row,
        full,
        full,
        pl.BlockSpec((1, 1, seq), lambda r: (r + row0, 0, 0)),
    ]
    args = [core, qkv, gatt, xt, lse, delta, seg.reshape(rows, 1, seq)]
    sums = [jax.ShapeDtypeStruct((3, groups, group, group), F32), jax.ShapeDtypeStruct((2, chans, 128), F32)]
    if carried is not None:
        in_specs += [pl.BlockSpec((3, groups, group, group), lambda r: (0, 0, 0, 0)), pl.BlockSpec((2, chans, 128), lambda r: (0, 0, 0))]
        args += list(carried)
    alias = {}
    if into is not None:
        in_specs.append(pl.BlockSpec(memory_space=pl.ANY))
        args.append(into)
        alias = {len(args) - 1: len(keeps)}
    for n, value in enumerate(keeps):
        alias[len(args)] = n
        in_specs.append(pl.BlockSpec(memory_space=pl.ANY))
        args.append(value)
    for value in sends:
        in_specs.append(pl.BlockSpec(memory_space=pl.ANY))
        args.append(value)
    if final:
        outs = [jax.ShapeDtypeStruct((PACK // 2, chans), F32), jax.ShapeDtypeStruct((PACK // 2, chans), BF)]
    else:
        outs = sums
    return pl.pallas_call(
        partial(back_kernel, head0=index * (chans // HEAD_DIM), fresh=carried is None, final=final, passed=len(keeps)),
        grid=(count,),
        in_specs=in_specs,
        out_specs=[pl.BlockSpec(memory_space=pl.ANY) for _ in keeps]
        + [pl.BlockSpec((1, 3, chans, seq), lambda r: (r + row0, 0, index, 0))]
        + [pl.BlockSpec(o.shape, lambda r, n=len(o.shape): (0,) * n) for o in outs],
        out_shape=[jax.ShapeDtypeStruct(value.shape, value.dtype) for value in keeps]
        + [jax.ShapeDtypeStruct((rows, 3, width, seq), BF)]
        + outs,
        scratch_shapes=[pltpu.VMEM((BUF, 80, seq), BF) for _ in range(4)]
        + [pltpu.VMEM((BUF, seq, seq), BF) for _ in range(2)]
        + [pltpu.VMEM((BUF, seq // 256, seq, 256), BF)]
        + [pltpu.VMEM(o.shape, F32) for o in sums],
        input_output_aliases=alias,
        compiler_params=params("arbitrary", mib=20),
        cost_estimate=pl.CostEstimate(flops=int(8e9 * count), transcendentals=0, bytes_accessed=20 * 2**20),
        name="back",
    )(*args)


def input_kernel(d_ref, gr1_ref, w_ref, *rest):
    gin_ref = rest[-1]
    groups, group = w_ref.shape[1:3]
    parts = []
    for g in range(groups):
        s = slice(g * group, (g + 1) * group)
        total = gr1_ref[0, s, :]
        for j in range(3):
            total = total + dot_nn(w_ref[j, g], d_ref[0, j, s, :])
        parts.append(total)
    gin_ref[...] = jnp.concatenate(parts, axis=0).T


def input_grad(d, gr1, w, row0, count, into, sends, keeps):
    rows, _, width, seq = d.shape
    in_specs = [
        pl.BlockSpec((1, 3, width, seq), lambda r: (r + row0, 0, 0, 0)),
        pl.BlockSpec((1, width, seq), lambda r: (r + row0, 0, 0)),
        pl.BlockSpec(w.shape, lambda r: (0, 0, 0, 0)),
    ]
    args = [d, gr1, w]
    alias = {}
    if into is not None:
        alias[len(args)] = len(keeps)
        args.append(into)
    for n, value in enumerate(keeps):
        alias[len(args)] = n
        args.append(value)
    args += sends
    in_specs += [pl.BlockSpec(memory_space=pl.ANY)] * (len(args) - len(in_specs))
    return pl.pallas_call(
        input_kernel,
        grid=(count,),
        in_specs=in_specs,
        out_specs=[pl.BlockSpec(memory_space=pl.ANY) for _ in keeps] + [pl.BlockSpec((seq, width), lambda r: (r + row0, 0))],
        out_shape=[jax.ShapeDtypeStruct(value.shape, value.dtype) for value in keeps]
        + [jax.ShapeDtypeStruct((rows * seq, width), F32)],
        input_output_aliases=alias,
        compiler_params=params("arbitrary", mib=20),
        cost_estimate=pl.CostEstimate(flops=int(8e9 * count), transcendentals=0, bytes_accessed=6 * count * 2**20),
        name="input_grad",
    )(*args)


class Pair:
    def __init__(self, name, size, bit):
        self.name, self.size, self.bit = name, size, bit
        self.side = (lax.axis_index(name) // bit) % 2

    def swap(self, values):
        pairs = [(i, i ^ self.bit) for i in range(self.size)]
        return [lax.ppermute(value, self.name, pairs) for value in values]

    def split(self, value):
        half = value.shape[0] // 2
        keep = lax.dynamic_slice_in_dim(value, self.side * half, half, 0)
        send = lax.dynamic_slice_in_dim(value, (1 - self.side) * half, half, 0)
        return keep, [send.astype(BF)]

    def join(self, value):
        (other,) = self.swap([value])
        return jnp.where(self.side == 0, jnp.concatenate([value, other]), jnp.concatenate([other, value]))


class Quad:
    def __init__(self, a, b):
        self.a, self.b = a, b

    def swap(self, values):
        a, b = self.a, self.b
        if a.name == b.name:
            both = Pair(a.name, a.size, a.bit | b.bit).swap(values[2:])
        else:
            pairs = [(i * b.size + j, (i ^ a.bit) * b.size + (j ^ b.bit)) for i in range(a.size) for j in range(b.size)]
            both = [lax.ppermute(values[2], (a.name, b.name), pairs)]
        return list(b.swap(values[:1])) + list(a.swap(values[1:2])) + list(both)

    def split(self, value):
        part = value.shape[0] // 4

        def piece(da, db):
            at = (self.a.side ^ da) * 2 + (self.b.side ^ db)
            return lax.dynamic_slice_in_dim(value, at * part, part, 0)

        return piece(0, 0), [piece(*d).astype(BF) for d in ((0, 1), (1, 0), (1, 1))]

    def join(self, value):
        near = jnp.stack([value] + self.swap([value] * 3)).reshape((2, 2) + value.shape)
        near = jnp.where(self.a.side == 0, near, near[::-1])
        near = jnp.where(self.b.side == 0, near, near[:, ::-1])
        return near.reshape((4 * value.shape[0],) + value.shape[1:])


def add(keep, got):
    total = keep
    for value in got:
        total = total + value.astype(F32)
    return total


def sum_across(low, bits):
    for bit in bits:
        (got,) = bit.swap([low])
        low = (low.astype(F32) + got.astype(F32)).astype(BF)
    return low


def finish_kernel(core_ref, own_ref, got_ref, dqkv_ref, qvb_ref, dwo_ref, dup_ref, upb_ref, ddown_ref, small_ref, all_ref):
    core = core_ref[0]
    all_ref[core] = own_ref[...]
    all_ref[1 - core] = got_ref[...]
    groups, group, part = dup_ref.shape
    aug = group + 16
    block = 2 * group + 32
    width = dwo_ref.shape[1]
    for c in range(2):
        for k in range(groups // 2):
            g, row = c * (groups // 2) + k, k * block
            dup_ref[g] = all_ref[c, row : row + group, :].astype(F32)
            upb_ref[g : g + 1, :] = all_ref[c, row + group : row + aug, :].astype(F32)[0:1]
            ddown_ref[g] = all_ref[c, row + aug : row + aug + group, :].astype(F32)
    lines = all_ref[0, aug + group : block, :].astype(F32)
    for n in range(6):
        for k in range(width // part):
            at = n * (width // part) + k
            small_ref[n : n + 1, k * part : (k + 1) * part] = lines[at : at + 1]
    rows = width // 8
    parts = width // part
    per = groups // parts
    quarter = PACK // 8
    place = 2 * rows + parts * quarter
    for q in range(4):
        base = (groups // 2) * block + q * place
        for c in range(2):
            to = c * (width // 2) + q * rows
            for k in range(2):
                at = base + k * rows
                dwo_ref[to : to + rows, k * part : (k + 1) * part] = all_ref[c, at : at + rows, :].astype(F32)
            for p in range(parts):
                at = base + 2 * rows + p * quarter
                row = c * (PACK // 2) + q * quarter
                done = 0
                while done < quarter:
                    j, i = (row + done) // group, (row + done) % group
                    n = min(quarter - done, group - i)
                    values = all_ref[c, at + done : at + done + n, :].astype(F32)
                    if j < 3:
                        for g in range(per):
                            dqkv_ref[j, p * per + g, i : i + n, :] = values[:, g * group : (g + 1) * group]
                    else:
                        qvb_ref[:, p * part : (p + 1) * part] = values[0:2]
                    done += n


def finish(core, own, got, groups, group, part):
    width = groups * group
    shapes = [(3, groups, group, group), (2, width), (width, width), (groups, group, part), (groups, part), (groups, group, part), (8, width)]

    def whole(shape):
        return pl.BlockSpec(shape, lambda i, n=len(shape): (0,) * n)

    return pl.pallas_call(
        finish_kernel,
        grid=(1,),
        in_specs=[pl.BlockSpec(memory_space=pltpu.SMEM), whole(own.shape), whole(got.shape)],
        out_specs=[whole(shape) for shape in shapes],
        out_shape=[jax.ShapeDtypeStruct(shape, F32) for shape in shapes],
        scratch_shapes=[pltpu.VMEM((2,) + own.shape, BF)],
        compiler_params=params("arbitrary", mib=20),
        name="finish",
    )(core, own, got)


def per_device(
    inputs, segments, cotangent, qkv_weight, qv_bias, out_weight, out_bias, ln1_gain, ln1_bias,
    up_weight, up_bias, down_weight, down_bias, ln2_gain, ln2_bias, *, dp, ffn,
):
    groups, group = qkv_weight.shape[1:3]
    part = up_weight.shape[2]
    assert ffn == 2
    bits = [Pair("dp", dp, 1 << k) for k in range(dp.bit_length() - 1)]
    core, ax, rest = bits[0], bits[1], bits[2:]
    ay = Pair("ffn", ffn, 1)
    plane = Quad(ax, ay)
    core_id = core.side.astype(jnp.int32).reshape(1)
    rows = segments.shape[0]

    wall = jnp.concatenate(
        [up_weight, up_bias[:, None, :], jnp.zeros((groups, 15, part), BF), down_weight], axis=1
    )
    (fetched,) = ay.swap([lax.dynamic_slice_in_dim(wall, core.side * (groups // 2), groups // 2, 0)])
    xt, qkv, att, lse = attend(inputs, segments, qkv_weight, qv_bias)
    other = core.join(jnp.where(lse[0, 0, :part] < jnp.inf, fetched, jnp.zeros_like(fetched)))
    zero = jnp.zeros_like(out_bias)
    vec = jnp.stack([out_bias, ln1_gain, ln1_bias, down_bias, ln2_gain, ln2_bias, zero, zero])
    layer_out, gr1, gatt, delta, *first = feed(core_id, xt, att, cotangent, out_weight, wall, other, vec)
    qkv = pltpu.with_memory_space_constraint(qkv, pltpu.HBM)
    gatt = pltpu.with_memory_space_constraint(gatt, pltpu.HBM)
    xt = pltpu.with_memory_space_constraint(xt, pltpu.HBM)
    gr1 = pltpu.with_memory_space_constraint(gr1, pltpu.HBM)

    parts = 2
    state = {"grads": None, "carried": None, "input": None}
    packs = []

    def under(calls, *stages):
        keeps = [keep for _, keep, _ in stages]
        got = [exchange.swap(sends) for exchange, _, sends in stages]
        for call in calls:
            keeps = call([], keeps)
        return [add(keep, arrived) for keep, arrived in zip(keeps, got)]

    def part_of_back(index, row0, count):
        def call(sends, keeps):
            final = row0 + count >= rows
            outs = back(
                core_id, qkv, gatt, xt, lse, delta, segments, qkv_weight, index, parts, row0, count,
                state["carried"], state["grads"], final, sends, keeps,
            )
            state["grads"], *carried = outs[len(keeps) :]
            state["carried"] = None if final else carried
            if final:
                packs.append(carried)
            return list(outs[: len(keeps)])

        return call

    def part_of_input(row0, count):
        def call(sends, keeps):
            *kept, state["input"] = input_grad(state["grads"], gr1, qkv_weight, row0, count, state["input"], sends, keeps)
            return kept

        return call

    def cut(index, at):
        return [part_of_back(index, row0, end - row0) for row0, end in zip([0] + at, at + [rows]) if end > row0]

    calls = [cut(0, [rows // 4]), cut(1, [rows // 2])]
    ffn1, out1 = under(calls[0][:1], (core, first[0], [first[1]]), (core, first[2], [first[3]]))
    ffn2, out2 = under(calls[0][1:], (ay, ffn1[0], [ffn1[1].astype(BF)]), (ax, *ax.split(out1)))
    keep, send = packs[0]
    ffn3, out3, sum0 = under(calls[1][:1], (ax, *ax.split(ffn2)), (ay, *ay.split(out2)), (core, keep, [send]))
    both = jnp.concatenate([ffn3[0], out3[:, :part], out3[:, part:]])
    both, sum0 = under(calls[1][1:], (rest[0], *rest[0].split(both)), (plane, *plane.split(sum0)))
    keep, send = packs[1]
    low = both.astype(BF)
    got = rest[1].swap([low])
    (kept,) = part_of_input(0, rows - rows // 2)([], [low.astype(F32)])
    if rows > 1:
        (kept,) = part_of_input(rows - rows // 2, rows // 2)([], [kept])
    both = add(kept, got)
    pack = add(keep, core.swap([send]))
    keep, sends = plane.split(pack)
    sum1 = add(keep, plane.swap(sends))
    sums = sum_across(jnp.stack([sum0, sum1]).astype(BF), rest)
    both = rest[0].join(sum_across(both.astype(BF), rest[2:]))
    block = 2 * group + 32
    ffns = ax.join(both[None, :block])
    rest_of = plane.join(jnp.concatenate([both[block:], sums.reshape(-1, part)])[None])
    own = jnp.concatenate([ffns.reshape(-1, part), rest_of.reshape(-1, part)])
    (got,) = core.swap([own])
    dqkv, qvb, dwo, dup, upb, ddown, small = finish(core_id, own, got, groups, group, part)
    grad_inputs = state["input"]
    return (
        layer_out, grad_inputs, dqkv, qvb, dwo, small[0], small[1], small[2],
        dup, upb, ddown, small[3], small[4], small[5],
    )


def solution(mesh):
    rows = P(("dp", "ffn"), None)
    shared = P()
    split = P(None, None, "ffn")
    return jax.shard_map(
        partial(per_device, dp=mesh.shape["dp"], ffn=mesh.shape["ffn"]),
        mesh=mesh,
        in_specs=(rows, rows, rows) + (shared,) * 6 + (split, P(None, "ffn"), split) + (shared,) * 3,
        out_specs=(rows, rows) + (shared,) * 6 + (split, P(None, "ffn"), split) + (shared,) * 3,
        check_vma=False,
    )
```

```python
from functools import partial

import jax
import jax.numpy as jnp
from jax import lax
from jax.experimental import pallas as pl
from jax.experimental.pallas import tpu as pltpu
from jax.sharding import PartitionSpec as P

HEADS = 12
HEAD_DIM = 64
EPS = 1e-05
NEG = -1e30
BF = jnp.bfloat16
F32 = jnp.float32


def dot_nn(a, b):
    return jnp.dot(a, b, preferred_element_type=F32)


def dot_nt(a, b):
    return lax.dot_general(a, b, (((1,), (1,)), ((), ())), preferred_element_type=F32)


def params(*sem, mib=32):
    return pltpu.CompilerParams(vmem_limit_bytes=mib * 2**20, dimension_semantics=sem)


def wide(column, lanes):
    return jnp.concatenate([column] * (lanes // 128), axis=1)


def fold(values):
    total = values[:, 0:128]
    for start in range(128, values.shape[1], 128):
        total = total + values[:, start : start + 128]
    return total


def sub_sum(values):
    total = values[0:8]
    for start in range(8, values.shape[0], 8):
        total = total + values[start : start + 8]
    return total


HB = 1
LT = 256


def attend_kernel(
    x_ref, seg_ref, w_ref, bias_in_ref, xt_ref, qkv_ref, att_ref, lse_ref,
    qa_ref, ka_ref, s_ref, p_ref, tot_ref, wt_ref, bias_ref,
):
    seq, width = x_ref.shape
    groups = wt_ref.shape[0]
    group = width // groups

    @pl.when(pl.program_id(0) == 0)
    def _():
        for g in range(groups):
            for j in range(3):
                wt_ref[g, j * group : (j + 1) * group, :] = w_ref[j, g].T
        columns = jnp.concatenate([bias_in_ref[...], jnp.zeros((6, width), F32)], axis=0).T
        for n in range(2):
            bias_ref[n] = jnp.broadcast_to(columns[:, n : n + 1], (width, 128))

    xt_ref[0] = x_ref[...].T
    seg = seg_ref[0]
    rank = lax.broadcasted_iota(jnp.int32, (16, seq), 0)
    same = rank == seg
    for n in range(2 * HB):
        qa_ref[n, 64:80, :] = jnp.where(same, 1.0, 0.0).astype(BF)
        ka_ref[n, 64:80, :] = jnp.where(same | (rank >= 4), 0.0, NEG).astype(BF)

    for g in range(groups):
        rows = slice(g * group, (g + 1) * group)
        out = dot_nn(wt_ref[g], xt_ref[0, rows, :])
        for j in range(3):
            part = out[j * group : (j + 1) * group]
            if j != 1:
                part = part + wide(bias_ref[j // 2, rows, :], seq)
            qkv_ref[0, j, rows, :] = part.astype(BF)

    def head_rows(h):
        return slice(h * HEAD_DIM, (h + 1) * HEAD_DIM)

    def scores(h, n):
        rows = head_rows(h)
        qa_ref[n, 0:64, :] = qkv_ref[0, 0, rows, :] * jnp.asarray(0.125, BF)
        ka_ref[n, 0:64, :] = qkv_ref[0, 1, rows, :]
        s_ref[n] = dot_nn(ka_ref[n].T, qa_ref[n])

    def soften(h, n):
        for l in range(0, seq, LT):
            cols = slice(l, l + LT)
            peak = s_ref[n, 0:8, cols]
            for c in range(8, seq, 8):
                peak = jnp.maximum(peak, s_ref[n, c : c + 8, cols])
            peak = jnp.max(peak, axis=0, keepdims=True)
            total = jnp.zeros((8, LT), F32)
            for c in range(0, seq, 16):
                e = jnp.exp(s_ref[n, c : c + 16, cols] - peak)
                total = total + (e[0:8] + e[8:16])
                p_ref[n, c : c + 16, cols] = e.astype(BF)
            total = jnp.sum(total, axis=0, keepdims=True)
            tot_ref[n, 0:1, cols] = 1.0 / total
            tot_ref[n, 1:2, cols] = peak + jnp.log(total)
        lse_ref[0, h : h + 1, :] = tot_ref[n, 1:2, :]

    def mix(h, n):
        rows = head_rows(h)
        att_ref[0, rows, :] = (dot_nn(qkv_ref[0, 2, rows, :], p_ref[n]) * tot_ref[n, 0:1, :]).astype(BF)

    G = HB
    def many(fn, b):
        for k in range(G):
            fn(b * G + k, (b % 2) * G + k)

    batches = HEADS // G
    for b in range(batches + 2):
        if b < batches:
            many(scores, b)
        if 0 <= b - 1 < batches:
            many(soften, b - 1)
        if 0 <= b - 2 < batches:
            many(mix, b - 2)


def attend(x, seg, w, bias):
    width = x.shape[1]
    groups, group = w.shape[1:3]
    rows, seq = seg.shape
    return pl.pallas_call(
        attend_kernel,
        grid=(rows,),
        in_specs=[
            pl.BlockSpec((seq, width), lambda r: (r, 0)),
            pl.BlockSpec((1, 1, seq), lambda r: (r, 0, 0)),
            pl.BlockSpec(w.shape, lambda r: (0, 0, 0, 0)),
            pl.BlockSpec(bias.shape, lambda r: (0, 0)),
        ],
        out_specs=[
            pl.BlockSpec((1, width, seq), lambda r: (r, 0, 0)),
            pl.BlockSpec((1, 3, width, seq), lambda r: (r, 0, 0, 0)),
            pl.BlockSpec((1, width, seq), lambda r: (r, 0, 0)),
            pl.BlockSpec((1, 16, seq), lambda r: (r, 0, 0)),
        ],
        out_shape=[
            jax.ShapeDtypeStruct((rows, width, seq), BF),
            jax.ShapeDtypeStruct((rows, 3, width, seq), BF),
            jax.ShapeDtypeStruct((rows, width, seq), BF),
            jax.ShapeDtypeStruct((rows, 16, seq), F32),
        ],
        scratch_shapes=[pltpu.VMEM((2 * HB, 80, seq), BF) for _ in range(2)]
        + [pltpu.VMEM((2 * HB, seq, seq), F32), pltpu.VMEM((2 * HB, seq, seq), BF), pltpu.VMEM((2 * HB, 8, seq), F32)]
        + [pltpu.VMEM((groups, 3 * group, group), BF), pltpu.VMEM((2, width, 128), F32)],
        compiler_params=params("arbitrary", mib=60),
        cost_estimate=pl.CostEstimate(flops=int(10e9), transcendentals=0, bytes_accessed=20 * 2**20),
        name="attend",
    )(x, seg.reshape(rows, 1, seq), w, bias)

CH = 64
EC = 64
DU = 768
DO = 384
ROOT_HALF = 0.7071067811865476
LOG2E = 1.4426950408889634


def feed_kernel(
    core_ref, xt_ref, att_ref, cot_ref, wo_ref, own_ref, other_ref, vec_in_ref,
    out_ref, gr1_ref, gatt_ref, delta_ref, keep_ref, send_ref, okeep_ref, osend_ref,
    a_ref, u1_ref, v2_ref, nlow_ref, act_ref, gp_ref, gd_ref, gup_ref, ct_ref, acc_ref,
    wot_ref, wut_ref, wdt_ref, vec_ref, dwo_ref, dff_ref,
):
    width, seq = a_ref.shape
    walls = (own_ref, other_ref)
    halves, groups = 2, own_ref.shape[0]
    group = width // groups
    part = own_ref.shape[2]
    full = halves * part
    first = pl.program_id(0) == 0
    last = pl.program_id(0) == pl.num_programs(0) - 1
    inv_width = 1.0 / width
    aug = group + 16

    @pl.when(first)
    def _():
        acc_ref[...] = jnp.zeros_like(acc_ref)
        dwo_ref[...] = jnp.zeros_like(dwo_ref)
        dff_ref[...] = jnp.zeros_like(dff_ref)
        row = lax.broadcasted_iota(jnp.int32, (16, seq), 0)
        for g in range(groups):
            nlow_ref[g, group:aug, :] = jnp.where(row == 0, 1.0, 0.0).astype(BF)
        columns = vec_in_ref[...].T
        for n in range(6):
            vec_ref[n] = jnp.broadcast_to(columns[:, n : n + 1], (width, 128))
        wot_ref[...] = wo_ref[...].T

        def prepare(g, carry):
            for h in range(halves):
                rows = slice(h * part, (h + 1) * part)
                wut_ref[g, rows, :] = walls[h][g, 0:aug, :].T
                wdt_ref[g, rows, :] = (walls[h][g, aug : aug + group, :] * jnp.asarray(0.5, BF)).T
            return carry

        lax.fori_loop(0, groups, prepare, 0)

    ct_ref[...] = cot_ref[...].T

    part_sum = jnp.zeros((8, seq), F32)
    for b in range(0, width, DO):
        mixed = dot_nn(wot_ref[b : b + DO, :], att_ref[0])
        for c in range(0, DO, EC):
            s = slice(b + c, b + c + EC)
            v = mixed[c : c + EC] + wide(vec_ref[0, s, :], seq) + xt_ref[0, s, :].astype(F32)
            a_ref[s, :] = v
            part_sum = part_sum + sub_sum(v)
    mean = jnp.sum(part_sum, axis=0, keepdims=True) * inv_width
    part_sum = jnp.zeros((8, seq), F32)
    for c in range(0, width, CH):
        v = a_ref[c : c + CH, :] - mean
        part_sum = part_sum + sub_sum(v * v)
    r1 = lax.rsqrt(jnp.sum(part_sum, axis=0, keepdims=True) * inv_width + EPS)
    for g in range(groups):
        for c in range(0, group, 64):
            s = slice(g * group + c, g * group + c + 64)
            u = (a_ref[s, :] - mean) * r1
            u1_ref[s, :] = u
            n = u * wide(vec_ref[1, s, :], seq) + wide(vec_ref[2, s, :], seq)
            v2_ref[s, :] = n
            nlow_ref[g, c : c + 64, :] = n.astype(BF)

    part_sum = jnp.zeros((8, seq), F32)
    for g in range(groups):
        for b in range(0, full, DU):
            upward = dot_nn(wut_ref[g, b : b + DU, :], nlow_ref[g])
            for c in range(0, DU, EC):
                s = slice(b + c, b + c + EC)
                u = upward[c : c + EC]
                one = 1.0 + lax.erf(u * ROOT_HALF)
                act_ref[g, s, :] = (u * one).astype(BF)
                bell = jnp.exp2((u * u) * (-0.5 * LOG2E))
                gp_ref[g, s, :] = one + (u * (1.1283791670955126 * ROOT_HALF)) * bell
        s = slice(g * group, (g + 1) * group)
        down = dot_nn(walls[0][g, aug : aug + group, :], act_ref[g, 0:part, :])
        for h in range(1, halves):
            down = down + dot_nn(walls[h][g, aug : aug + group, :], act_ref[g, h * part : (h + 1) * part, :])
        v = v2_ref[s, :] + (down * 0.5 + wide(vec_ref[3, s, :], seq))
        v2_ref[s, :] = v
        part_sum = part_sum + sub_sum(v)

    mean = jnp.sum(part_sum, axis=0, keepdims=True) * inv_width
    part_sum = jnp.zeros((8, seq), F32)
    for c in range(0, width, CH):
        v = v2_ref[c : c + CH, :] - mean
        part_sum = part_sum + sub_sum(v * v)
    r2 = lax.rsqrt(jnp.sum(part_sum, axis=0, keepdims=True) * inv_width + EPS)
    sum_e = jnp.zeros((8, seq), F32)
    sum_eu = jnp.zeros((8, seq), F32)
    for c in range(0, width, CH):
        s = slice(c, c + CH)
        u = (v2_ref[s, :] - mean) * r2
        v2_ref[s, :] = u
        gain = wide(vec_ref[4, s, :], seq)
        out_ref[:, s] = (u * gain + wide(vec_ref[5, s, :], seq)).T
        cot = ct_ref[s, :].astype(F32)
        cu = cot * u
        acc_ref[4, s, :] += fold(cu)
        acc_ref[5, s, :] += fold(cot)
        sum_e = sum_e + sub_sum(cot * gain)
        sum_eu = sum_eu + sub_sum(cu * gain)
    mean_e = jnp.sum(sum_e, axis=0, keepdims=True) * inv_width
    mean_eu = jnp.sum(sum_eu, axis=0, keepdims=True) * inv_width
    for c in range(0, width, CH):
        s = slice(c, c + CH)
        e = ct_ref[s, :].astype(F32) * wide(vec_ref[4, s, :], seq)
        gr = r2 * (e - mean_e - v2_ref[s, :] * mean_eu)
        a_ref[s, :] = gr
        acc_ref[3, s, :] += fold(gr)
        gd_ref[s, :] = gr.astype(BF)

    for g in range(groups):
        rows = slice(g * group, (g + 1) * group)
        for b in range(0, full, DU):
            gact = dot_nn(wdt_ref[g, b : b + DU, :], gd_ref[rows, :])
            for c in range(0, DU, EC):
                s = slice(b + c, b + c + EC)
                gup_ref[g % 2, s, :] = (gact[c : c + EC] * gp_ref[g, s, :]).astype(BF)
        for h in range(halves):
            s = slice(h * part, (h + 1) * part)
            dff_ref[h, g, aug : aug + group, :] += dot_nt(gd_ref[rows, :], act_ref[g, s, :])
            dff_ref[h, g, 0:aug, :] += dot_nt(nlow_ref[g], gup_ref[g % 2, s, :])
        back = dot_nn(walls[0][g, 0:group, :], gup_ref[g % 2, 0:part, :])
        for h in range(1, halves):
            back = back + dot_nn(walls[h][g, 0:group, :], gup_ref[g % 2, h * part : (h + 1) * part, :])
        a_ref[rows, :] += back

    sum_e = jnp.zeros((8, seq), F32)
    sum_eu = jnp.zeros((8, seq), F32)
    for c in range(0, width, CH):
        s = slice(c, c + CH)
        gn = a_ref[s, :]
        gu = gn * u1_ref[s, :]
        acc_ref[1, s, :] += fold(gu)
        acc_ref[2, s, :] += fold(gn)
        gain = wide(vec_ref[1, s, :], seq)
        sum_e = sum_e + sub_sum(gn * gain)
        sum_eu = sum_eu + sub_sum(gu * gain)
    mean_e = jnp.sum(sum_e, axis=0, keepdims=True) * inv_width
    mean_eu = jnp.sum(sum_eu, axis=0, keepdims=True) * inv_width
    for c in range(0, width, CH):
        s = slice(c, c + CH)
        e = a_ref[s, :] * wide(vec_ref[1, s, :], seq)
        gr = r1 * (e - mean_e - u1_ref[s, :] * mean_eu)
        gr1_ref[0, s, :] = gr
        acc_ref[0, s, :] += fold(gr)
        gd_ref[s, :] = gr.astype(BF)
    for b in range(0, width, DO):
        grad = dot_nn(wo_ref[b : b + DO, :], gd_ref[...])
        for c in range(0, DO, HEAD_DIM):
            s = slice(b + c, b + c + HEAD_DIM)
            ga = grad[c : c + HEAD_DIM].astype(BF)
            gatt_ref[0, s, :] = ga
            prod = ga.astype(F32) * att_ref[0, s, :].astype(F32)
            head = (b + c) // HEAD_DIM
            delta_ref[0, head : head + 1, :] = jnp.sum(prod, axis=0, keepdims=True)
    half = width // 2
    for k in range(2):
        dwo_ref[k] += dot_nt(att_ref[0, k * half : (k + 1) * half, :], gd_ref[...])

    @pl.when(last)
    def _():
        for n in range(6):
            line = jnp.sum(acc_ref[n].T, axis=0, keepdims=True)
            for k in range(width // part):
                for h in range(halves):
                    at = aug + group + n * (width // part) + k
                    dff_ref[h, 0, at : at + 1, :] = line[:, k * part : (k + 1) * part]
        core = core_ref[0]
        okeep_ref[...] = dwo_ref[core]
        osend_ref[...] = dwo_ref[1 - core].astype(BF)
        two = groups // 2

        def hand(i, carry):
            h, k = i // two, i % two
            for ref, g in ((keep_ref, core * two + k), (send_ref, (1 - core) * two + k)):
                ref[h, k, 0:aug, :] = dff_ref[h, g, 0:aug, :].astype(ref.dtype)
                ref[h, k, aug : aug + group, :] = (dff_ref[h, g, aug : aug + group, :] * 0.5).astype(ref.dtype)
                ref[h, k, aug + group :, :] = dff_ref[h, g, aug + group :, :].astype(ref.dtype)
            return carry

        lax.fori_loop(0, halves * two, hand, 0)


def feed(core, xt, att, cot, wo, own, other, vec):
    rows, width, seq = xt.shape
    halves, (groups, _, part) = 2, own.shape
    group = width // groups
    aug = group + 16
    full = halves * part

    def whole(a):
        return pl.BlockSpec(a.shape, lambda r: (0,) * len(a.shape), pipeline_mode=pl.Buffered(1))

    per_row = pl.BlockSpec((1, width, seq), lambda r: (r, 0, 0))
    token = pl.BlockSpec((seq, width), lambda r: (r, 0))
    sums = (halves, groups // 2, 2 * group + 32, part)
    outs = [
        jax.ShapeDtypeStruct((rows * seq, width), F32),
        jax.ShapeDtypeStruct((rows, width, seq), F32),
        jax.ShapeDtypeStruct((rows, width, seq), BF),
        jax.ShapeDtypeStruct((rows, 16, seq), F32),
        jax.ShapeDtypeStruct(sums, F32),
        jax.ShapeDtypeStruct(sums, BF),
        jax.ShapeDtypeStruct((width // 2, width), F32),
        jax.ShapeDtypeStruct((width // 2, width), BF),
    ]
    return pl.pallas_call(
        feed_kernel,
        grid=(rows,),
        in_specs=[pl.BlockSpec(memory_space=pltpu.SMEM), per_row, per_row, token] + [whole(a) for a in (wo, own, other, vec)],
        out_specs=[token, per_row, per_row, pl.BlockSpec((1, 16, seq), lambda r: (r, 0, 0))]
        + [whole(a) for a in outs[4:]],
        out_shape=outs,
        scratch_shapes=[
            pltpu.VMEM((width, seq), F32),
            pltpu.VMEM((width, seq), F32),
            pltpu.VMEM((width, seq), F32),
            pltpu.VMEM((groups, aug, seq), BF),
            pltpu.VMEM((groups, full, seq), BF),
            pltpu.VMEM((groups, full, seq), F32),
            pltpu.VMEM((width, seq), BF),
            pltpu.VMEM((2, full, seq), BF),
            pltpu.VMEM((width, seq), BF),
            pltpu.VMEM((6, width, 128), F32),
            pltpu.VMEM((width, width), BF),
            pltpu.VMEM((groups, full, aug), BF),
            pltpu.VMEM((groups, full, group), BF),
            pltpu.VMEM((6, width, 128), F32),
            pltpu.VMEM((2, width // 2, width), F32),
            pltpu.VMEM((halves, groups, 2 * group + 32, part), F32),
        ],
        compiler_params=pltpu.CompilerParams(vmem_limit_bytes=63 * 2**20),
        cost_estimate=pl.CostEstimate(flops=int(25e9), transcendentals=0, bytes_accessed=35 * 2**20),
        name="feed",
    )(core, xt, att, cot, wo, own, other, vec)


def split3(v):
    hi = v.astype(BF).astype(F32)
    mid = (v - hi).astype(BF).astype(F32)
    return hi, mid, v - hi - mid


def back_kernel(
    core_ref, qkv_ref, gatt_ref, xt_ref, lse_ref, delta_ref, seg_ref, *rest, head0, fresh, final, passed
):
    rest = list(rest)
    if passed:
        del rest[-12 - passed : -12]
    if not fresh:
        dwin_ref, bsin_ref = rest[:2]
    d_ref = rest[-12]
    oa_ref, ob_ref = rest[-11:-9]
    qa_ref, ka_ref, va_ref, ga_ref, p_ref, dst_ref, ds_ref, dw_ref, bsum_ref = rest[-9:]
    chans, seq = xt_ref.shape[1:]
    groups, group = dw_ref.shape[1:3]
    first = pl.program_id(0) == 0
    last = pl.program_id(0) == pl.num_programs(0) - 1

    @pl.when(first)
    def _():
        if fresh:
            dw_ref[...] = jnp.zeros_like(dw_ref)
            bsum_ref[...] = jnp.zeros_like(bsum_ref)
        else:
            dw_ref[...] = dwin_ref[...]
            bsum_ref[...] = bsin_ref[...]

    seg = seg_ref[0]
    rank = lax.broadcasted_iota(jnp.int32, (16, seq), 0)
    same = rank == seg
    hot = jnp.where(same, 1.0, 0.0)
    for n in range(BUF):
        ka_ref[n, 64:80, :] = jnp.where(rank < 4, jnp.where(same, 0.0, NEG), jnp.where(rank < 7, -1.0, 0.0)).astype(BF)
        va_ref[n, 64:80, :] = jnp.where(rank < 3, -1.0, 0.0).astype(BF)

    def weigh(h):
        n = h % BUF
        rows = slice(h * HEAD_DIM, (h + 1) * HEAD_DIM)
        hi, mid, lo = split3(lse_ref[0, head0 + h : head0 + h + 1, :])
        tail = jnp.where(rank == 4, hi, jnp.where(rank == 5, mid, jnp.where(rank == 6, lo, 0.0)))
        qa_ref[n, 64:80, :] = jnp.where(rank < 4, hot, tail).astype(BF)
        hi, mid, lo = split3(delta_ref[0, head0 + h : head0 + h + 1, :])
        ga_ref[n, 64:80, :] = jnp.where(rank == 0, hi, jnp.where(rank == 1, mid, jnp.where(rank == 2, lo, 0.0))).astype(BF)
        qa_ref[n, 0:64, :] = qkv_ref[0, 0, rows, :] * jnp.asarray(0.125, BF)
        ka_ref[n, 0:64, :] = qkv_ref[0, 1, rows, :]
        va_ref[n, 0:64, :] = qkv_ref[0, 2, rows, :]
        ga_ref[n, 0:64, :] = gatt_ref[0, rows, :]
        kn = ka_ref[n].T
        vn = va_ref[n].T
        for t in range(seq // 256):
            cols = slice(t * 256, t * 256 + 256)
            p = jnp.exp(dot_nn(kn, qa_ref[n, :, cols]))
            low = p.astype(BF)
            p_ref[n, cols, :] = low.T
            ds = (p * dot_nn(vn, ga_ref[n, :, cols])).astype(BF)
            ds_ref[n, t] = ds
            dst_ref[n, cols, :] = ds.T

    def gather_head(h):
        n = h % BUF
        rows = slice(h * HEAD_DIM, (h + 1) * HEAD_DIM)
        kt = qkv_ref[0, 1, rows, :]
        dv = dot_nn(gatt_ref[0, rows, :], p_ref[n])
        dk = dot_nn(qa_ref[n, 0:64, :], dst_ref[n])
        dq = []
        for t in range(seq // 256):
            cols = slice(t * 256, t * 256 + 256)
            dq.append(dot_nn(kt, ds_ref[n, t]) * 0.125)
        dq = jnp.concatenate(dq, axis=1)
        bsum_ref[0, rows, :] += fold(dq)
        bsum_ref[1, rows, :] += fold(dv)
        d_ref[0, 0, rows, :] = dq.astype(BF)
        d_ref[0, 1, rows, :] = dk.astype(BF)
        d_ref[0, 2, rows, :] = dv.astype(BF)

    heads = chans // HEAD_DIM
    for h in range(heads + 1):
        if h < heads:
            weigh(h)
        if h > 0:
            gather_head(h - 1)
    for g in range(groups):
        s = slice(g * group, (g + 1) * group)
        for j in range(3):
            dw_ref[j, g] += dot_nt(xt_ref[0, s, :], d_ref[0, j, s, :])

    if not final:
        @pl.when(last)
        def _():
            oa_ref[...] = dw_ref[...]
            ob_ref[...] = bsum_ref[...]

    else:
        @pl.when(last)
        def _():
            half = PACK // 2
            core = core_ref[0]

            def put(row, value):
                where = row // half
                at = slice(row % half, row % half + value.shape[0])

                @pl.when(core == where)
                def _():
                    oa_ref[at, :] = value

                @pl.when(core != where)
                def _():
                    ob_ref[at, :] = value.astype(BF)

            for j in range(3):
                both = jnp.concatenate([dw_ref[j, g] for g in range(groups)], axis=1)
                for a in range(0, group, 64):
                    put(j * group + a, both[a : a + 64])
            bias = [jnp.sum(bsum_ref[n].T, axis=0, keepdims=True) for n in range(2)]
            put(3 * group, jnp.concatenate(bias + [jnp.zeros((62, chans), F32)], axis=0))


PACK = 640
BUF = 2


def back(core, qkv, gatt, xt, lse, delta, seg, w, index, parts, row0, count, carried, into, final, sends, keeps):
    rows, _, width, seq = qkv.shape
    chans = width // parts
    groups, group = w.shape[1] // parts, w.shape[2]
    per_row = pl.BlockSpec((1, chans, seq), lambda r: (r + row0, index, 0))
    full = pl.BlockSpec((1, 16, seq), lambda r: (r + row0, 0, 0))
    in_specs = [
        pl.BlockSpec(memory_space=pltpu.SMEM),
        pl.BlockSpec((1, 3, chans, seq), lambda r: (r + row0, 0, index, 0)),
        per_row,
        per_row,
        full,
        full,
        pl.BlockSpec((1, 1, seq), lambda r: (r + row0, 0, 0)),
    ]
    args = [core, qkv, gatt, xt, lse, delta, seg.reshape(rows, 1, seq)]
    sums = [jax.ShapeDtypeStruct((3, groups, group, group), F32), jax.ShapeDtypeStruct((2, chans, 128), F32)]
    if carried is not None:
        in_specs += [pl.BlockSpec((3, groups, group, group), lambda r: (0, 0, 0, 0)), pl.BlockSpec((2, chans, 128), lambda r: (0, 0, 0))]
        args += list(carried)
    alias = {}
    if into is not None:
        in_specs.append(pl.BlockSpec(memory_space=pl.ANY))
        args.append(into)
        alias = {len(args) - 1: len(keeps)}
    for n, value in enumerate(keeps):
        alias[len(args)] = n
        in_specs.append(pl.BlockSpec(memory_space=pl.ANY))
        args.append(value)
    for value in sends:
        in_specs.append(pl.BlockSpec(memory_space=pl.ANY))
        args.append(value)
    if final:
        outs = [jax.ShapeDtypeStruct((PACK // 2, chans), F32), jax.ShapeDtypeStruct((PACK // 2, chans), BF)]
    else:
        outs = sums
    return pl.pallas_call(
        partial(back_kernel, head0=index * (chans // HEAD_DIM), fresh=carried is None, final=final, passed=len(keeps)),
        grid=(count,),
        in_specs=in_specs,
        out_specs=[pl.BlockSpec(memory_space=pl.ANY) for _ in keeps]
        + [pl.BlockSpec((1, 3, chans, seq), lambda r: (r + row0, 0, index, 0))]
        + [pl.BlockSpec(o.shape, lambda r, n=len(o.shape): (0,) * n) for o in outs],
        out_shape=[jax.ShapeDtypeStruct(value.shape, value.dtype) for value in keeps]
        + [jax.ShapeDtypeStruct((rows, 3, width, seq), BF)]
        + outs,
        scratch_shapes=[pltpu.VMEM((BUF, 80, seq), BF) for _ in range(4)]
        + [pltpu.VMEM((BUF, seq, seq), BF) for _ in range(2)]
        + [pltpu.VMEM((BUF, seq // 256, seq, 256), BF)]
        + [pltpu.VMEM(o.shape, F32) for o in sums],
        input_output_aliases=alias,
        compiler_params=params("arbitrary", mib=20),
        cost_estimate=pl.CostEstimate(flops=int(8e9 * count), transcendentals=0, bytes_accessed=20 * 2**20),
        name="back",
    )(*args)


def input_kernel(d_ref, gr1_ref, w_ref, *rest):
    gin_ref = rest[-1]
    groups, group = w_ref.shape[1:3]
    parts = []
    for g in range(groups):
        s = slice(g * group, (g + 1) * group)
        total = gr1_ref[0, s, :]
        for j in range(3):
            total = total + dot_nn(w_ref[j, g], d_ref[0, j, s, :])
        parts.append(total)
    gin_ref[...] = jnp.concatenate(parts, axis=0).T


def input_grad(d, gr1, w, row0, count, into, sends, keeps):
    rows, _, width, seq = d.shape
    in_specs = [
        pl.BlockSpec((1, 3, width, seq), lambda r: (r + row0, 0, 0, 0)),
        pl.BlockSpec((1, width, seq), lambda r: (r + row0, 0, 0)),
        pl.BlockSpec(w.shape, lambda r: (0, 0, 0, 0)),
    ]
    args = [d, gr1, w]
    alias = {}
    if into is not None:
        alias[len(args)] = len(keeps)
        args.append(into)
    for n, value in enumerate(keeps):
        alias[len(args)] = n
        args.append(value)
    args += sends
    in_specs += [pl.BlockSpec(memory_space=pl.ANY)] * (len(args) - len(in_specs))
    return pl.pallas_call(
        input_kernel,
        grid=(count,),
        in_specs=in_specs,
        out_specs=[pl.BlockSpec(memory_space=pl.ANY) for _ in keeps] + [pl.BlockSpec((seq, width), lambda r: (r + row0, 0))],
        out_shape=[jax.ShapeDtypeStruct(value.shape, value.dtype) for value in keeps]
        + [jax.ShapeDtypeStruct((rows * seq, width), F32)],
        input_output_aliases=alias,
        compiler_params=params("arbitrary", mib=20),
        cost_estimate=pl.CostEstimate(flops=int(8e9 * count), transcendentals=0, bytes_accessed=6 * count * 2**20),
        name="input_grad",
    )(*args)


class Pair:
    def __init__(self, name, size, bit):
        self.name, self.size, self.bit = name, size, bit
        self.side = (lax.axis_index(name) // bit) % 2

    def swap(self, values):
        pairs = [(i, i ^ self.bit) for i in range(self.size)]
        return [lax.ppermute(value, self.name, pairs) for value in values]

    def split(self, value):
        half = value.shape[0] // 2
        keep = lax.dynamic_slice_in_dim(value, self.side * half, half, 0)
        send = lax.dynamic_slice_in_dim(value, (1 - self.side) * half, half, 0)
        return keep, [send.astype(BF)]

    def join(self, value):
        (other,) = self.swap([value])
        return jnp.where(self.side == 0, jnp.concatenate([value, other]), jnp.concatenate([other, value]))


class Quad:
    def __init__(self, a, b):
        self.a, self.b = a, b

    def swap(self, values):
        a, b = self.a, self.b
        if a.name == b.name:
            both = Pair(a.name, a.size, a.bit | b.bit).swap(values[2:])
        else:
            pairs = [(i * b.size + j, (i ^ a.bit) * b.size + (j ^ b.bit)) for i in range(a.size) for j in range(b.size)]
            both = [lax.ppermute(values[2], (a.name, b.name), pairs)]
        return list(b.swap(values[:1])) + list(a.swap(values[1:2])) + list(both)

    def split(self, value):
        part = value.shape[0] // 4

        def piece(da, db):
            at = (self.a.side ^ da) * 2 + (self.b.side ^ db)
            return lax.dynamic_slice_in_dim(value, at * part, part, 0)

        return piece(0, 0), [piece(*d).astype(BF) for d in ((0, 1), (1, 0), (1, 1))]

    def join(self, value):
        near = jnp.stack([value] + self.swap([value] * 3)).reshape((2, 2) + value.shape)
        near = jnp.where(self.a.side == 0, near, near[::-1])
        near = jnp.where(self.b.side == 0, near, near[:, ::-1])
        return near.reshape((4 * value.shape[0],) + value.shape[1:])


def add(keep, got):
    total = keep
    for value in got:
        total = total + value.astype(F32)
    return total


def sum_across(low, bits):
    for bit in bits:
        (got,) = bit.swap([low])
        low = (low.astype(F32) + got.astype(F32)).astype(BF)
    return low


def finish_kernel(core_ref, own_ref, got_ref, dqkv_ref, qvb_ref, dwo_ref, dup_ref, upb_ref, ddown_ref, small_ref, all_ref):
    core = core_ref[0]
    all_ref[core] = own_ref[...]
    all_ref[1 - core] = got_ref[...]
    groups, group, part = dup_ref.shape
    aug = group + 16
    block = 2 * group + 32
    width = dwo_ref.shape[1]
    for c in range(2):
        for k in range(groups // 2):
            g, row = c * (groups // 2) + k, k * block
            dup_ref[g] = all_ref[c, row : row + group, :].astype(F32)
            upb_ref[g : g + 1, :] = all_ref[c, row + group : row + aug, :].astype(F32)[0:1]
            ddown_ref[g] = all_ref[c, row + aug : row + aug + group, :].astype(F32)
    lines = all_ref[0, aug + group : block, :].astype(F32)
    for n in range(6):
        for k in range(width // part):
            at = n * (width // part) + k
            small_ref[n : n + 1, k * part : (k + 1) * part] = lines[at : at + 1]
    rows = width // 8
    parts = width // part
    per = groups // parts
    quarter = PACK // 8
    place = 2 * rows + parts * quarter
    for q in range(4):
        base = (groups // 2) * block + q * place
        for c in range(2):
            to = c * (width // 2) + q * rows
            for k in range(2):
                at = base + k * rows
                dwo_ref[to : to + rows, k * part : (k + 1) * part] = all_ref[c, at : at + rows, :].astype(F32)
            for p in range(parts):
                at = base + 2 * rows + p * quarter
                row = c * (PACK // 2) + q * quarter
                done = 0
                while done < quarter:
                    j, i = (row + done) // group, (row + done) % group
                    n = min(quarter - done, group - i)
                    values = all_ref[c, at + done : at + done + n, :].astype(F32)
                    if j < 3:
                        for g in range(per):
                            dqkv_ref[j, p * per + g, i : i + n, :] = values[:, g * group : (g + 1) * group]
                    else:
                        qvb_ref[:, p * part : (p + 1) * part] = values[0:2]
                    done += n


def finish(core, own, got, groups, group, part):
    width = groups * group
    shapes = [(3, groups, group, group), (2, width), (width, width), (groups, group, part), (groups, part), (groups, group, part), (8, width)]

    def whole(shape):
        return pl.BlockSpec(shape, lambda i, n=len(shape): (0,) * n)

    return pl.pallas_call(
        finish_kernel,
        grid=(1,),
        in_specs=[pl.BlockSpec(memory_space=pltpu.SMEM), whole(own.shape), whole(got.shape)],
        out_specs=[whole(shape) for shape in shapes],
        out_shape=[jax.ShapeDtypeStruct(shape, F32) for shape in shapes],
        scratch_shapes=[pltpu.VMEM((2,) + own.shape, BF)],
        compiler_params=params("arbitrary", mib=20),
        name="finish",
    )(core, own, got)


def per_device(
    inputs, segments, cotangent, qkv_weight, qv_bias, out_weight, out_bias, ln1_gain, ln1_bias,
    up_weight, up_bias, down_weight, down_bias, ln2_gain, ln2_bias, *, dp, ffn,
):
    groups, group = qkv_weight.shape[1:3]
    part = up_weight.shape[2]
    assert ffn == 2
    bits = [Pair("dp", dp, 1 << k) for k in range(dp.bit_length() - 1)]
    core, ax, rest = bits[0], bits[1], bits[2:]
    ay = Pair("ffn", ffn, 1)
    plane = Quad(ax, ay)
    core_id = core.side.astype(jnp.int32).reshape(1)
    rows = segments.shape[0]

    wall = jnp.concatenate(
        [up_weight, up_bias[:, None, :], jnp.zeros((groups, 15, part), BF), down_weight], axis=1
    )
    (fetched,) = ay.swap([lax.dynamic_slice_in_dim(wall, core.side * (groups // 2), groups // 2, 0)])
    xt, qkv, att, lse = attend(inputs, segments, qkv_weight, qv_bias)
    other = core.join(jnp.where(lse[0, 0, :part] < jnp.inf, fetched, jnp.zeros_like(fetched)))
    zero = jnp.zeros_like(out_bias)
    vec = jnp.stack([out_bias, ln1_gain, ln1_bias, down_bias, ln2_gain, ln2_bias, zero, zero])
    layer_out, gr1, gatt, delta, *first = feed(core_id, xt, att, cotangent, out_weight, wall, other, vec)
    qkv = pltpu.with_memory_space_constraint(qkv, pltpu.HBM)
    gatt = pltpu.with_memory_space_constraint(gatt, pltpu.HBM)
    xt = pltpu.with_memory_space_constraint(xt, pltpu.HBM)
    gr1 = pltpu.with_memory_space_constraint(gr1, pltpu.HBM)
    first = [pltpu.with_memory_space_constraint(v, pltpu.HBM) if v.dtype == F32 else v for v in first]

    parts = 2
    state = {"grads": None, "carried": None, "input": None}
    packs = []

    def under(calls, *stages):
        keeps = [keep for _, keep, _ in stages]
        got = [exchange.swap(sends) for exchange, _, sends in stages]
        for call in calls:
            keeps = call([], keeps)
        return [add(keep, arrived) for keep, arrived in zip(keeps, got)]

    def part_of_back(index, row0, count):
        def call(sends, keeps):
            final = row0 + count >= rows
            outs = back(
                core_id, qkv, gatt, xt, lse, delta, segments, qkv_weight, index, parts, row0, count,
                state["carried"], state["grads"], final, sends, keeps,
            )
            state["grads"], *carried = outs[len(keeps) :]
            state["carried"] = None if final else carried
            if final:
                packs.append(carried)
            return list(outs[: len(keeps)])

        return call

    def part_of_input(row0, count):
        def call(sends, keeps):
            *kept, state["input"] = input_grad(state["grads"], gr1, qkv_weight, row0, count, state["input"], sends, keeps)
            return kept

        return call

    def cut(index, at):
        return [part_of_back(index, row0, end - row0) for row0, end in zip([0] + at, at + [rows]) if end > row0]

    calls = [cut(0, [rows // 4]), cut(1, [rows // 2])]
    ffn1, out1 = under(calls[0][:1], (core, first[0], [first[1]]), (core, first[2], [first[3]]))
    ffn2, out2 = under(calls[0][1:], (ay, ffn1[0], [ffn1[1].astype(BF)]), (ax, *ax.split(out1)))
    keep, send = packs[0]
    ffn3, out3, sum0 = under(calls[1][:1], (ax, *ax.split(ffn2)), (ay, *ay.split(out2)), (core, keep, [send]))
    both = jnp.concatenate([ffn3[0], out3[:, :part], out3[:, part:]])
    both, sum0 = under(calls[1][1:], (rest[0], *rest[0].split(both)), (plane, *plane.split(sum0)))
    keep, send = packs[1]
    low = both.astype(BF)
    got = rest[1].swap([low])
    (kept,) = part_of_input(0, rows - rows // 2)([], [low.astype(F32)])
    if rows > 1:
        (kept,) = part_of_input(rows - rows // 2, rows // 2)([], [kept])
    both = add(kept, got)
    pack = add(keep, core.swap([send]))
    keep, sends = plane.split(pack)
    sum1 = add(keep, plane.swap(sends))
    sums = sum_across(jnp.stack([sum0, sum1]).astype(BF), rest)
    both = rest[0].join(sum_across(both.astype(BF), rest[2:]))
    block = 2 * group + 32
    ffns = ax.join(both[None, :block])
    rest_of = plane.join(jnp.concatenate([both[block:], sums.reshape(-1, part)])[None])
    own = jnp.concatenate([ffns.reshape(-1, part), rest_of.reshape(-1, part)])
    (got,) = core.swap([own])
    dqkv, qvb, dwo, dup, upb, ddown, small = finish(core_id, own, got, groups, group, part)
    grad_inputs = state["input"]
    return (
        layer_out, grad_inputs, dqkv, qvb, dwo, small[0], small[1], small[2],
        dup, upb, ddown, small[3], small[4], small[5],
    )


def solution(mesh):
    rows = P(("dp", "ffn"), None)
    shared = P()
    split = P(None, None, "ffn")
    return jax.shard_map(
        partial(per_device, dp=mesh.shape["dp"], ffn=mesh.shape["ffn"]),
        mesh=mesh,
        in_specs=(rows, rows, rows) + (shared,) * 6 + (split, P(None, "ffn"), split) + (shared,) * 3,
        out_specs=(rows, rows) + (shared,) * 6 + (split, P(None, "ffn"), split) + (shared,) * 3,
        check_vma=False,
    )
```
